32 devices in a mesh: block: 16 (over z, y, core), tok: 2 (over x).
Axes of the slice: x: 2, y: 2, z: 4, core: 2. Of those that a mesh axis runs over, the one named last changes fastest.
Arguments:
- keys: bfloat16 [2, 24576, 768], P(None, ('block', 'tok')), may hold values from -6 to 6
- values: bfloat16 [2, 24576, 768], P(None, ('block', 'tok')), may hold values from -6 to 6
- queries: bfloat16 [2, 24576, 768], P(None, ('block', 'tok')), may hold values from -6 to 6
- fast_in: bfloat16 [16, 3, 2, 384, 384], P('block', None, None, None, 'tok'), may hold values from -0.3125 to 0.3125
- moment_in: float32 [16, 3, 2, 384, 384], P('block', None, None, None, 'tok'), may hold values from -0.06 to 0.06
- initial_fast: bfloat16 [3, 2, 384, 384], P(None, None, None, 'tok'), may hold values from -0.3125 to 0.3125
- rates: float32 [3, 2], replicated, may hold values from 0.5 to 4
- decays: float32 [2], replicated, may hold values from 0.3 to 0.9
Outputs:
- outputs: bfloat16 [2, 24576, 768], P(None, ('block', 'tok'))
- fast_out: bfloat16 [16, 3, 2, 384, 384], P('block', None, None, None, 'tok')
- moment_out: float32 [16, 3, 2, 384, 384], P('block', None, None, None, 'tok')
The draws below stay inside these ranges and needn't reach their ends.
All inputs are finite; a program needn't handle non-finite values.
Results may differ from the reference program's by a relative error of at most 0.0091.
Values may be sent and summed in bfloat16 or wider, within the bound.
No kernel may reach another device: no remote copies, remote signals or barrier semaphores. Data moves between devices by JAX's collectives and lax.ppermute only.
A program may use at most 64 MiB of HBM per device.

```python
import math
import jax
import jax.numpy as jnp
from jax import lax

HEADS = 2
HEAD_DIM = 384
STEPS = 2
TOKENS = 24576
FEATURES = 768
N_BLOCK = 16


def block_levels(key, dims, cuts, smallest, high):
    loudness = 1.0
    for dim, parts in cuts:
        heights = jax.random.uniform(jax.random.fold_in(jax.random.fold_in(key, 6), dim), (parts,), jnp.float32, smallest / len(cuts), high / len(cuts))
        loudness = loudness * jnp.repeat(jnp.exp(heights), dims[dim] // parts).reshape((-1,) + (1,) * (len(dims) - 1 - dim))
    return loudness


def gaussian(rng, extent, spread, most, pieces=(), kind=jnp.bfloat16):
    factor_of = block_levels(rng, extent, pieces, -0.22, 0.18) if pieces else 1.0
    array = jax.random.normal(rng, extent, jnp.float32) * spread * factor_of
    return jnp.minimum(jnp.maximum(array, -most), most).astype(kind)


def setup_inputs(seed: int = 0) -> dict:
    key_of = jax.random.split(jax.random.key(seed), 9)
    keys = gaussian(key_of[0], (STEPS, TOKENS, FEATURES), 1.0, 6.0, ((1, 32),))
    values = gaussian(key_of[1], (STEPS, TOKENS, FEATURES), 1.0, 6.0, ((1, 32),))
    queries = gaussian(key_of[2], (STEPS, TOKENS, FEATURES), 1.0, 6.0, ((1, 32),))
    fast_in = gaussian(key_of[3], (N_BLOCK, 3, HEADS, HEAD_DIM, HEAD_DIM), HEAD_DIM ** -0.5, 0.3125, ((0, 16), (4, 2)))
    moment_in = gaussian(key_of[4], (N_BLOCK, 3, HEADS, HEAD_DIM, HEAD_DIM), 0.01, 0.06, ((0, 16), (4, 2)), jnp.float32)
    initial_fast = gaussian(key_of[5], (3, HEADS, HEAD_DIM, HEAD_DIM), HEAD_DIM ** -0.5, 0.3125, ((3, 2),))
    rates = jnp.clip(jnp.exp(jax.random.uniform(key_of[6], (3, HEADS), jnp.float32, math.log(0.5), math.log(4.0))), 0.5, 4.0)
    decays = jnp.clip(jax.random.uniform(key_of[7], (HEADS,), jnp.float32, 0.3, 0.9), 0.3, 0.9)
    return {"keys": keys, "values": values, "queries": queries, "fast_in": fast_in, "moment_in": moment_in, "initial_fast": initial_fast, "rates": rates, "decays": decays}


def swiglu_parts(rows, weights):
    xf = rows.astype(jnp.float32)
    gate = jnp.einsum('rhi,hio->rho', xf, weights[0].astype(jnp.float32))
    upper = jnp.einsum('rhi,hio->rho', xf, weights[1].astype(jnp.float32))
    return (gate, upper)

def group_step(weights, moment, kin, vin, qin, rates, decays, divisor):
    gate, upper = swiglu_parts(kin, weights)
    silu_gate = jax.nn.silu(gate)
    hidden = (silu_gate * upper).astype(jnp.bfloat16)
    dout = (-vin.astype(jnp.float32) / divisor).astype(jnp.bfloat16)
    grad_down = jnp.einsum('rhi,rho->hio', hidden.astype(jnp.float32), dout.astype(jnp.float32))
    dhid = jnp.einsum('rho,hio->rhi', dout.astype(jnp.float32), weights[2].astype(jnp.float32))
    sigma = jax.nn.sigmoid(gate)
    dgate = (dhid * upper * sigma * (1.0 + gate * (1.0 - sigma))).astype(jnp.bfloat16)
    dup = (dhid * silu_gate).astype(jnp.bfloat16)
    kf = kin.astype(jnp.float32)
    grad_gate = jnp.einsum('rhi,rho->hio', kf, dgate.astype(jnp.float32))
    grad_up = jnp.einsum('rhi,rho->hio', kf, dup.astype(jnp.float32))
    grad = jnp.stack([grad_gate, grad_up, grad_down])
    new_moment = decays[None, :, None, None] * moment + grad
    old = weights.astype(jnp.float32)
    moved = old - rates[:, :, None, None] * new_moment
    old_norm = jnp.sqrt(lax.optimization_barrier(jnp.mean(old * old, axis=-2, keepdims=True)) + 1e-06)
    new_norm = jnp.sqrt(lax.optimization_barrier(jnp.mean(moved * moved, axis=-2, keepdims=True)) + 1e-06)
    new_weights = (moved * (old_norm / new_norm)).astype(jnp.bfloat16)
    qgate, qup = swiglu_parts(qin, new_weights)
    qhid = (jax.nn.silu(qgate) * qup).astype(jnp.bfloat16)
    result = jnp.einsum('rhi,hio->rho', qhid.astype(jnp.float32), new_weights[2].astype(jnp.float32))
    return (new_weights, new_moment, result.astype(jnp.bfloat16))

def reference(keys, values, queries, fast_in, moment_in, initial_fast, rates, decays):
    block = keys.shape[1] // N_BLOCK
    heads = rates.shape[1]
    width = keys.shape[2] // heads

    def take(arr, step, index):
        part = lax.dynamic_slice_in_dim(arr[step], (index * block).astype(jnp.int32), block, 0)
        return part.reshape(block, heads, width)

    def run(step):

        def one(item):
            weights, moment, index = item
            return group_step(weights, moment, take(keys, step, index), take(values, step, index), take(queries, step, index), rates, decays, float(block))
        return one
    index = jnp.arange(N_BLOCK, dtype=jnp.int32)
    weights_one, moment_one, out_one = lax.map(run(0), (fast_in, moment_in, index))
    weights_two = jnp.concatenate([initial_fast[None], weights_one[:-1]], axis=0)
    moment_two = jnp.concatenate([jnp.zeros_like(moment_one[:1]), moment_one[:-1]], axis=0)
    weights_fin, moment_fin, out_two = lax.map(run(1), (weights_two, moment_two, index))
    total = N_BLOCK * block
    outputs = jnp.stack([out_one.reshape(total, heads * width), out_two.reshape(total, heads * width)])
    return (outputs, weights_fin, moment_fin)
```

```python
import functools

import jax
import jax.numpy as jnp
from jax import lax
from jax.experimental import pallas as pl
from jax.experimental.pallas import tpu as pltpu
from jax.sharding import PartitionSpec as P

F32 = jnp.float32
BF16 = jnp.bfloat16
VMEM = pl.BlockSpec(memory_space=pltpu.VMEM)
SMEM = pl.BlockSpec(memory_space=pltpu.SMEM)


def mm(a, b, dims):
    return lax.dot_general(a, b, (dims, ((), ())), preferred_element_type=F32)


def call(kernel, name, out, in_specs, out_specs=None, scratch=(), aliases=None):
    return pl.pallas_call(
        kernel,
        name=name,
        grid=(1,),
        out_shape=out,
        in_specs=in_specs,
        out_specs=out_specs,
        scratch_shapes=list(scratch),
        input_output_aliases=aliases or {},
    )


def whole_spec(*shape):
    return pl.BlockSpec(shape, lambda i: (0,) * len(shape))


def row_chunk(rows):
    for size in (256, 384, 128):
        if rows % size == 0:
            return size
    return rows


def spread(shards, own, width):
    n = len(shards)
    part = shards[0].shape[-1]
    owner = lax.broadcasted_iota(jnp.int32, (shards[0].shape[0], width), 1) // part
    total = None
    for r, shard in enumerate(shards):
        tiled = jnp.concatenate([shard] * n, axis=1)
        source = lax.rem(own - r + n, n)
        total = tiled if total is None else jnp.where(owner == source, tiled, total)
    return total


def grads_core(divisor, k_ref, v_ref, gu_ref, down_ref, hid_s, dout_s, dgu_s):
    rows, width = k_ref.shape
    size = row_chunk(rows)
    for first in range(0, rows, size):
        at = pl.ds(first, size)
        both = mm(k_ref[at, :], gu_ref[...], ((1,), (0,)))
        gate, upper = both[:, :width], both[:, width:]
        dout = (-v_ref[at, :].astype(F32) / divisor).astype(BF16)
        dhid = mm(dout, down_ref[...], ((1,), (1,)))
        sigma = jax.nn.sigmoid(gate)
        silu = gate * sigma
        hid_s[at, :] = (silu * upper).astype(BF16)
        dout_s[at, :] = dout
        dgu_s[at, :width] = (dhid * upper * sigma * (1.0 + gate * (1.0 - sigma))).astype(BF16)
        dgu_s[at, width:] = (dhid * silu).astype(BF16)
    grad_down = mm(hid_s[...], dout_s[...], ((0,), (0,)))
    grad_gu = mm(k_ref[...], dgu_s[...], ((0,), (0,)))
    return grad_gu, grad_down


def grads_one(n, head, divisor, tok_ref, decay_ref, k_ref, v_ref, m_ref, *refs):
    shards = refs[:n]
    gu_ref, down_ref, send_gu, send_down, own_gu, own_down, hid_s, dout_s, dgu_s = refs[n:]
    width = down_ref.shape[1]
    me = tok_ref[0]
    gu_ref[:, :width] = spread([s[0] for s in shards], me, width)
    gu_ref[:, width:] = spread([s[1] for s in shards], me, width)
    down_ref[...] = spread([s[2] for s in shards], me, width)
    grad_gu, grad_down = grads_core(
        divisor, k_ref, v_ref, gu_ref, down_ref, hid_s, dout_s, dgu_s
    )
    decay = decay_ref[head]
    part = m_ref.shape[-1]
    mine = lax.broadcasted_iota(jnp.int32, (width, width), 1) // part == me

    def folded(grad, m):
        tiled = jnp.concatenate([m_ref[m]] * n, axis=1)
        return grad + jnp.where(mine, decay * tiled, 0.0)

    for m in range(2):
        cols = slice(m * width, (m + 1) * width)
        total = folded(grad_gu[:, cols], m)
        own_gu[:, cols] = total
        send_gu[:, cols] = total.astype(BF16)
    total = folded(grad_down, 2)
    own_down[...] = total
    send_down[...] = total.astype(BF16)


def grads_two(head, divisor, tok_ref, decay_ref, k_ref, v_ref, pgu_ref, pdown_ref, *refs):
    send_gu, send_down, own_gu, own_down, hid_s, dout_s, dgu_s = refs
    width = k_ref.shape[1]
    grad_gu, grad_down = grads_core(
        divisor,
        k_ref,
        v_ref,
        pgu_ref.at[pl.ds(0, width), :],
        pdown_ref.at[pl.ds(0, width), :],
        hid_s,
        dout_s,
        dgu_s,
    )
    decay = decay_ref[head]
    held = pgu_ref.shape[0] - width
    mine = pl.ds(pl.multiple_of(tok_ref[0] * held, held), held)
    old = pl.ds(width, held)
    own_gu[...] = grad_gu
    own_gu[mine, :] += decay * pgu_ref[old, :].astype(F32)
    send_gu[...] = own_gu[...].astype(BF16)
    own_down[...] = grad_down
    own_down[mine, :] += decay * pdown_ref[old, :].astype(F32)
    send_down[...] = own_down[...].astype(BF16)


def updated(rate, old_ref, own_ref, recvs, cols):
    width = own_ref.shape[0]
    moment = own_ref[:, cols]
    for recv in recvs:
        moment = moment + recv[:, cols].astype(F32)
    old = old_ref[pl.ds(0, width), cols].astype(F32)
    moved = old - rate * moment
    old_norm = jnp.sqrt(jnp.mean(old * old, axis=0, keepdims=True) + 1e-06)
    new_norm = jnp.sqrt(jnp.mean(moved * moved, axis=0, keepdims=True) + 1e-06)
    return (moved * (old_norm / new_norm)).astype(BF16), moment


def update_one(n, head, mats, tok_ref, rate_ref, old_ref, own_ref, *refs):
    recvs = refs[: n - 1]
    pack_ref, moment_s = refs[n - 1 :]
    width = own_ref.shape[0]
    held = width // n
    for i, m in enumerate(mats):
        cols = slice(i * width, (i + 1) * width)
        new, moment = updated(rate_ref[m, head], old_ref, own_ref, recvs, cols)
        pack_ref[:width, cols] = new
        moment_s[:, cols] = moment
    mine = pl.ds(pl.multiple_of(tok_ref[0] * held, held), held)
    pack_ref[width:, :] = moment_s[mine, :].astype(BF16)


def columns_of(n, me, x):
    part = x.shape[1] // n
    picked = x[:, :part]
    for j in range(1, n):
        picked = jnp.where(me == j, x[:, j * part : (j + 1) * part], picked)
    return picked


def update_two_gu(n, head, tok_ref, rate_ref, old_ref, own_ref, q_ref, *refs):
    recvs = refs[: n - 1]
    hq_ref, fast_ref, moment_ref, gu_s = refs[-4:]
    width = own_ref.shape[0]
    me = tok_ref[0]
    for m in range(2):
        cols = slice(m * width, (m + 1) * width)
        new, moment = updated(rate_ref[m, head], old_ref, own_ref, recvs, cols)
        gu_s[:, cols] = new
        fast_ref[m] = columns_of(n, me, new)
        moment_ref[m] = columns_of(n, me, moment)
    rows = q_ref.shape[0]
    size = row_chunk(rows)
    for first in range(0, rows, size):
        at = pl.ds(first, size)
        both = mm(q_ref[at, :], gu_s[...], ((1,), (0,)))
        hq_ref[at, :] = (jax.nn.silu(both[:, :width]) * both[:, width:]).astype(BF16)


def update_two_down(n, head, tok_ref, rate_ref, old_ref, own_ref, hq_ref, *refs):
    recvs = refs[: n - 1]
    out_ref, fast_ref, moment_ref = refs[-3:]
    me = tok_ref[0]
    new, moment = updated(rate_ref[2, head], old_ref, own_ref, recvs, slice(None))
    fast_ref[0] = columns_of(n, me, new)
    moment_ref[0] = columns_of(n, me, moment)
    out_ref[...] = mm(hq_ref[...], new, ((1,), (0,))).astype(BF16)


def apply_one(q_ref, pgu_ref, pdown_ref, *refs):
    out_ref = refs[-1]
    rows, width = q_ref.shape
    size = row_chunk(rows)
    for first in range(0, rows, size):
        at = pl.ds(first, size)
        both = mm(q_ref[at, :], pgu_ref[pl.ds(0, width), :], ((1,), (0,)))
        hq = (jax.nn.silu(both[:, :width]) * both[:, width:]).astype(BF16)
        out_ref[at, :] = mm(hq, pdown_ref[pl.ds(0, width), :], ((1,), (0,))).astype(BF16)


def on_device(keys, values, queries, fast_in, moment_in, initial_fast, rates, decays):
    n = lax.axis_size("tok")
    blocks = lax.axis_size("block")
    steps, rows, features = keys.shape
    heads = rates.shape[1]
    width = features // heads
    part = fast_in.shape[4]
    held = width // n
    divisor = float(rows * n)
    me = lax.axis_index("tok").astype(jnp.int32)
    tok = me.reshape(1)
    leading = lax.axis_index("block") == 0

    def others(x):
        return [
            lax.ppermute(x, "tok", [(i, (i + r) % n) for i in range(n)]) for r in range(1, n)
        ]

    def forward(x):
        return lax.ppermute(x, "block", [(i, i + 1) for i in range(blocks - 1)])

    def rows_spec(step, head):
        return pl.BlockSpec((None, rows, width), lambda i: (step, 0, head))

    def shape(*dims, dtype=BF16):
        return jax.ShapeDtypeStruct(dims, dtype)

    w1 = whole_spec(width, width)
    w2 = whole_spec(width, 2 * width)
    p1 = whole_spec(width + held, width)
    p2 = whole_spec(width + held, 2 * width)
    scratch = (
        pltpu.VMEM((rows, width), BF16),
        pltpu.VMEM((rows, width), BF16),
        pltpu.VMEM((rows, 2 * width), BF16),
    )
    grad_out = (
        shape(width, 2 * width),
        shape(width, width),
        shape(width, 2 * width, dtype=F32),
        shape(width, width, dtype=F32),
    )

    owned = [fast_in[0, :, h] for h in range(heads)]
    shards = [[owned[h]] + others(owned[h]) for h in range(heads)]
    first = []
    for h in range(heads):
        first.append(
            call(
                functools.partial(grads_one, n, h, divisor),
                "grads_one",
                (shape(width, 2 * width), shape(width, width)) + grad_out,
                [
                    SMEM,
                    SMEM,
                    rows_spec(0, h),
                    rows_spec(0, h),
                    pl.BlockSpec((None, 3, None, width, part), lambda i, h=h: (0, 0, h, 0, 0)),
                ]
                + [whole_spec(3, width, part)] * n,
                (w2, w1, w2, w1, w2, w1),
                scratch,
            )(tok, decays, keys, values, moment_in, *shards[h])
        )
    start = [[initial_fast[:, h]] + others(initial_fast[:, h]) for h in range(heads)]

    packs = []
    for h in range(heads):
        gu, down, send_gu, send_down, own_gu, own_down = first[h]
        recv_gu, recv_down = others(send_gu), others(send_down)
        pair = []
        for mats, old, own, recvs, w, p in (
            ((0, 1), gu, own_gu, recv_gu, w2, p2),
            ((2,), down, own_down, recv_down, w1, p1),
        ):
            cols = len(mats) * width
            pair.append(
                call(
                    functools.partial(update_one, n, h, mats),
                    "update_one",
                    shape(width + held, cols),
                    [SMEM, SMEM, w, w] + [w] * (n - 1),
                    p,
                    (pltpu.VMEM((width, cols), F32),),
                )(tok, rates, old, own, *recvs)
            )
        packs.append(pair)

    second, seeds = [], []
    for h in range(heads):
        shard_list = start[h]
        order = [
            sum(jnp.where(lax.rem(me - r + n, n) == j, s, 0) for r, s in enumerate(shard_list))
            for j in range(n)
        ]
        begin = jnp.concatenate(order, axis=2)
        blank = jnp.zeros((held, width), BF16)
        begin_gu = jnp.concatenate(
            [
                jnp.concatenate([begin[0], begin[1]], axis=1),
                jnp.concatenate([blank, blank], axis=1),
            ],
            axis=0,
        )
        begin_down = jnp.concatenate([begin[2], blank], axis=0)
        seed_gu = jnp.where(leading, begin_gu, forward(packs[h][0]))
        seed_down = jnp.where(leading, begin_down, forward(packs[h][1]))
        seeds.append((seed_gu, seed_down))
        second.append(
            call(
                functools.partial(grads_two, h, divisor),
                "grads_two",
                grad_out,
                [SMEM, SMEM, rows_spec(1, h), rows_spec(1, h), p2, p1],
                (w2, w1, w2, w1),
                scratch,
            )(tok, decays, keys, values, seed_gu, seed_down)
        )

    out_shape = jax.ShapeDtypeStruct(keys.shape, BF16)
    any_spec = pl.BlockSpec(memory_space=pl.ANY)
    outputs = None
    for h in range(heads):
        prior = [] if outputs is None else [outputs]
        outputs = call(
            apply_one,
            "apply_one",
            out_shape,
            [rows_spec(0, h), p2, p1] + [any_spec] * len(prior),
            rows_spec(0, h),
            aliases={3: 0} if prior else None,
        )(queries, packs[h][0], packs[h][1], *prior)

    fast_shape = jax.ShapeDtypeStruct(fast_in.shape, BF16)
    moment_shape = jax.ShapeDtypeStruct(moment_in.shape, F32)
    fast_out = moment_out = None
    for h in range(heads):
        send_gu, send_down, own_gu, own_down = second[h]
        recv_gu, recv_down = others(send_gu), others(send_down)
        pair_spec = pl.BlockSpec((None, 2, None, width, part), lambda i, h=h: (0, 0, h, 0, 0))
        lone_spec = pl.BlockSpec((None, 1, None, width, part), lambda i, h=h: (0, 2, h, 0, 0))
        prior = [] if fast_out is None else [fast_out, moment_out]
        at = 5 + (n - 1)
        hq, fast_out, moment_out = call(
            functools.partial(update_two_gu, n, h),
            "update_two_gu",
            (shape(rows, width), fast_shape, moment_shape),
            [SMEM, SMEM, w2, w2, rows_spec(1, h)]
            + [w2] * (n - 1)
            + [any_spec] * len(prior),
            (whole_spec(rows, width), pair_spec, pair_spec),
            (pltpu.VMEM((width, 2 * width), BF16),),
            aliases={at: 1, at + 1: 2} if prior else None,
        )(tok, rates, seeds[h][0], own_gu, queries, *recv_gu, *prior)
        outputs, fast_out, moment_out = call(
            functools.partial(update_two_down, n, h),
            "update_two_down",
            (out_shape, fast_shape, moment_shape),
            [SMEM, SMEM, w1, w1, whole_spec(rows, width)]
            + [w1] * (n - 1)
            + [any_spec] * 3,
            (rows_spec(1, h), lone_spec, lone_spec),
            aliases={at: 0, at + 1: 1, at + 2: 2},
        )(
            tok,
            rates,
            seeds[h][1],
            own_down,
            hq,
            *recv_down,
            outputs,
            fast_out,
            moment_out,
        )
    return (outputs, fast_out, moment_out)


def solution(mesh):
    placed = (
        P(None, ("block", "tok"), None),
        P(None, ("block", "tok"), None),
        P(None, ("block", "tok"), None),
        P("block", None, None, None, "tok"),
        P("block", None, None, None, "tok"),
        P(None, None, None, "tok"),
        P(),
        P(),
    )
    step = jax.shard_map(
        on_device,
        mesh=mesh,
        in_specs=placed,
        out_specs=(
            P(None, ("block", "tok"), None),
            P("block", None, None, None, "tok"),
            P("block", None, None, None, "tok"),
        ),
        check_vma=False,
    )

    def run(*args):
        with jax.sharding.use_abstract_mesh(mesh.abstract_mesh):
            return step(*args)

    return run
```

```python
import functools

import jax
import jax.numpy as jnp
from jax import lax
from jax.experimental import pallas as pl
from jax.experimental.pallas import tpu as pltpu
from jax.sharding import PartitionSpec as P


F32 = jnp.float32
BF16 = jnp.bfloat16
VMEM = pl.BlockSpec(memory_space=pltpu.VMEM)
SMEM = pl.BlockSpec(memory_space=pltpu.SMEM)


def mm(a, b, dims):
    return lax.dot_general(a, b, (dims, ((), ())), preferred_element_type=F32)


def call(kernel, out, in_specs, out_specs, scratch=(), aliases=None, grid=()):
    return pl.pallas_call(
        kernel,
        grid=grid,
        out_shape=out,
        in_specs=in_specs,
        out_specs=out_specs,
        scratch_shapes=list(scratch),
        input_output_aliases=aliases or {},
        compiler_params=pltpu.CompilerParams(vmem_limit_bytes=12 << 20),
    )


def row_chunk(rows):
    for size in (256, 384, 128):
        if rows % size == 0:
            return size
    return rows


def shard_rows(me, r, n, part):
    source = lax.rem(me - r + n, n)
    return pl.multiple_of(source * part, part)


def assemble(me, shards, gu_ref, down_ref):
    n = len(shards)
    width = down_ref.shape[0]
    part = width // n
    for r, shard in enumerate(shards):
        at = shard_rows(me, r, n, part)
        gu_ref[pl.ds(at, part), :] = shard(0)
        gu_ref[pl.ds(width + at, part), :] = shard(1)
        down_ref[pl.ds(at, part), :] = shard(2)


def grads_core(divisor, keys, values, gu_ref, down_ref, own_gu, own_down, hid_s, dout_s, dgu_s):
    rows, width = hid_s.shape
    size = row_chunk(rows)
    for first in range(0, rows, size):
        at = pl.ds(first, size)
        both = mm(keys(at), gu_ref[...], ((1,), (1,)))
        gate, upper = both[:, :width], both[:, width:]
        dout = (-values(at).astype(F32) / divisor).astype(BF16)
        dhid = mm(dout, down_ref[...], ((1,), (0,)))
        sigma = jax.nn.sigmoid(gate)
        silu = gate * sigma
        hid_s[at, :] = (silu * upper).astype(BF16)
        dout_s[at, :] = dout
        dgu_s[at, :width] = (dhid * upper * sigma * (1.0 + gate * (1.0 - sigma))).astype(BF16)
        dgu_s[at, width:] = (dhid * silu).astype(BF16)
    own_gu[...] = mm(dgu_s[...], keys(pl.ds(0, rows)), ((0,), (0,)))
    own_down[...] = mm(dout_s[...], hid_s[...], ((0,), (0,)))


def take_head(head, fast_ref, own_ref):
    pltpu.sync_copy(fast_ref.at[0, :, head], own_ref)


def grads_one(n, head, divisor, tok_ref, decay_ref, k_ref, v_ref, m_ref, *refs):
    shards = refs[:n]
    gu_ref, down_ref, send_gu, send_down, own_gu, own_down, hid_s, dout_s, dgu_s = refs[n:]
    width = down_ref.shape[0]
    part = width // n
    me = tok_ref[0]
    assemble(me, [lambda m, ref=ref: ref[m] for ref in shards], gu_ref, down_ref)
    cols = pl.ds(head * width, width)
    grads_core(
        divisor,
        lambda at: k_ref[0, at, cols],
        lambda at: v_ref[0, at, cols],
        gu_ref,
        down_ref,
        own_gu,
        own_down,
        hid_s,
        dout_s,
        dgu_s,
    )
    decay = decay_ref[head]
    mine = pl.multiple_of(me * part, part)
    own_gu[pl.ds(mine, part), :] += decay * m_ref[0, 0, head]
    own_gu[pl.ds(width + mine, part), :] += decay * m_ref[0, 1, head]
    own_down[pl.ds(mine, part), :] += decay * m_ref[0, 2, head]
    send_gu[...] = own_gu[...].astype(BF16)
    send_down[...] = own_down[...].astype(BF16)


def grads_two(n, head, divisor, tok_ref, lead_ref, decay_ref, k_ref, v_ref, pgu_ref, pdown_ref, *refs):
    begins = refs[:n]
    gu_ref, down_ref, send_gu, send_down, own_gu, own_down, hid_s, dout_s, dgu_s = refs[n:]
    width = down_ref.shape[0]
    part = width // n
    me = tok_ref[0]
    leading = lead_ref[0] == 1

    @pl.when(leading)
    def _():
        assemble(me, [lambda m, ref=ref: ref[m, head] for ref in begins], gu_ref, down_ref)

    @pl.when(jnp.logical_not(leading))
    def _():
        gu_ref[...] = pgu_ref[: 2 * width, :]
        down_ref[...] = pdown_ref[:width, :]

    cols = pl.ds(head * width, width)
    grads_core(
        divisor,
        lambda at: k_ref[1, at, cols],
        lambda at: v_ref[1, at, cols],
        gu_ref,
        down_ref,
        own_gu,
        own_down,
        hid_s,
        dout_s,
        dgu_s,
    )
    decay = decay_ref[head]
    mine = pl.multiple_of(me * part, part)

    @pl.when(jnp.logical_not(leading))
    def _():
        for m in range(2):
            old = pgu_ref[2 * width + m * part : 2 * width + (m + 1) * part, :]
            own_gu[pl.ds(m * width + mine, part), :] += decay * old.astype(F32)
        own_down[pl.ds(mine, part), :] += decay * pdown_ref[width:, :].astype(F32)

    send_gu[...] = own_gu[...].astype(BF16)
    send_down[...] = own_down[...].astype(BF16)


def updated(rate, old_ref, own_ref, recvs, at):
    moment = own_ref[at, :]
    for recv in recvs:
        moment = moment + recv[at, :].astype(F32)
    old = old_ref[at, :].astype(F32)
    moved = old - rate * moment
    old_norm = jnp.sqrt(jnp.mean(old * old, axis=1, keepdims=True) + 1e-06)
    new_norm = jnp.sqrt(jnp.mean(moved * moved, axis=1, keepdims=True) + 1e-06)
    return (moved * (old_norm / new_norm)).astype(BF16), moment


def update_one(n, head, mats, tok_ref, rate_ref, old_ref, own_ref, *refs):
    recvs = refs[: n - 1]
    pack_ref, moment_s = refs[n - 1 :]
    width = own_ref.shape[1]
    part = width // n
    total = len(mats) * width
    mine = pl.multiple_of(tok_ref[0] * part, part)
    for i, m in enumerate(mats):
        at = pl.ds(i * width, width)
        new, moment = updated(rate_ref[head, m], old_ref, own_ref, recvs, at)
        pack_ref[at, :] = new
        moment_s[...] = moment
        pack_ref[pl.ds(total + i * part, part), :] = moment_s[pl.ds(mine, part), :].astype(BF16)


def update_two_gu(n, head, tok_ref, rate_ref, old_ref, own_ref, q_ref, *refs):
    recvs = refs[: n - 1]
    hq_ref, fast_ref, moment_ref, gu_s, moment_s = refs[-5:]
    width = own_ref.shape[1]
    part = width // n
    mine = pl.multiple_of(tok_ref[0] * part, part)
    for m in range(2):
        at = pl.ds(m * width, width)
        new, moment = updated(rate_ref[head, m], old_ref, own_ref, recvs, at)
        gu_s[at, :] = new
        moment_s[...] = moment
        fast_ref[m] = gu_s[pl.ds(m * width + mine, part), :]
        moment_ref[m] = moment_s[pl.ds(mine, part), :]
    cols = pl.ds(head * width, width)
    rows = q_ref.shape[1]
    size = row_chunk(rows)
    for first in range(0, rows, size):
        at = pl.ds(first, size)
        both = mm(q_ref[1, at, cols], gu_s[...], ((1,), (1,)))
        hq_ref[at, :] = (jax.nn.silu(both[:, :width]) * both[:, width:]).astype(BF16)


def update_two_down(n, head, tok_ref, rate_ref, old_ref, own_ref, hq_ref, *refs):
    recvs = refs[: n - 1]
    out_ref, fast_ref, moment_ref, down_s, moment_s = refs[-5:]
    width = own_ref.shape[1]
    part = width // n
    mine = pl.multiple_of(tok_ref[0] * part, part)
    new, moment = updated(rate_ref[head, 2], old_ref, own_ref, recvs, pl.ds(0, width))
    down_s[...] = new
    moment_s[...] = moment
    fast_ref[...] = down_s[pl.ds(mine, part), :]
    moment_ref[...] = moment_s[pl.ds(mine, part), :]
    out_ref[...] = mm(hq_ref[...], down_s[...], ((1,), (1,))).astype(BF16)


def apply_one(head, q_ref, pgu_ref, pdown_ref, *refs):
    out_ref = refs[-1]
    rows, width = out_ref.shape
    cols = pl.ds(head * width, width)
    size = row_chunk(rows)
    for first in range(0, rows, size):
        at = pl.ds(first, size)
        both = mm(q_ref[0, at, cols], pgu_ref[: 2 * width, :], ((1,), (1,)))
        hq = (jax.nn.silu(both[:, :width]) * both[:, width:]).astype(BF16)
        out_ref[at, :] = mm(hq, pdown_ref[:width, :], ((1,), (1,))).astype(BF16)


def on_device(keys, values, queries, fast_in, moment_in, initial_fast, rates, decays):
    n = lax.axis_size("tok")
    blocks = lax.axis_size("block")
    _, rows, features = keys.shape
    heads = rates.shape[1]
    width = features // heads
    part = width // n
    divisor = float(rows * n)
    tok = lax.axis_index("tok").astype(jnp.int32).reshape(1)
    lead = (lax.axis_index("block") == 0).astype(jnp.int32).reshape(1)
    fast_t = jnp.swapaxes(fast_in, 3, 4)
    moment_t = jnp.swapaxes(moment_in, 3, 4)
    begin_t = jnp.swapaxes(initial_fast, 2, 3)
    rates = rates.T

    def others(x):
        return [lax.ppermute(x, "tok", [(i, (i + r) % n) for i in range(n)]) for r in range(1, n)]

    def forward(x):
        return lax.ppermute(x, "block", [(i, i + 1) for i in range(blocks - 1)])

    def shape(*dims, dtype=BF16):
        return jax.ShapeDtypeStruct(dims, dtype)

    def out_spec(step, head):
        return pl.BlockSpec((None, rows, width), lambda i: (step, 0, head))

    scratch = (
        pltpu.VMEM((rows, width), BF16),
        pltpu.VMEM((rows, width), BF16),
        pltpu.VMEM((rows, 2 * width), BF16),
    )
    grad_out = (
        shape(2 * width, width),
        shape(width, width),
        shape(2 * width, width),
        shape(width, width),
        shape(2 * width, width, dtype=F32),
        shape(width, width, dtype=F32),
    )

    owned = [
        call(
            functools.partial(take_head, h),
            shape(3, part, width),
            [pl.BlockSpec(memory_space=pl.ANY)],
            VMEM,
        )(fast_t)
        for h in range(heads)
    ]
    recv_fast = [others(x) for x in owned]
    first = [
        call(
            functools.partial(grads_one, n, h, divisor),
            grad_out,
            [SMEM, SMEM] + [VMEM] * (4 + n - 1),
            (VMEM,) * 6,
            scratch,
        )(tok, decays, keys, values, moment_t, owned[h], *recv_fast[h])
        for h in range(heads)
    ]
    begins = [begin_t] + [
        lax.ppermute(begin_t, ("block", "tok"), [(i, (i + r) % n) for i in range(n)])
        for r in range(1, n)
    ]

    packs = []
    for h in range(heads):
        gu, down, send_gu, send_down, own_gu, own_down = first[h]
        recv_gu, recv_down = others(send_gu), others(send_down)
        pair = []
        for mats, old, own, recvs in (
            ((0, 1), gu, own_gu, recv_gu), ((2,), down, own_down, recv_down)
        ):
            pair.append(
                call(
                    functools.partial(update_one, n, h, mats),
                    shape(len(mats) * (width + part), width),
                    [SMEM, SMEM] + [VMEM] * (2 + n - 1),
                    VMEM,
                    (pltpu.VMEM((width, width), F32),),
                )(tok, rates, old, own, *recvs)
            )
        packs.append(pair)

    second = [
        call(
            functools.partial(grads_two, n, h, divisor),
            grad_out,
            [SMEM, SMEM, SMEM] + [VMEM] * (4 + n),
            (VMEM,) * 6,
            scratch,
        )(tok, lead, decays, keys, values, forward(packs[h][0]), forward(packs[h][1]), *begins)
        for h in range(heads)
    ]

    out_shape = jax.ShapeDtypeStruct(keys.shape, BF16)
    any_spec = pl.BlockSpec(memory_space=pl.ANY)
    outputs = None
    for h in range(heads):
        prior = [] if outputs is None else [outputs]
        outputs = call(
            functools.partial(apply_one, h),
            out_shape,
            [VMEM] * 3 + [any_spec] * len(prior),
            out_spec(0, h),
            aliases={3: 0} if prior else None,
            grid=(1,),
        )(queries, packs[h][0], packs[h][1], *prior)

    fast_shape = jax.ShapeDtypeStruct(fast_t.shape, BF16)
    moment_shape = jax.ShapeDtypeStruct(moment_t.shape, F32)
    fast_out = moment_out = None
    for h in range(heads):
        gu, down, send_gu, send_down, own_gu, own_down = second[h]
        recv_gu, recv_down = others(send_gu), others(send_down)
        pair_spec = pl.BlockSpec((None, 2, None, part, width), lambda i, h=h: (0, 0, h, 0, 0))
        lone_spec = pl.BlockSpec((None, None, None, part, width), lambda i, h=h: (0, 2, h, 0, 0))
        prior = [] if fast_out is None else [fast_out, moment_out]
        at = 5 + (n - 1)
        hq, fast_out, moment_out = call(
            functools.partial(update_two_gu, n, h),
            (shape(rows, width), fast_shape, moment_shape),
            [SMEM, SMEM] + [VMEM] * (3 + n - 1) + [any_spec] * len(prior),
            (VMEM, pair_spec, pair_spec),
            (pltpu.VMEM((2 * width, width), BF16), pltpu.VMEM((width, width), F32)),
            aliases={at: 1, at + 1: 2} if prior else None,
            grid=(1,),
        )(tok, rates, gu, own_gu, queries, *recv_gu, *prior)
        outputs, fast_out, moment_out = call(
            functools.partial(update_two_down, n, h),
            (out_shape, fast_shape, moment_shape),
            [SMEM, SMEM] + [VMEM] * (3 + n - 1) + [any_spec] * 3,
            (out_spec(1, h), lone_spec, lone_spec),
            (pltpu.VMEM((width, width), BF16), pltpu.VMEM((width, width), F32)),
            aliases={at: 0, at + 1: 1, at + 2: 2},
            grid=(1,),
        )(tok, rates, down, own_down, hq, *recv_down, outputs, fast_out, moment_out)
    return (outputs, jnp.swapaxes(fast_out, 3, 4), jnp.swapaxes(moment_out, 3, 4))


def solution(mesh):
    placed = (
        P(None, ("block", "tok"), None),
        P(None, ("block", "tok"), None),
        P(None, ("block", "tok"), None),
        P("block", None, None, None, "tok"),
        P("block", None, None, None, "tok"),
        P(None, None, None, "tok"),
        P(),
        P(),
    )
    step = jax.shard_map(
        on_device,
        mesh=mesh,
        in_specs=placed,
        out_specs=(
            P(None, ("block", "tok"), None),
            P("block", None, None, None, "tok"),
            P("block", None, None, None, "tok"),
        ),
        check_vma=False,
    )

    def run(*args):
        with jax.sharding.use_abstract_mesh(mesh.abstract_mesh):
            return step(*args)

    return run
```

```python
import functools

import jax
import jax.numpy as jnp
from jax import lax
from jax.experimental import pallas as pl
from jax.experimental.pallas import tpu as pltpu
from jax.sharding import PartitionSpec as P


F32 = jnp.float32
BF16 = jnp.bfloat16
VMEM = pl.BlockSpec(memory_space=pltpu.VMEM)
SMEM = pl.BlockSpec(memory_space=pltpu.SMEM)
HBM = pl.BlockSpec(memory_space=pltpu.HBM)
DMA = pltpu.SemaphoreType.DMA


def mm(a, b, dims):
    return lax.dot_general(a, b, (dims, ((), ())), preferred_element_type=F32)


def call(kernel, out, in_specs, out_specs, scratch=(), aliases=None):
    return pl.pallas_call(
        kernel,
        out_shape=out,
        in_specs=in_specs,
        out_specs=out_specs,
        scratch_shapes=list(scratch),
        input_output_aliases=aliases or {},
        compiler_params=pltpu.CompilerParams(vmem_limit_bytes=12 << 20),
    )


def row_chunks(rows):
    for size in (256, 384, 128):
        if rows % size == 0:
            return [pl.ds(first, size) for first in range(0, rows, size)]
    return [pl.ds(0, rows)]


def fetch_rows(step, head, ref, scratch, sems, which):
    rows, width = scratch.shape
    copies = [
        pltpu.make_async_copy(
            ref.at[step, at, pl.ds(head * width, width)], scratch.at[at, :], sems.at[which, i]
        )
        for i, at in enumerate(row_chunks(rows))
    ]
    for copy in copies:
        copy.start()
    return copies


def assemble(me, shards, gu_ref, down_ref):
    n = len(shards)
    width = down_ref.shape[0]
    part = width // n
    for r, shard in enumerate(shards):
        at = pl.multiple_of(lax.rem(me - r + n, n) * part, part)
        gu_ref[pl.ds(at, part), :] = shard(0)
        gu_ref[pl.ds(width + at, part), :] = shard(1)
        down_ref[pl.ds(at, part), :] = shard(2)


def grads_core(divisor, loads, k_s, v_s, gu_ref, down_ref, own_gu, own_down, hid_s, dout_s, dgu_s):
    rows, width = k_s.shape
    for at, load_k, load_v in zip(row_chunks(rows), *loads):
        load_k.wait()
        both = mm(k_s[at, :], gu_ref[...], ((1,), (1,)))
        gate, upper = both[:, :width], both[:, width:]
        load_v.wait()
        dout = (-v_s[at, :].astype(F32) / divisor).astype(BF16)
        dhid = mm(dout, down_ref[...], ((1,), (0,)))
        sigma = jax.nn.sigmoid(gate)
        silu = gate * sigma
        hid_s[at, :] = (silu * upper).astype(BF16)
        dout_s[at, :] = dout
        dgu_s[at, :width] = (dhid * upper * sigma * (1.0 + gate * (1.0 - sigma))).astype(BF16)
        dgu_s[at, width:] = (dhid * silu).astype(BF16)
    own_gu[...] = mm(dgu_s[...], k_s[...], ((0,), (0,)))
    own_down[...] = mm(dout_s[...], hid_s[...], ((0,), (0,)))


def round_out(own_gu, own_down, send_gate, send_up, send_down):
    width = own_down.shape[0]
    send_gate[...] = own_gu[:width, :].astype(BF16)
    send_up[...] = own_gu[width:, :].astype(BF16)
    send_down[...] = own_down[...].astype(BF16)


def take_head(head, fast_ref, own_ref):
    pltpu.sync_copy(fast_ref.at[0, :, head], own_ref)


def take_piece(sources, block_ref, begin_ref, piece_ref):
    block = block_ref[0]
    piece = jnp.int32(0)
    for p, source in enumerate(sources):
        piece = jnp.where(block == source, jnp.int32(p), piece)
    heads = begin_ref.shape[1]
    pltpu.sync_copy(begin_ref.at[piece // heads, lax.rem(piece, heads)], piece_ref)


def grads_one(n, head, divisor, tok_ref, decay_ref, k_ref, v_ref, m_ref, *refs):
    shards = refs[:n]
    gu_ref, down_ref, send_gate, send_up, send_down, own_gu, own_down = refs[n : n + 7]
    k_s, v_s, m_s, hid_s, dout_s, dgu_s, sems, m_sem = refs[n + 7 :]
    loads = (
        fetch_rows(0, head, k_ref, k_s, sems, 0),
        fetch_rows(0, head, v_ref, v_s, sems, 1),
    )
    load_m = pltpu.make_async_copy(m_ref.at[0, :, head], m_s, m_sem)
    load_m.start()
    width = down_ref.shape[0]
    part = width // n
    me = tok_ref[0]
    assemble(me, [lambda m, ref=ref: ref[m] for ref in shards], gu_ref, down_ref)
    grads_core(
        divisor, loads, k_s, v_s, gu_ref, down_ref, own_gu, own_down, hid_s, dout_s, dgu_s
    )
    decay = decay_ref[head]
    mine = pl.multiple_of(me * part, part)
    load_m.wait()
    own_gu[pl.ds(mine, part), :] += decay * m_s[0]
    own_gu[pl.ds(width + mine, part), :] += decay * m_s[1]
    own_down[pl.ds(mine, part), :] += decay * m_s[2]
    round_out(own_gu, own_down, send_gate, send_up, send_down)


def grads_two(n, head, divisor, tok_ref, block_ref, decay_ref, k_ref, v_ref, begin_ref, *refs):
    packs, pieces = refs[:3], refs[3 : 3 * n]
    gu_ref, down_ref, send_gate, send_up, send_down, own_gu, own_down = refs[3 * n : 3 * n + 7]
    k_s, v_s, b_s, hid_s, dout_s, dgu_s, sems, b_sem = refs[3 * n + 7 :]
    loads = (
        fetch_rows(1, head, k_ref, k_s, sems, 0),
        fetch_rows(1, head, v_ref, v_s, sems, 1),
    )
    load_b = pltpu.make_async_copy(begin_ref.at[:, head], b_s, b_sem)
    load_b.start()
    width = down_ref.shape[0]
    part = width // n
    me = tok_ref[0]
    leading = block_ref[0] == 0
    load_b.wait()

    @pl.when(leading)
    def _():
        shards = [lambda m: b_s[m]]
        for r in range(n - 1):
            shards.append(lambda m, r=r: pieces[3 * r + m][...])
        assemble(me, shards, gu_ref, down_ref)

    @pl.when(jnp.logical_not(leading))
    def _():
        gu_ref[:width, :] = packs[0][:width, :]
        gu_ref[width:, :] = packs[1][:width, :]
        down_ref[...] = packs[2][:width, :]

    grads_core(
        divisor, loads, k_s, v_s, gu_ref, down_ref, own_gu, own_down, hid_s, dout_s, dgu_s
    )
    decay = decay_ref[head]
    mine = pl.multiple_of(me * part, part)

    @pl.when(jnp.logical_not(leading))
    def _():
        own_gu[pl.ds(mine, part), :] += decay * packs[0][width:, :].astype(F32)
        own_gu[pl.ds(width + mine, part), :] += decay * packs[1][width:, :].astype(F32)
        own_down[pl.ds(mine, part), :] += decay * packs[2][width:, :].astype(F32)

    round_out(own_gu, own_down, send_gate, send_up, send_down)


def updated(rate, old_ref, own_ref, recvs, first):
    width = own_ref.shape[1]
    at = pl.ds(first, width)
    moment = own_ref[at, :]
    for recv in recvs:
        moment = moment + recv[...].astype(F32)
    old = old_ref[at, :].astype(F32)
    moved = old - rate * moment
    old_norm = jnp.sqrt(jnp.mean(old * old, axis=1, keepdims=True) + 1e-06)
    new_norm = jnp.sqrt(jnp.mean(moved * moved, axis=1, keepdims=True) + 1e-06)
    return (moved * (old_norm / new_norm)).astype(BF16), moment


def update_one(n, head, m, tok_ref, rate_ref, old_ref, own_ref, *refs):
    recvs = refs[: n - 1]
    pack_ref, moment_s = refs[n - 1 :]
    width = own_ref.shape[1]
    part = width // n
    mine = pl.multiple_of(tok_ref[0] * part, part)
    first = width if m == 1 else 0
    new, moment = updated(rate_ref[head, m], old_ref, own_ref, recvs, first)
    pack_ref[:width, :] = new
    moment_s[...] = moment
    pack_ref[width:, :] = moment_s[pl.ds(mine, part), :].astype(BF16)


def update_two(n, head, m, tok_ref, rate_ref, old_ref, own_ref, *refs):
    recvs = refs[: n - 1]
    rest = refs[n - 1 :]
    width = own_ref.shape[1]
    part = width // n
    mine = pl.multiple_of(tok_ref[0] * part, part)
    first = width if m == 1 else 0
    new_s, moment_s, fast_s, mine_s, sems = rest[-5:]
    if m == 0:
        new_ref, fast_ref, moment_ref = rest[-8:-5]
    elif m == 1:
        q_ref, gate_ref = rest[:2]
        new_ref = new_s
        q_s, q_sems = rest[-7:-5]
        hq_ref, fast_ref, moment_ref = rest[-10:-7]
        load_q = fetch_rows(1, head, q_ref, q_s, q_sems, 0)
    else:
        hq_ref = rest[0]
        new_ref = new_s
        out_s, out_sems = rest[-7:-5]
        out_ref, fast_ref, moment_ref = rest[-10:-7]
    new, moment = updated(rate_ref[head, m], old_ref, own_ref, recvs, first)
    new_ref[...] = new
    moment_s[...] = moment
    fast_s[...] = new_ref[pl.ds(mine, part), :]
    mine_s[...] = moment_s[pl.ds(mine, part), :]
    stores = [
        pltpu.make_async_copy(fast_s, fast_ref.at[0, m, head], sems.at[0]),
        pltpu.make_async_copy(mine_s, moment_ref.at[0, m, head], sems.at[1]),
    ]
    for store in stores:
        store.start()
    if m == 1:
        for at, load in zip(row_chunks(q_s.shape[0]), load_q):
            load.wait()
            gate = mm(q_s[at, :], gate_ref[...], ((1,), (1,)))
            upper = mm(q_s[at, :], new_ref[...], ((1,), (1,)))
            hq_ref[at, :] = (jax.nn.silu(gate) * upper).astype(BF16)
    if m == 2:
        for i, at in enumerate(row_chunks(hq_ref.shape[0])):
            out_s[at, :] = mm(hq_ref[at, :], new_ref[...], ((1,), (1,))).astype(BF16)
            store = pltpu.make_async_copy(
                out_s.at[at, :],
                out_ref.at[1, at, pl.ds(head * width, width)],
                out_sems.at[0, i],
            )
            store.start()
            stores.append(store)
    for store in stores:
        store.wait()


def apply_one(head, q_ref, gate_ref, up_ref, down_ref, *refs):
    out_ref, q_s, out_s, sems = refs[-4:]
    rows, width = q_s.shape
    loads = fetch_rows(0, head, q_ref, q_s, sems, 0)
    stores = []
    for i, at in enumerate(row_chunks(rows)):
        loads[i].wait()
        gate = mm(q_s[at, :], gate_ref[:width, :], ((1,), (1,)))
        upper = mm(q_s[at, :], up_ref[:width, :], ((1,), (1,)))
        hq = (jax.nn.silu(gate) * upper).astype(BF16)
        out_s[at, :] = mm(hq, down_ref[:width, :], ((1,), (1,))).astype(BF16)
        store = pltpu.make_async_copy(
            out_s.at[at, :], out_ref.at[0, at, pl.ds(head * width, width)], sems.at[1, i]
        )
        store.start()
        stores.append(store)
    for store in stores:
        store.wait()


def on_device(keys, values, queries, fast_in, moment_in, initial_fast, rates, decays):
    n = lax.axis_size("tok")
    blocks = lax.axis_size("block")
    _, rows, features = keys.shape
    heads = rates.shape[1]
    width = features // heads
    part = width // n
    chunks = len(row_chunks(rows))
    divisor = float(rows * n)
    tok = lax.axis_index("tok").astype(jnp.int32).reshape(1)
    block = lax.axis_index("block").astype(jnp.int32).reshape(1)
    fast_t = jnp.swapaxes(fast_in, 3, 4)
    moment_t = jnp.swapaxes(moment_in, 3, 4)
    begin_t = jnp.swapaxes(initial_fast, 2, 3)
    rates = rates.T
    keys, values, queries, fast_t, moment_t, begin_t = (
        pltpu.with_memory_space_constraint(x, pltpu.HBM)
        for x in (keys, values, queries, fast_t, moment_t, begin_t)
    )

    def turned(x):
        return [lax.ppermute(x, "tok", [(i, (i + r) % n) for i in range(n)]) for r in range(1, n)]

    def forward(x):
        return lax.ppermute(x, "block", [(i, i + 1) for i in range(blocks - 1)])

    def shape(*dims, dtype=BF16):
        return jax.ShapeDtypeStruct(dims, dtype)

    matrix = shape(width, width)
    row_scratch = pltpu.VMEM((rows, width), BF16)
    grad_scratch = (
        row_scratch,
        row_scratch,
        None,
        row_scratch,
        row_scratch,
        pltpu.VMEM((rows, 2 * width), BF16),
        DMA((2, chunks)),
        DMA(()),
    )
    grad_out = (
        shape(2 * width, width),
        matrix,
        matrix,
        matrix,
        matrix,
        shape(2 * width, width, dtype=F32),
        shape(width, width, dtype=F32),
    )

    def grad_call(kernel, n_vmem, extra, hbm_at):
        scratch = tuple(pltpu.VMEM((3, part, width), extra) if s is None else s for s in grad_scratch)
        specs = [SMEM] * hbm_at + [HBM] * 3 + [VMEM] * n_vmem
        return call(kernel, grad_out, specs, (VMEM,) * 7, scratch)

    recv_fast, owned = [], []
    for h in range(heads):
        owned.append(
            call(functools.partial(take_head, h), shape(3, part, width), [HBM], VMEM)(fast_t)
        )
        recv_fast.append(turned(owned[h]))

    n_pieces = 3 * heads
    sources = [(2 * (p + 1)) % blocks for p in range(n_pieces)]
    piece = call(
        functools.partial(take_piece, sources), shape(part, width), [SMEM, HBM], VMEM
    )(block, begin_t)
    crossed = [
        lax.ppermute(
            piece,
            ("block", "tok"),
            [(s * n + i, s * n + (i + r) % n) for s in sorted(set(sources)) for i in range(n)],
        )
        for r in range(1, n)
    ]

    first = [
        grad_call(functools.partial(grads_one, n, h, divisor), n, F32, 2)(
            tok, decays, keys, values, moment_t, owned[h], *recv_fast[h]
        )
        for h in range(heads)
    ]

    def olds(state):
        gu, down, own_gu, own_down = state[0], state[1], state[5], state[6]
        return ((gu, own_gu), (gu, own_gu), (down, own_down))

    packs = []
    for h in range(heads):
        packs.append([])
        for m in range(3):
            recvs = turned(first[h][2 + m])
            old, own = olds(first[h])[m]
            packs[h].append(
                call(
                    functools.partial(update_one, n, h, m),
                    shape(width + part, width),
                    [SMEM, SMEM] + [VMEM] * (1 + n),
                    VMEM,
                    (pltpu.VMEM((width, width), F32),),
                )(tok, rates, old, own, *recvs)
            )

    begins = []
    for p in range(n_pieces):
        begins.append(
            [
                lax.ppermute(
                    x, ("block", "tok"), [(sources[p] * n + i, i) for i in range(n)]
                )
                for x in crossed
            ]
        )

    second = []
    for h in range(heads):
        arrived = [forward(packs[h][m]) for m in range(3)]
        pieces = [begins[m * heads + h][r] for r in range(n - 1) for m in range(3)]
        second.append(
            grad_call(
                functools.partial(grads_two, n, h, divisor), 3 * n, BF16, 3
            )(tok, block, decays, keys, values, begin_t, *arrived, *pieces)
        )

    out_shape = jax.ShapeDtypeStruct(keys.shape, BF16)
    outputs = None
    for h in range(heads):
        prior = [] if outputs is None else [outputs]
        outputs = call(
            functools.partial(apply_one, h),
            out_shape,
            [HBM] + [VMEM] * 3 + [HBM] * len(prior),
            HBM,
            (row_scratch, row_scratch, DMA((2, chunks))),
            aliases={4: 0} if prior else None,
        )(queries, *packs[h], *prior)

    fast_shape = jax.ShapeDtypeStruct(fast_t.shape, BF16)
    moment_shape = jax.ShapeDtypeStruct(moment_t.shape, F32)
    ends = []
    last_scratch = (
        pltpu.VMEM((width, width), BF16),
        pltpu.VMEM((width, width), F32),
        pltpu.VMEM((part, width), BF16),
        pltpu.VMEM((part, width), F32),
        DMA((2,)),
    )
    for h in range(heads):
        recvs = [turned(second[h][2 + m]) for m in range(3)]
        state = olds(second[h])
        at = 4 + (n - 1)
        specs = [SMEM, SMEM] + [VMEM] * (1 + n)
        rows_sems = (row_scratch, DMA((1, chunks)))
        gate, *ends = call(
            functools.partial(update_two, n, h, 0),
            (matrix, fast_shape, moment_shape),
            specs + [HBM] * len(ends),
            (VMEM, HBM, HBM),
            last_scratch,
            aliases={at: 1, at + 1: 2} if ends else None,
        )(tok, rates, *state[0], *recvs[0], *ends)
        hq, *ends = call(
            functools.partial(update_two, n, h, 1),
            (shape(rows, width), fast_shape, moment_shape),
            specs + [HBM, VMEM, HBM, HBM],
            (VMEM, HBM, HBM),
            rows_sems + last_scratch,
            aliases={at + 2: 1, at + 3: 2},
        )(tok, rates, *state[1], *recvs[1], queries, gate, *ends)
        outputs, *ends = call(
            functools.partial(update_two, n, h, 2),
            (out_shape, fast_shape, moment_shape),
            specs + [VMEM] + [HBM] * 3,
            (HBM,) * 3,
            rows_sems + last_scratch,
            aliases={at + 1: 0, at + 2: 1, at + 3: 2},
        )(tok, rates, *state[2], *recvs[2], hq, outputs, *ends)
    return (outputs, jnp.swapaxes(ends[0], 3, 4), jnp.swapaxes(ends[1], 3, 4))


def solution(mesh):
    placed = (
        P(None, ("block", "tok"), None),
        P(None, ("block", "tok"), None),
        P(None, ("block", "tok"), None),
        P("block", None, None, None, "tok"),
        P("block", None, None, None, "tok"),
        P(None, None, None, "tok"),
        P(),
        P(),
    )
    step = jax.shard_map(
        on_device,
        mesh=mesh,
        in_specs=placed,
        out_specs=(
            P(None, ("block", "tok"), None),
            P("block", None, None, None, "tok"),
            P("block", None, None, None, "tok"),
        ),
        check_vma=False,
    )

    def run(*args):
        with jax.sharding.use_abstract_mesh(mesh.abstract_mesh):
            return step(*args)

    return run
```

```python
import functools

import jax
import jax.numpy as jnp
from jax import lax
from jax.experimental import pallas as pl
from jax.experimental.pallas import tpu as pltpu
from jax.sharding import PartitionSpec as P


F32 = jnp.float32
BF16 = jnp.bfloat16
VMEM = pl.BlockSpec(memory_space=pltpu.VMEM)
SMEM = pl.BlockSpec(memory_space=pltpu.SMEM)
HBM = pl.BlockSpec(memory_space=pltpu.HBM)
DMA = pltpu.SemaphoreType.DMA


def mm(a, b, dims):
    return lax.dot_general(a, b, (dims, ((), ())), preferred_element_type=F32)


def call(kernel, out, in_specs, out_specs, scratch=(), aliases=None):
    return pl.pallas_call(
        kernel,
        out_shape=out,
        in_specs=in_specs,
        out_specs=out_specs,
        scratch_shapes=list(scratch),
        input_output_aliases=aliases or {},
        compiler_params=pltpu.CompilerParams(vmem_limit_bytes=12 << 20),
    )


def row_chunks(rows):
    for size in (256, 384, 128):
        if rows % size == 0:
            return [pl.ds(first, size) for first in range(0, rows, size)]
    return [pl.ds(0, rows)]


def assemble(me, shards, gu_ref, down_ref):
    n = len(shards)
    width = down_ref.shape[0]
    part = width // n
    for r, shard in enumerate(shards):
        at = pl.multiple_of(lax.rem(me - r + n, n) * part, part)
        gu_ref[pl.ds(at, part), :] = shard(0)
        gu_ref[pl.ds(width + at, part), :] = shard(1)
        down_ref[pl.ds(at, part), :] = shard(2)


def grads_core(divisor, k_ref, v_ref, gu_ref, down_ref, own_gu, own_down, hid_s, dout_s, dgu_s):
    rows, width = k_ref.shape
    for at in row_chunks(rows):
        both = mm(k_ref[at, :], gu_ref[...], ((1,), (1,)))
        gate, upper = both[:, :width], both[:, width:]
        dout = (-v_ref[at, :].astype(F32) / divisor).astype(BF16)
        dhid = mm(dout, down_ref[...], ((1,), (0,)))
        sigma = jax.nn.sigmoid(gate)
        silu = gate * sigma
        hid_s[at, :] = (silu * upper).astype(BF16)
        dout_s[at, :] = dout
        dgu_s[at, :width] = (dhid * upper * sigma * (1.0 + gate * (1.0 - sigma))).astype(BF16)
        dgu_s[at, width:] = (dhid * silu).astype(BF16)
    own_gu[...] = mm(dgu_s[...], k_ref[...], ((0,), (0,)))
    own_down[...] = mm(dout_s[...], hid_s[...], ((0,), (0,)))


def take_head(head, fast_ref, own_ref):
    pltpu.sync_copy(fast_ref.at[0, :, head], own_ref)


def take_piece(sources, block_ref, begin_ref, piece_ref):
    block = block_ref[0]
    piece = jnp.int32(0)
    for p, source in enumerate(sources):
        piece = jnp.where(block == source, jnp.int32(p), piece)
    pltpu.sync_copy(begin_ref.at[piece], piece_ref)


def load_all(steps, heads, k_ref, v_ref, q_ref, m_ref, begin_ref, *refs):
    sems = refs[-1]
    copies = []

    def add(source, target):
        copies.append(pltpu.make_async_copy(source, target, sems.at[len(copies)]))
        copies[-1].start()

    targets = list(refs[:-1])
    for step in range(steps):
        for head in range(heads):
            for ref in (k_ref, v_ref, q_ref):
                target = targets.pop(0)
                width = target.shape[1]
                add(ref.at[step, :, pl.ds(head * width, width)], target)
    for head in range(heads):
        add(m_ref.at[0, :, head], targets.pop(0))
    for head in range(heads):
        add(begin_ref.at[:, head], targets.pop(0))
    for copy in copies:
        copy.wait()


def grads_one(n, head, divisor, tok_ref, decay_ref, k_ref, v_ref, m_ref, *refs):
    shards = refs[:n]
    gu_ref, down_ref, send_gu, send_down, own_gu, own_down, hid_s, dout_s, dgu_s = refs[n:]
    width = down_ref.shape[0]
    part = width // n
    me = tok_ref[0]
    assemble(me, [lambda m, ref=ref: ref[m] for ref in shards], gu_ref, down_ref)
    grads_core(divisor, k_ref, v_ref, gu_ref, down_ref, own_gu, own_down, hid_s, dout_s, dgu_s)
    decay = decay_ref[head]
    mine = pl.multiple_of(me * part, part)
    own_gu[pl.ds(mine, part), :] += decay * m_ref[0]
    own_gu[pl.ds(width + mine, part), :] += decay * m_ref[1]
    own_down[pl.ds(mine, part), :] += decay * m_ref[2]
    send_gu[...] = own_gu[...].astype(BF16)
    send_down[...] = own_down[...].astype(BF16)


def grads_two(n, head, divisor, tok_ref, block_ref, decay_ref, k_ref, v_ref, begin_ref, *refs):
    (pgu_ref, pdown_ref), pieces = refs[:2], refs[2 : 2 + 3 * (n - 1)]
    gu_ref, down_ref, send_gu, send_down, own_gu, own_down, hid_s, dout_s, dgu_s = refs[-9:]
    width = down_ref.shape[0]
    part = width // n
    me = tok_ref[0]
    leading = block_ref[0] == 0

    @pl.when(leading)
    def _():
        shards = [lambda m: begin_ref[m]]
        for r in range(n - 1):
            shards.append(lambda m, r=r: pieces[3 * r + m][head])
        assemble(me, shards, gu_ref, down_ref)

    @pl.when(jnp.logical_not(leading))
    def _():
        gu_ref[...] = pgu_ref[: 2 * width, :]
        down_ref[...] = pdown_ref[:width, :]

    grads_core(divisor, k_ref, v_ref, gu_ref, down_ref, own_gu, own_down, hid_s, dout_s, dgu_s)
    decay = decay_ref[head]
    mine = pl.multiple_of(me * part, part)

    @pl.when(jnp.logical_not(leading))
    def _():
        for m in range(2):
            old = pgu_ref[2 * width + m * part : 2 * width + (m + 1) * part, :]
            own_gu[pl.ds(m * width + mine, part), :] += decay * old.astype(F32)
        own_down[pl.ds(mine, part), :] += decay * pdown_ref[width:, :].astype(F32)

    send_gu[...] = own_gu[...].astype(BF16)
    send_down[...] = own_down[...].astype(BF16)


def updated(rate, old_ref, own_ref, recvs, first):
    width = own_ref.shape[1]
    at = pl.ds(first, width)
    moment = own_ref[at, :]
    for recv in recvs:
        moment = moment + recv[at, :].astype(F32)
    old = old_ref[at, :].astype(F32)
    moved = old - rate * moment
    old_norm = jnp.sqrt(jnp.mean(old * old, axis=1, keepdims=True) + 1e-06)
    new_norm = jnp.sqrt(jnp.mean(moved * moved, axis=1, keepdims=True) + 1e-06)
    return (moved * (old_norm / new_norm)).astype(BF16), moment


def update_one(n, head, mats, tok_ref, rate_ref, old_ref, own_ref, *refs):
    recvs = refs[: n - 1]
    pack_ref, moment_s = refs[n - 1 :]
    width = own_ref.shape[1]
    part = width // n
    total = len(mats) * width
    mine = pl.multiple_of(tok_ref[0] * part, part)
    for i, m in enumerate(mats):
        new, moment = updated(rate_ref[head, m], old_ref, own_ref, recvs, i * width)
        pack_ref[i * width : (i + 1) * width, :] = new
        moment_s[...] = moment
        held = slice(total + i * part, total + (i + 1) * part)
        pack_ref[held, :] = moment_s[pl.ds(mine, part), :].astype(BF16)


def store_mine(n, m, head, me, new_s, moment_s, fast_s, mine_s, fast_ref, moment_ref, sems):
    width = moment_s.shape[1]
    part = width // n
    mine = pl.multiple_of(me * part, part)
    fast_s[...] = new_s[pl.ds(mine, part), :]
    mine_s[...] = moment_s[pl.ds(mine, part), :]
    stores = [
        pltpu.make_async_copy(fast_s, fast_ref.at[0, m, head], sems.at[0]),
        pltpu.make_async_copy(mine_s, moment_ref.at[0, m, head], sems.at[1]),
    ]
    for store in stores:
        store.start()
    return stores


def update_two_gu(n, head, tok_ref, rate_ref, old_ref, own_ref, q_ref, *refs):
    recvs = refs[: n - 1]
    hq_ref, fast_ref, moment_ref, gu_s, moment_s, fast_s, mine_s, sems = refs[-8:]
    width = own_ref.shape[1]
    stores = []
    for m in range(2):
        new, moment = updated(rate_ref[head, m], old_ref, own_ref, recvs, m * width)
        new_s = gu_s.at[pl.ds(m * width, width), :]
        new_s[...] = new
        moment_s[...] = moment
        stores += store_mine(
            n,
            m,
            head,
            tok_ref[0],
            new_s,
            moment_s,
            fast_s.at[m],
            mine_s.at[m],
            fast_ref,
            moment_ref,
            sems.at[m],
        )
    for at in row_chunks(q_ref.shape[0]):
        both = mm(q_ref[at, :], gu_s[...], ((1,), (1,)))
        hq_ref[at, :] = (jax.nn.silu(both[:, :width]) * both[:, width:]).astype(BF16)
    for store in stores:
        store.wait()


def update_two_down(n, head, tok_ref, rate_ref, old_ref, own_ref, hq_ref, *refs):
    recvs = refs[: n - 1]
    out_ref, fast_ref, moment_ref, out_s, down_s, moment_s, fast_s, mine_s, out_sems, sems = refs[-10:]
    width = own_ref.shape[1]
    new, moment = updated(rate_ref[head, 2], old_ref, own_ref, recvs, 0)
    down_s[...] = new
    moment_s[...] = moment
    stores = store_mine(
        n, 2, head, tok_ref[0], down_s, moment_s, fast_s, mine_s, fast_ref, moment_ref, sems
    )
    for i, at in enumerate(row_chunks(hq_ref.shape[0])):
        out_s[at, :] = mm(hq_ref[at, :], down_s[...], ((1,), (1,))).astype(BF16)
        stores.append(
            pltpu.make_async_copy(
                out_s.at[at, :], out_ref.at[1, at, pl.ds(head * width, width)], out_sems.at[i]
            )
        )
        stores[-1].start()
    for store in stores:
        store.wait()


def apply_one(head, q_ref, pgu_ref, pdown_ref, *refs):
    out_ref, out_s, sems = refs[-3:]
    rows, width = q_ref.shape
    stores = []
    for i, at in enumerate(row_chunks(rows)):
        both = mm(q_ref[at, :], pgu_ref[: 2 * width, :], ((1,), (1,)))
        hq = (jax.nn.silu(both[:, :width]) * both[:, width:]).astype(BF16)
        out_s[at, :] = mm(hq, pdown_ref[:width, :], ((1,), (1,))).astype(BF16)
        stores.append(
            pltpu.make_async_copy(
                out_s.at[at, :], out_ref.at[0, at, pl.ds(head * width, width)], sems.at[i]
            )
        )
        stores[-1].start()
    for store in stores:
        store.wait()


def on_device(keys, values, queries, fast_in, moment_in, initial_fast, rates, decays):
    n = lax.axis_size("tok")
    blocks = lax.axis_size("block")
    steps, rows, features = keys.shape
    heads = rates.shape[1]
    width = features // heads
    part = width // n
    chunks = len(row_chunks(rows))
    divisor = float(rows * n)
    tok = lax.axis_index("tok").astype(jnp.int32).reshape(1)
    block = lax.axis_index("block").astype(jnp.int32).reshape(1)
    fast_t = jnp.swapaxes(fast_in, 3, 4)
    moment_t = jnp.swapaxes(moment_in, 3, 4)
    begin_t = jnp.swapaxes(initial_fast, 2, 3)
    rates = rates.T
    keys, values, queries, fast_t, moment_t, begin_t = (
        pltpu.with_memory_space_constraint(x, pltpu.HBM)
        for x in (keys, values, queries, fast_t, moment_t, begin_t)
    )

    def turned(x):
        return [lax.ppermute(x, "tok", [(i, (i + r) % n) for i in range(n)]) for r in range(1, n)]

    def forward(x):
        return lax.ppermute(x, "block", [(i, i + 1) for i in range(blocks - 1)])

    def shape(*dims, dtype=BF16):
        return jax.ShapeDtypeStruct(dims, dtype)

    row_scratch = pltpu.VMEM((rows, width), BF16)
    grad_scratch = (row_scratch, row_scratch, pltpu.VMEM((rows, 2 * width), BF16))
    grad_out = (
        shape(2 * width, width),
        shape(width, width),
        shape(2 * width, width),
        shape(width, width),
        shape(2 * width, width, dtype=F32),
        shape(width, width, dtype=F32),
    )

    recv_fast, owned = [], []
    for h in range(heads):
        owned.append(
            call(functools.partial(take_head, h), shape(3, part, width), [HBM], VMEM)(fast_t)
        )
        recv_fast.append(turned(owned[h]))

    sources = [(2 * (m + 1)) % blocks for m in range(3)]
    piece = call(
        functools.partial(take_piece, sources), shape(heads, part, width), [SMEM, HBM], VMEM
    )(block, begin_t)
    crossed = [
        lax.ppermute(
            piece,
            ("block", "tok"),
            [(s * n + i, s * n + (i + r) % n) for s in sorted(set(sources)) for i in range(n)],
        )
        for r in range(1, n)
    ]

    loaded = list(
        call(
            functools.partial(load_all, steps, heads),
            (shape(rows, width),) * (3 * steps * heads)
            + (shape(3, part, width, dtype=F32),) * heads
            + (shape(3, part, width),) * heads,
            [HBM] * 5,
            (VMEM,) * (3 * steps * heads + 2 * heads),
            (DMA((3 * steps * heads + 2 * heads,)),),
        )(keys, values, queries, moment_t, begin_t)
    )
    kvq = [[[loaded.pop(0) for _ in range(3)] for _ in range(heads)] for _ in range(steps)]
    m_own, begin_own = loaded[:heads], loaded[heads:]

    first = [
        call(
            functools.partial(grads_one, n, h, divisor),
            grad_out,
            [SMEM, SMEM] + [VMEM] * (3 + n),
            (VMEM,) * 6,
            grad_scratch,
        )(tok, decays, *kvq[0][h][:2], m_own[h], owned[h], *recv_fast[h])
        for h in range(heads)
    ]

    packs = []
    for h in range(heads):
        gu, down, send_gu, send_down, own_gu, own_down = first[h]
        recv_gu, recv_down = turned(send_gu), turned(send_down)
        packs.append(
            [
                call(
                    functools.partial(update_one, n, h, mats),
                    shape(len(mats) * (width + part), width),
                    [SMEM, SMEM] + [VMEM] * (1 + n),
                    VMEM,
                    (pltpu.VMEM((width, width), F32),),
                )(tok, rates, old, own, *recvs)
                for mats, old, own, recvs in (
                    ((0, 1), gu, own_gu, recv_gu), ((2,), down, own_down, recv_down)
                )
            ]
        )

    begins = []
    for m in range(3):
        begins.append(
            [
                lax.ppermute(
                    x, ("block", "tok"), [(sources[m] * n + i, i) for i in range(n)]
                )
                for x in crossed
            ]
        )

    second = []
    for h in range(heads):
        arrived = [forward(packs[h][0]), forward(packs[h][1])]
        pieces = [begins[m][r] for r in range(n - 1) for m in range(3)]
        second.append(
            call(
                functools.partial(grads_two, n, h, divisor),
                grad_out,
                [SMEM] * 3 + [VMEM] * (5 + 3 * (n - 1)),
                (VMEM,) * 6,
                grad_scratch,
            )(tok, block, decays, *kvq[1][h][:2], begin_own[h], *arrived, *pieces)
        )

    out_shape = jax.ShapeDtypeStruct(keys.shape, BF16)
    outputs = None
    for h in range(heads):
        prior = [] if outputs is None else [outputs]
        outputs = call(
            functools.partial(apply_one, h),
            out_shape,
            [VMEM] * 3 + [HBM] * len(prior),
            HBM,
            (row_scratch, DMA((chunks,))),
            aliases={3: 0} if prior else None,
        )(kvq[0][h][2], *packs[h], *prior)

    fast_shape = jax.ShapeDtypeStruct(fast_t.shape, BF16)
    moment_shape = jax.ShapeDtypeStruct(moment_t.shape, F32)
    ends = []
    for h in range(heads):
        gu, down, send_gu, send_down, own_gu, own_down = second[h]
        recv_gu, recv_down = turned(send_gu), turned(send_down)
        at = 4 + n
        hq, *ends = call(
            functools.partial(update_two_gu, n, h),
            (shape(rows, width), fast_shape, moment_shape),
            [SMEM, SMEM] + [VMEM] * (2 + n) + [HBM] * len(ends),
            (VMEM, HBM, HBM),
            (
                pltpu.VMEM((2 * width, width), BF16),
                pltpu.VMEM((width, width), F32),
                pltpu.VMEM((2, part, width), BF16),
                pltpu.VMEM((2, part, width), F32),
                DMA((2, 2)),
            ),
            aliases={at: 1, at + 1: 2} if ends else None,
        )(tok, rates, gu, own_gu, kvq[1][h][2], *recv_gu, *ends)
        outputs, *ends = call(
            functools.partial(update_two_down, n, h),
            (out_shape, fast_shape, moment_shape),
            [SMEM, SMEM] + [VMEM] * (2 + n) + [HBM] * 3,
            (HBM,) * 3,
            (
                row_scratch,
                pltpu.VMEM((width, width), BF16),
                pltpu.VMEM((width, width), F32),
                pltpu.VMEM((part, width), BF16),
                pltpu.VMEM((part, width), F32),
                DMA((chunks,)),
                DMA((2,)),
            ),
            aliases={at: 0, at + 1: 1, at + 2: 2},
        )(tok, rates, down, own_down, hq, *recv_down, outputs, *ends)
    return (outputs, jnp.swapaxes(ends[0], 3, 4), jnp.swapaxes(ends[1], 3, 4))


def solution(mesh):
    placed = (
        P(None, ("block", "tok"), None),
        P(None, ("block", "tok"), None),
        P(None, ("block", "tok"), None),
        P("block", None, None, None, "tok"),
        P("block", None, None, None, "tok"),
        P(None, None, None, "tok"),
        P(),
        P(),
    )
    step = jax.shard_map(
        on_device,
        mesh=mesh,
        in_specs=placed,
        out_specs=(
            P(None, ("block", "tok"), None),
            P("block", None, None, None, "tok"),
            P("block", None, None, None, "tok"),
        ),
        check_vma=False,
    )

    def run(*args):
        with jax.sharding.use_abstract_mesh(mesh.abstract_mesh):
            return step(*args)

    return run
```

```python
import functools

import jax
import jax.numpy as jnp
from jax import lax
from jax.experimental import pallas as pl
from jax.experimental.pallas import tpu as pltpu
from jax.sharding import PartitionSpec as P


F32 = jnp.float32
BF16 = jnp.bfloat16
VMEM = pl.BlockSpec(memory_space=pltpu.VMEM)
SMEM = pl.BlockSpec(memory_space=pltpu.SMEM)
HBM = pl.BlockSpec(memory_space=pltpu.HBM)
DMA = pltpu.SemaphoreType.DMA


def mm(a, b, dims):
    return lax.dot_general(a, b, (dims, ((), ())), preferred_element_type=F32)


def call(kernel, out, in_specs, out_specs, scratch=(), aliases=None):
    return pl.pallas_call(
        kernel,
        out_shape=out,
        in_specs=in_specs,
        out_specs=out_specs,
        scratch_shapes=list(scratch),
        input_output_aliases=aliases or {},
        compiler_params=pltpu.CompilerParams(vmem_limit_bytes=12 << 20),
    )


def row_chunks(rows):
    for size in (256, 384, 128):
        if rows % size == 0:
            return [pl.ds(first, size) for first in range(0, rows, size)]
    return [pl.ds(0, rows)]


def assemble(me, shards, gu_ref, down_ref):
    n = len(shards)
    width = down_ref.shape[0]
    part = width // n
    for r, shard in enumerate(shards):
        at = pl.multiple_of(lax.rem(me - r + n, n) * part, part)
        gu_ref[pl.ds(at, part), :] = shard(0)
        gu_ref[pl.ds(width + at, part), :] = shard(1)
        down_ref[pl.ds(at, part), :] = shard(2)


def grads_core(divisor, k_ref, v_ref, gu_ref, down_ref, own_gu, own_down, hid_s, dout_s, dgu_s):
    rows, width = k_ref.shape
    for at in row_chunks(rows):
        both = mm(k_ref[at, :], gu_ref[...], ((1,), (1,)))
        gate, upper = both[:, :width], both[:, width:]
        dout = (-v_ref[at, :].astype(F32) / divisor).astype(BF16)
        dhid = mm(dout, down_ref[...], ((1,), (0,)))
        sigma = jax.nn.sigmoid(gate)
        silu = gate * sigma
        hid_s[at, :] = (silu * upper).astype(BF16)
        dout_s[at, :] = dout
        dgu_s[at, :width] = (dhid * upper * sigma * (1.0 + gate * (1.0 - sigma))).astype(BF16)
        dgu_s[at, width:] = (dhid * silu).astype(BF16)
    own_gu[...] = mm(dgu_s[...], k_ref[...], ((0,), (0,)))
    own_down[...] = mm(dout_s[...], hid_s[...], ((0,), (0,)))


def take_head(head, fast_ref, own_ref):
    pltpu.sync_copy(fast_ref.at[0, :, head], own_ref)


def take_piece(sources, begin_ref, piece_ref):
    block = lax.axis_index("block")
    piece = jnp.int32(0)
    for p, source in enumerate(sources):
        piece = jnp.where(block == source, jnp.int32(p), piece)
    pltpu.sync_copy(begin_ref.at[lax.rem(piece, 3), piece // 3], piece_ref)


def load_all(steps, heads, k_ref, v_ref, q_ref, m_ref, begin_ref, *refs):
    sems = refs[-1]
    copies = []

    def add(source, target):
        copies.append(pltpu.make_async_copy(source, target, sems.at[len(copies)]))
        copies[-1].start()

    targets = list(refs[:-1])
    for step in range(steps):
        for head in range(heads):
            for ref in (k_ref, v_ref, q_ref):
                target = targets.pop(0)
                width = target.shape[1]
                add(ref.at[step, :, pl.ds(head * width, width)], target)
    for head in range(heads):
        add(m_ref.at[0, :, head], targets.pop(0))
    for head in range(heads):
        add(begin_ref.at[:, head], targets.pop(0))
    for copy in copies:
        copy.wait()


def grads_one(n, head, divisor, decay_ref, k_ref, v_ref, m_ref, *refs):
    shards = refs[:n]
    gu_ref, down_ref, send_gu, send_down, own_gu, own_down, hid_s, dout_s, dgu_s = refs[n:]
    width = down_ref.shape[0]
    part = width // n
    me = lax.axis_index("tok")
    assemble(me, [lambda m, ref=ref: ref[m] for ref in shards], gu_ref, down_ref)
    grads_core(divisor, k_ref, v_ref, gu_ref, down_ref, own_gu, own_down, hid_s, dout_s, dgu_s)
    decay = decay_ref[head]
    mine = pl.multiple_of(me * part, part)
    own_gu[pl.ds(mine, part), :] += decay * m_ref[0]
    own_gu[pl.ds(width + mine, part), :] += decay * m_ref[1]
    own_down[pl.ds(mine, part), :] += decay * m_ref[2]
    send_gu[...] = own_gu[...].astype(BF16)
    send_down[...] = own_down[...].astype(BF16)


def grads_two(n, divisor, k_ref, v_ref, begin_ref, *refs):
    (pgu_ref, pdown_ref), pieces = refs[:2], refs[2 : 2 + 3 * (n - 1)]
    gu_ref, down_ref, send_gu, send_down, own_gu, own_down, hid_s, dout_s, dgu_s = refs[-9:]
    leading = lax.axis_index("block") == 0

    @pl.when(leading)
    def _():
        shards = [lambda m: begin_ref[m]]
        for r in range(n - 1):
            shards.append(lambda m, r=r: pieces[3 * r + m][...])
        assemble(lax.axis_index("tok"), shards, gu_ref, down_ref)

    @pl.when(jnp.logical_not(leading))
    def _():
        gu_ref[...] = pgu_ref[...]
        down_ref[...] = pdown_ref[...]

    grads_core(divisor, k_ref, v_ref, gu_ref, down_ref, own_gu, own_down, hid_s, dout_s, dgu_s)
    send_gu[...] = own_gu[...].astype(BF16)
    send_down[...] = own_down[...].astype(BF16)


def updated(rate, old_ref, moments, first):
    width = old_ref.shape[1]
    at = pl.ds(first, width)
    moment = moments(at)
    old = old_ref[at, :].astype(F32)
    moved = old - rate * moment
    old_norm = jnp.sqrt(jnp.mean(old * old, axis=1, keepdims=True) + 1e-06)
    new_norm = jnp.sqrt(jnp.mean(moved * moved, axis=1, keepdims=True) + 1e-06)
    return (moved * (old_norm / new_norm)).astype(BF16), moment


def summed(own_ref, recvs, at):
    total = own_ref[at, :]
    for recv in recvs:
        total = total + recv[at, :].astype(F32)
    return total


def update_one(n, head, mats, rate_ref, old_ref, own_ref, *refs):
    recvs = refs[: n - 1]
    new_ref, moment_ref = refs[-2:]
    width = own_ref.shape[1]
    for i, m in enumerate(mats):
        at = slice(i * width, (i + 1) * width)
        new, moment = updated(
            rate_ref[head, m], old_ref, lambda at: summed(own_ref, recvs, at), i * width
        )
        new_ref[at, :] = new
        moment_ref[m * width : (m + 1) * width, :] = moment.astype(BF16)


def later_moment(decay, m, earlier_ref, own_ref, recvs):
    width = earlier_ref.shape[1]

    def moment(at):
        earlier = earlier_ref[m * width : (m + 1) * width, :].astype(F32)
        return decay * earlier + summed(own_ref, recvs, at)

    return moment


def store_mine(n, m, head, me, new_s, moment_s, fast_s, mine_s, fast_ref, moment_ref, sems):
    width = moment_s.shape[1]
    part = width // n
    mine = pl.multiple_of(me * part, part)
    fast_s[...] = new_s[pl.ds(mine, part), :]
    mine_s[...] = moment_s[pl.ds(mine, part), :]
    stores = [
        pltpu.make_async_copy(fast_s, fast_ref.at[0, m, head], sems.at[0]),
        pltpu.make_async_copy(mine_s, moment_ref.at[0, m, head], sems.at[1]),
    ]
    for store in stores:
        store.start()
    return stores


def update_two_gu(n, head, rate_ref, decay_ref, old_ref, own_ref, earlier_ref, q_ref, *refs):
    recvs = refs[: n - 1]
    hq_ref, fast_ref, moment_ref, gu_s, moment_s, fast_s, mine_s, sems = refs[-8:]
    width = own_ref.shape[1]
    stores = []
    for m in range(2):
        moments = later_moment(decay_ref[head], m, earlier_ref, own_ref, recvs)
        new, moment = updated(rate_ref[head, m], old_ref, moments, m * width)
        new_s = gu_s.at[pl.ds(m * width, width), :]
        new_s[...] = new
        moment_s[...] = moment
        stores += store_mine(
            n,
            m,
            head,
            lax.axis_index("tok"),
            new_s,
            moment_s,
            fast_s.at[m],
            mine_s.at[m],
            fast_ref,
            moment_ref,
            sems.at[m],
        )
    for at in row_chunks(q_ref.shape[0]):
        both = mm(q_ref[at, :], gu_s[...], ((1,), (1,)))
        hq_ref[at, :] = (jax.nn.silu(both[:, :width]) * both[:, width:]).astype(BF16)
    for store in stores:
        store.wait()


def update_two_down(n, head, rate_ref, decay_ref, old_ref, own_ref, earlier_ref, hq_ref, *refs):
    recvs = refs[: n - 1]
    out_ref, fast_ref, moment_ref, out_s, down_s, moment_s, fast_s, mine_s, out_sems, sems = refs[-10:]
    width = own_ref.shape[1]
    moments = later_moment(decay_ref[head], 2, earlier_ref, own_ref, recvs)
    new, moment = updated(rate_ref[head, 2], old_ref, moments, 0)
    down_s[...] = new
    moment_s[...] = moment
    stores = store_mine(
        n, 2, head, lax.axis_index("tok"), down_s, moment_s, fast_s, mine_s, fast_ref, moment_ref, sems
    )
    for i, at in enumerate(row_chunks(hq_ref.shape[0])):
        out_s[at, :] = mm(hq_ref[at, :], down_s[...], ((1,), (1,))).astype(BF16)
        stores.append(
            pltpu.make_async_copy(
                out_s.at[at, :], out_ref.at[1, at, pl.ds(head * width, width)], out_sems.at[i]
            )
        )
        stores[-1].start()
    for store in stores:
        store.wait()


def apply_one(head, q_ref, pgu_ref, pdown_ref, *refs):
    out_ref, out_s, sems = refs[-3:]
    rows, width = q_ref.shape
    stores = []
    for i, at in enumerate(row_chunks(rows)):
        both = mm(q_ref[at, :], pgu_ref[...], ((1,), (1,)))
        hq = (jax.nn.silu(both[:, :width]) * both[:, width:]).astype(BF16)
        out_s[at, :] = mm(hq, pdown_ref[...], ((1,), (1,))).astype(BF16)
        stores.append(
            pltpu.make_async_copy(
                out_s.at[at, :], out_ref.at[0, at, pl.ds(head * width, width)], sems.at[i]
            )
        )
        stores[-1].start()
    for store in stores:
        store.wait()


def on_device(keys, values, queries, fast_in, moment_in, initial_fast, rates, decays):
    n = lax.axis_size("tok")
    blocks = lax.axis_size("block")
    steps, rows, features = keys.shape
    heads = rates.shape[1]
    width = features // heads
    part = width // n
    chunks = len(row_chunks(rows))
    divisor = float(rows * n)
    fast_t = jnp.swapaxes(fast_in, 3, 4)
    moment_t = jnp.swapaxes(moment_in, 3, 4)
    begin_t = jnp.swapaxes(initial_fast, 2, 3)
    rates = rates.T
    keys, values, queries, fast_t, moment_t, begin_t = (
        pltpu.with_memory_space_constraint(x, pltpu.HBM)
        for x in (keys, values, queries, fast_t, moment_t, begin_t)
    )

    def turned(x):
        return [lax.ppermute(x, "tok", [(i, (i + r) % n) for i in range(n)]) for r in range(1, n)]

    def forward(x):
        return lax.ppermute(x, "block", [(i, i + 1) for i in range(blocks - 1)])

    def shape(*dims, dtype=BF16):
        return jax.ShapeDtypeStruct(dims, dtype)

    row_scratch = pltpu.VMEM((rows, width), BF16)
    grad_scratch = (row_scratch, row_scratch, pltpu.VMEM((rows, 2 * width), BF16))
    grad_out = (
        shape(2 * width, width),
        shape(width, width),
        shape(2 * width, width),
        shape(width, width),
        shape(2 * width, width, dtype=F32),
        shape(width, width, dtype=F32),
    )

    recv_fast, owned = [], []
    for h in range(heads):
        owned.append(
            call(functools.partial(take_head, h), shape(3, part, width), [HBM], VMEM)(fast_t)
        )
        recv_fast.append(turned(owned[h]))

    sources = [(2 * (p + 1)) % blocks for p in range(3 * heads)]
    piece = call(functools.partial(take_piece, sources), shape(part, width), [HBM], VMEM)(begin_t)
    crossed = [
        lax.ppermute(
            piece,
            ("block", "tok"),
            [(s * n + i, s * n + (i + r) % n) for s in sorted(set(sources)) for i in range(n)],
        )
        for r in range(1, n)
    ]

    loaded = list(
        call(
            functools.partial(load_all, steps, heads),
            (shape(rows, width),) * (3 * steps * heads)
            + (shape(3, part, width, dtype=F32),) * heads
            + (shape(3, part, width),) * heads,
            [HBM] * 5,
            (VMEM,) * (3 * steps * heads + 2 * heads),
            (DMA((3 * steps * heads + 2 * heads,)),),
        )(keys, values, queries, moment_t, begin_t)
    )
    kvq = [[[loaded.pop(0) for _ in range(3)] for _ in range(heads)] for _ in range(steps)]
    m_own, begin_own = loaded[:heads], loaded[heads:]

    first = [
        call(
            functools.partial(grads_one, n, h, divisor),
            grad_out,
            [SMEM] + [VMEM] * (3 + n),
            (VMEM,) * 6,
            grad_scratch,
        )(decays, *kvq[0][h][:2], m_own[h], owned[h], *recv_fast[h])
        for h in range(heads)
    ]

    packs, moments = [], []
    for h in range(heads):
        gu, down, send_gu, send_down, own_gu, own_down = first[h]
        recv_gu, recv_down = turned(send_gu), turned(send_down)
        pack, moment = [], []
        for mats, old, own, recvs in (
            ((0, 1), gu, own_gu, recv_gu), ((2,), down, own_down, recv_down)
        ):
            new, *moment = call(
                functools.partial(update_one, n, h, mats),
                (shape(len(mats) * width, width), shape(3 * width, width)),
                [SMEM] + [VMEM] * (1 + n + len(moment)),
                (VMEM, VMEM),
                aliases={2 + n: 1} if moment else None,
            )(rates, old, own, *recvs, *moment)
            pack.append(new)
        packs.append(pack)
        moments.append(forward(moment[0]))

    begins = []
    for p in range(3 * heads):
        begins.append(
            [
                lax.ppermute(
                    x, ("block", "tok"), [(sources[p] * n + i, i) for i in range(n)]
                )
                for x in crossed
            ]
        )

    second = []
    for h in range(heads):
        arrived = [forward(packs[h][0]), forward(packs[h][1])]
        pieces = [begins[3 * h + m][r] for r in range(n - 1) for m in range(3)]
        second.append(
            call(
                functools.partial(grads_two, n, divisor),
                grad_out,
                [VMEM] * (5 + 3 * (n - 1)),
                (VMEM,) * 6,
                grad_scratch,
            )(*kvq[1][h][:2], begin_own[h], *arrived, *pieces)
        )

    out_shape = jax.ShapeDtypeStruct(keys.shape, BF16)
    outputs = None
    for h in range(heads):
        prior = [] if outputs is None else [outputs]
        outputs = call(
            functools.partial(apply_one, h),
            out_shape,
            [VMEM] * 3 + [HBM] * len(prior),
            HBM,
            (row_scratch, DMA((chunks,))),
            aliases={3: 0} if prior else None,
        )(kvq[0][h][2], *packs[h], *prior)

    fast_shape = jax.ShapeDtypeStruct(fast_t.shape, BF16)
    moment_shape = jax.ShapeDtypeStruct(moment_t.shape, F32)
    ends = []
    for h in range(heads):
        gu, down, send_gu, send_down, own_gu, own_down = second[h]
        recv_gu, recv_down = turned(send_gu), turned(send_down)
        at = 5 + n
        hq, *ends = call(
            functools.partial(update_two_gu, n, h),
            (shape(rows, width), fast_shape, moment_shape),
            [SMEM] * 2 + [VMEM] * (3 + n) + [HBM] * len(ends),
            (VMEM, HBM, HBM),
            (
                pltpu.VMEM((2 * width, width), BF16),
                pltpu.VMEM((width, width), F32),
                pltpu.VMEM((2, part, width), BF16),
                pltpu.VMEM((2, part, width), F32),
                DMA((2, 2)),
            ),
            aliases={at: 1, at + 1: 2} if ends else None,
        )(rates, decays, gu, own_gu, moments[h], kvq[1][h][2], *recv_gu, *ends)
        outputs, *ends = call(
            functools.partial(update_two_down, n, h),
            (out_shape, fast_shape, moment_shape),
            [SMEM] * 2 + [VMEM] * (3 + n) + [HBM] * 3,
            (HBM,) * 3,
            (
                row_scratch,
                pltpu.VMEM((width, width), BF16),
                pltpu.VMEM((width, width), F32),
                pltpu.VMEM((part, width), BF16),
                pltpu.VMEM((part, width), F32),
                DMA((chunks,)),
                DMA((2,)),
            ),
            aliases={at: 0, at + 1: 1, at + 2: 2},
        )(rates, decays, down, own_down, moments[h], hq, *recv_down, outputs, *ends)
    return (outputs, jnp.swapaxes(ends[0], 3, 4), jnp.swapaxes(ends[1], 3, 4))


def solution(mesh):
    placed = (
        P(None, ("block", "tok"), None),
        P(None, ("block", "tok"), None),
        P(None, ("block", "tok"), None),
        P("block", None, None, None, "tok"),
        P("block", None, None, None, "tok"),
        P(None, None, None, "tok"),
        P(),
        P(),
    )
    step = jax.shard_map(
        on_device,
        mesh=mesh,
        in_specs=placed,
        out_specs=(
            P(None, ("block", "tok"), None),
            P("block", None, None, None, "tok"),
            P("block", None, None, None, "tok"),
        ),
        check_vma=False,
    )

    def run(*args):
        with jax.sharding.use_abstract_mesh(mesh.abstract_mesh):
            return step(*args)

    return run
```

```python
import functools

import jax
import jax.numpy as jnp
from jax import lax
from jax.experimental import pallas as pl
from jax.experimental.pallas import tpu as pltpu
from jax.sharding import PartitionSpec as P


F32 = jnp.float32
BF16 = jnp.bfloat16
VMEM = pl.BlockSpec(memory_space=pltpu.VMEM)
SMEM = pl.BlockSpec(memory_space=pltpu.SMEM)
HBM = pl.BlockSpec(memory_space=pltpu.HBM)
DMA = pltpu.SemaphoreType.DMA


def mm(a, b, dims):
    return lax.dot_general(a, b, (dims, ((), ())), preferred_element_type=F32)


def call(kernel, out, in_specs, out_specs, scratch=(), aliases=None):
    return pl.pallas_call(
        kernel,
        out_shape=out,
        in_specs=in_specs,
        out_specs=out_specs,
        scratch_shapes=list(scratch),
        input_output_aliases=aliases or {},
        compiler_params=pltpu.CompilerParams(vmem_limit_bytes=12 << 20),
    )


def row_chunks(rows):
    for size in (256, 384, 128):
        if rows % size == 0:
            return [pl.ds(first, size) for first in range(0, rows, size)]
    return [pl.ds(0, rows)]


def assemble(me, shards, gu_ref, down_ref):
    n = len(shards)
    width = down_ref.shape[0]
    part = width // n
    for r, shard in enumerate(shards):
        at = pl.multiple_of(lax.rem(me - r + n, n) * part, part)
        gu_ref[pl.ds(at, part), :] = shard(0)
        gu_ref[pl.ds(width + at, part), :] = shard(1)
        down_ref[pl.ds(at, part), :] = shard(2)


def grads_core(divisor, k_ref, v_ref, gu_ref, down_ref, own_gu, own_down, hid_s, dout_s, dgu_s):
    rows, width = k_ref.shape
    for at in row_chunks(rows):
        both = mm(k_ref[at, :], gu_ref[...], ((1,), (1,)))
        gate, upper = both[:, :width], both[:, width:]
        dout = (-v_ref[at, :].astype(F32) / divisor).astype(BF16)
        dhid = mm(dout, down_ref[...], ((1,), (0,)))
        sigma = jax.nn.sigmoid(gate)
        silu = gate * sigma
        hid_s[at, :] = (silu * upper).astype(BF16)
        dout_s[at, :] = dout
        dgu_s[at, :width] = (dhid * upper * sigma * (1.0 + gate * (1.0 - sigma))).astype(BF16)
        dgu_s[at, width:] = (dhid * silu).astype(BF16)
    own_gu[...] = mm(dgu_s[...], k_ref[...], ((0,), (0,)))
    own_down[...] = mm(dout_s[...], hid_s[...], ((0,), (0,)))


def take_head(head, fast_ref, own_ref):
    pltpu.sync_copy(fast_ref.at[0, :, head], own_ref)


def take_piece(sources, begin_ref, piece_ref):
    block = lax.axis_index("block")
    piece = jnp.int32(0)
    for p, source in enumerate(sources):
        piece = jnp.where(block == source, jnp.int32(p), piece)
    pltpu.sync_copy(begin_ref.at[lax.rem(piece, 3), piece // 3], piece_ref)


def load_all(steps, heads, k_ref, v_ref, q_ref, m_ref, begin_ref, *refs):
    sems = refs[-1]
    copies = []

    def add(source, target):
        copies.append(pltpu.make_async_copy(source, target, sems.at[len(copies)]))
        copies[-1].start()

    targets = list(refs[:-1])
    for step in range(steps):
        for head in range(heads):
            for ref in (k_ref, v_ref, q_ref):
                target = targets.pop(0)
                width = target.shape[1]
                add(ref.at[step, :, pl.ds(head * width, width)], target)
    for head in range(heads):
        add(m_ref.at[0, :, head], targets.pop(0))
    for head in range(heads):
        add(begin_ref.at[:, head], targets.pop(0))
    for copy in copies:
        copy.wait()


def grads_one(n, head, divisor, decay_ref, k_ref, v_ref, m_ref, *refs):
    shards = refs[:n]
    gu_ref, down_ref, send_gu, send_down, own_gu, own_down, hid_s, dout_s, dgu_s = refs[n:]
    width = down_ref.shape[0]
    part = width // n
    me = lax.axis_index("tok")
    assemble(me, [lambda m, ref=ref: ref[m] for ref in shards], gu_ref, down_ref)
    grads_core(divisor, k_ref, v_ref, gu_ref, down_ref, own_gu, own_down, hid_s, dout_s, dgu_s)
    decay = decay_ref[head]
    mine = pl.multiple_of(me * part, part)
    own_gu[pl.ds(mine, part), :] += decay * m_ref[0]
    own_gu[pl.ds(width + mine, part), :] += decay * m_ref[1]
    own_down[pl.ds(mine, part), :] += decay * m_ref[2]
    send_gu[...] = own_gu[...].astype(BF16)
    send_down[...] = own_down[...].astype(BF16)


def grads_two(n, divisor, k_ref, v_ref, begin_ref, *refs):
    (pgu_ref, pdown_ref), pieces = refs[:2], refs[2 : 2 + 3 * (n - 1)]
    gu_ref, down_ref, own_gu, own_down, send_gu, *sends = refs[2 + 3 * (n - 1) : -3]
    hid_s, dout_s, dgu_s = refs[-3:]
    leading = lax.axis_index("block") == 0

    @pl.when(leading)
    def _():
        shards = [lambda m: begin_ref[m]]
        for r in range(n - 1):
            shards.append(lambda m, r=r: pieces[3 * r + m][...])
        assemble(lax.axis_index("tok"), shards, gu_ref, down_ref)

    @pl.when(jnp.logical_not(leading))
    def _():
        gu_ref[...] = pgu_ref[...]
        down_ref[...] = pdown_ref[...]

    grads_core(divisor, k_ref, v_ref, gu_ref, down_ref, own_gu, own_down, hid_s, dout_s, dgu_s)
    send_gu[...] = own_gu[...].astype(BF16)
    first = 0
    for send in sends:
        send[...] = own_down[pl.ds(first, send.shape[0]), :].astype(BF16)
        first += send.shape[0]


def updated(rate, old_ref, at, moment):
    old = old_ref[at, :].astype(F32)
    moved = old - rate * moment
    old_norm = jnp.sqrt(jnp.mean(old * old, axis=1, keepdims=True) + 1e-06)
    new_norm = jnp.sqrt(jnp.mean(moved * moved, axis=1, keepdims=True) + 1e-06)
    return (moved * (old_norm / new_norm)).astype(BF16)


def summed(own_ref, recvs, first, size, sent_from=0):
    total = own_ref[pl.ds(first, size), :]
    for recv in recvs:
        total = total + recv[pl.ds(first - sent_from, size), :].astype(F32)
    return total


def update_one(n, head, mats, rate_ref, old_ref, own_ref, *refs):
    recvs = refs[: n - 1]
    new_ref, moment_ref = refs[-2:]
    width = own_ref.shape[1]
    for i, m in enumerate(mats):
        at = pl.ds(i * width, width)
        moment = summed(own_ref, recvs, i * width, width)
        new_ref[at, :] = updated(rate_ref[head, m], old_ref, at, moment)
        moment_ref[m * width : (m + 1) * width, :] = moment.astype(BF16)


def store_mine(n, m, head, me, new_s, moment_s, fast_s, mine_s, fast_ref, moment_ref, sems):
    width = moment_s.shape[1]
    part = width // n
    mine = pl.multiple_of(me * part, part)
    fast_s[...] = new_s[pl.ds(mine, part), :]
    mine_s[...] = moment_s[pl.ds(mine, part), :]
    stores = [
        pltpu.make_async_copy(fast_s, fast_ref.at[0, m, head], sems.at[0]),
        pltpu.make_async_copy(mine_s, moment_ref.at[0, m, head], sems.at[1]),
    ]
    for store in stores:
        store.start()
    return stores


def update_two_gu(n, head, rate_ref, decay_ref, old_ref, own_ref, earlier_ref, q_ref, *refs):
    recvs = refs[: n - 1]
    hq_ref, fast_ref, moment_ref, gu_s, moment_s, fast_s, mine_s, sems = refs[-8:]
    width = own_ref.shape[1]
    stores = []
    for m in range(2):
        at = pl.ds(m * width, width)
        moment = decay_ref[head] * earlier_ref[at, :].astype(F32)
        moment = moment + summed(own_ref, recvs, m * width, width)
        new_s = gu_s.at[at, :]
        new_s[...] = updated(rate_ref[head, m], old_ref, at, moment)
        moment_s[...] = moment
        stores += store_mine(
            n,
            m,
            head,
            lax.axis_index("tok"),
            new_s,
            moment_s,
            fast_s.at[m],
            mine_s.at[m],
            fast_ref,
            moment_ref,
            sems.at[m],
        )
    for at in row_chunks(q_ref.shape[0]):
        both = mm(q_ref[at, :], gu_s[...], ((1,), (1,)))
        hq_ref[at, :] = (jax.nn.silu(both[:, :width]) * both[:, width:]).astype(BF16)
    for store in stores:
        store.wait()


def update_two_down(n, head, first, rate_ref, decay_ref, old_ref, own_ref, earlier_ref, hq_ref, *refs):
    recvs = refs[: n - 1]
    width = old_ref.shape[1]
    size = recvs[0].shape[0]
    last = first + size == width
    if last:
        out_ref, fast_ref, moment_ref, new_s, kept_s, out_s, fast_s, mine_s, out_sems, sems = refs[-10:]
    else:
        out_ref, new_s, kept_s, out_s, out_sems = refs[-5:]
    if first and last:
        before_new, before_kept = refs[n - 1 : n + 1]
        new_s[:first, :] = before_new[:first, :]
        kept_s[:first, :] = before_kept[:first, :]
    at = pl.ds(first, size)
    moment = decay_ref[head] * earlier_ref[pl.ds(2 * width + first, size), :].astype(F32)
    moment = moment + summed(own_ref, recvs, first, size, first)
    new_s[at, :] = updated(rate_ref[head, 2], old_ref, at, moment)
    kept_s[at, :] = moment
    stores = []
    if last:
        me = lax.axis_index("tok")
        stores = store_mine(
            n, 2, head, me, new_s, kept_s, fast_s, mine_s, fast_ref, moment_ref, sems
        )
    cols = pl.ds(head * width + first, size)
    for i, rows in enumerate(row_chunks(hq_ref.shape[0])):
        out_s[rows, :] = mm(hq_ref[rows, :], new_s[at, :], ((1,), (1,))).astype(BF16)
        stores.append(
            pltpu.make_async_copy(out_s.at[rows, :], out_ref.at[1, rows, cols], out_sems.at[i])
        )
        stores[-1].start()
    for store in stores:
        store.wait()


def apply_one(head, q_ref, pgu_ref, pdown_ref, *refs):
    out_ref, out_s, sems = refs[-3:]
    rows, width = q_ref.shape
    stores = []
    for i, at in enumerate(row_chunks(rows)):
        both = mm(q_ref[at, :], pgu_ref[...], ((1,), (1,)))
        hq = (jax.nn.silu(both[:, :width]) * both[:, width:]).astype(BF16)
        out_s[at, :] = mm(hq, pdown_ref[...], ((1,), (1,))).astype(BF16)
        stores.append(
            pltpu.make_async_copy(
                out_s.at[at, :], out_ref.at[0, at, pl.ds(head * width, width)], sems.at[i]
            )
        )
        stores[-1].start()
    for store in stores:
        store.wait()


def on_device(keys, values, queries, fast_in, moment_in, initial_fast, rates, decays):
    n = lax.axis_size("tok")
    blocks = lax.axis_size("block")
    steps, rows, features = keys.shape
    heads = rates.shape[1]
    width = features // heads
    part = width // n
    chunks = len(row_chunks(rows))
    divisor = float(rows * n)
    fast_t = jnp.swapaxes(fast_in, 3, 4)
    moment_t = jnp.swapaxes(moment_in, 3, 4)
    begin_t = jnp.swapaxes(initial_fast, 2, 3)
    rates = rates.T
    keys, values, queries, fast_t, moment_t, begin_t = (
        pltpu.with_memory_space_constraint(x, pltpu.HBM)
        for x in (keys, values, queries, fast_t, moment_t, begin_t)
    )

    def turned(x):
        return [lax.ppermute(x, "tok", [(i, (i + r) % n) for i in range(n)]) for r in range(1, n)]

    def forward(x):
        return lax.ppermute(x, "block", [(i, i + 1) for i in range(blocks - 1)])

    def shape(*dims, dtype=BF16):
        return jax.ShapeDtypeStruct(dims, dtype)

    row_scratch = pltpu.VMEM((rows, width), BF16)
    grad_scratch = (row_scratch, row_scratch, pltpu.VMEM((rows, 2 * width), BF16))
    grad_out = (
        shape(2 * width, width),
        shape(width, width),
        shape(2 * width, width),
        shape(width, width),
        shape(2 * width, width, dtype=F32),
        shape(width, width, dtype=F32),
    )

    recv_fast, owned = [], []
    for h in range(heads):
        owned.append(
            call(functools.partial(take_head, h), shape(3, part, width), [HBM], VMEM)(fast_t)
        )
        recv_fast.append(turned(owned[h]))

    sources = [(2 * (p + 1)) % blocks for p in range(3 * heads)]
    piece = call(functools.partial(take_piece, sources), shape(part, width), [HBM], VMEM)(begin_t)
    crossed = [
        lax.ppermute(
            piece,
            ("block", "tok"),
            [(s * n + i, s * n + (i + r) % n) for s in sorted(set(sources)) for i in range(n)],
        )
        for r in range(1, n)
    ]

    loaded = list(
        call(
            functools.partial(load_all, steps, heads),
            (shape(rows, width),) * (3 * steps * heads)
            + (shape(3, part, width, dtype=F32),) * heads
            + (shape(3, part, width),) * heads,
            [HBM] * 5,
            (VMEM,) * (3 * steps * heads + 2 * heads),
            (DMA((3 * steps * heads + 2 * heads,)),),
        )(keys, values, queries, moment_t, begin_t)
    )
    kvq = [[[loaded.pop(0) for _ in range(3)] for _ in range(heads)] for _ in range(steps)]
    m_own, begin_own = loaded[:heads], loaded[heads:]

    first = [
        call(
            functools.partial(grads_one, n, h, divisor),
            grad_out,
            [SMEM] + [VMEM] * (3 + n),
            (VMEM,) * 6,
            grad_scratch,
        )(decays, *kvq[0][h][:2], m_own[h], owned[h], *recv_fast[h])
        for h in range(heads)
    ]

    packs, moments = [], []
    for h in range(heads):
        gu, down, send_gu, send_down, own_gu, own_down = first[h]
        recv_gu, recv_down = turned(send_gu), turned(send_down)
        pack, moment = [], []
        for mats, old, own, recvs in (
            ((0, 1), gu, own_gu, recv_gu), ((2,), down, own_down, recv_down)
        ):
            new, *moment = call(
                functools.partial(update_one, n, h, mats),
                (shape(len(mats) * width, width), shape(3 * width, width)),
                [SMEM] + [VMEM] * (1 + n + len(moment)),
                (VMEM, VMEM),
                aliases={2 + n: 1} if moment else None,
            )(rates, old, own, *recvs, *moment)
            pack.append(new)
        packs.append(pack)
        moments.append(forward(moment[0]))

    begins = []
    for p in range(3 * heads):
        begins.append(
            [
                lax.ppermute(
                    x, ("block", "tok"), [(sources[p] * n + i, i) for i in range(n)]
                )
                for x in crossed
            ]
        )

    second = []
    for h in range(heads):
        arrived = [forward(packs[h][0]), forward(packs[h][1])]
        pieces = [begins[3 * h + m][r] for r in range(n - 1) for m in range(3)]
        cuts = [width - 128, 128] if h == heads - 1 and width % 128 == 0 else [width]
        second.append(
            call(
                functools.partial(grads_two, n, divisor),
                (
                    shape(2 * width, width),
                    shape(width, width),
                    shape(2 * width, width, dtype=F32),
                    shape(width, width, dtype=F32),
                    shape(2 * width, width),
                )
                + tuple(shape(size, width) for size in cuts),
                [VMEM] * (5 + 3 * (n - 1)),
                (VMEM,) * (5 + len(cuts)),
                grad_scratch,
            )(*kvq[1][h][:2], begin_own[h], *arrived, *pieces)
        )

    out_shape = jax.ShapeDtypeStruct(keys.shape, BF16)
    outputs = None
    for h in range(heads):
        prior = [] if outputs is None else [outputs]
        outputs = call(
            functools.partial(apply_one, h),
            out_shape,
            [VMEM] * 3 + [HBM] * len(prior),
            HBM,
            (row_scratch, DMA((chunks,))),
            aliases={3: 0} if prior else None,
        )(kvq[0][h][2], *packs[h], *prior)

    fast_shape = jax.ShapeDtypeStruct(fast_t.shape, BF16)
    moment_shape = jax.ShapeDtypeStruct(moment_t.shape, F32)
    ends = []
    for h in range(heads):
        gu, down, own_gu, own_down, send_gu, *sends = second[h]
        recv_gu = turned(send_gu)
        recv_down = [turned(x) for x in sends]
        at = 5 + n
        hq, *ends = call(
            functools.partial(update_two_gu, n, h),
            (shape(rows, width), fast_shape, moment_shape),
            [SMEM] * 2 + [VMEM] * (3 + n) + [HBM] * len(ends),
            (VMEM, HBM, HBM),
            (
                pltpu.VMEM((2 * width, width), BF16),
                pltpu.VMEM((width, width), F32),
                pltpu.VMEM((2, part, width), BF16),
                pltpu.VMEM((2, part, width), F32),
                DMA((2, 2)),
            ),
            aliases={at: 1, at + 1: 2} if ends else None,
        )(rates, decays, gu, own_gu, moments[h], kvq[1][h][2], *recv_gu, *ends)
        kept, first_row = [], 0
        for recvs in recv_down:
            size = recvs[0].shape[0]
            last = first_row + size == width
            if last:
                outs = (out_shape, fast_shape, moment_shape)
                aliases = {at + len(kept) + j: j for j in range(3)}
                extra = [*kept, outputs, *ends]
            else:
                outs = (out_shape, shape(width, width), shape(width, width, dtype=F32))
                aliases = {at: 0}
                extra = [outputs]
            buffers = (pltpu.VMEM((width, width), BF16), pltpu.VMEM((width, width), F32))
            mine = (pltpu.VMEM((part, width), BF16), pltpu.VMEM((part, width), F32))
            outputs, *rest = call(
                functools.partial(update_two_down, n, h, first_row),
                outs,
                [SMEM] * 2 + [VMEM] * (3 + n + len(kept)) + [HBM] * (len(extra) - len(kept)),
                (HBM,) * 3 if last else (HBM, VMEM, VMEM),
                (buffers if last else ())
                + (pltpu.VMEM((rows, size), BF16),)
                + (mine if last else ())
                + (DMA((chunks,)),)
                + ((DMA((2,)),) if last else ()),
                aliases=aliases,
            )(rates, decays, down, own_down, moments[h], hq, *recvs, *extra)
            if last:
                ends = rest
            else:
                kept = rest
            first_row += size
    return (outputs, jnp.swapaxes(ends[0], 3, 4), jnp.swapaxes(ends[1], 3, 4))


def solution(mesh):
    placed = (
        P(None, ("block", "tok"), None),
        P(None, ("block", "tok"), None),
        P(None, ("block", "tok"), None),
        P("block", None, None, None, "tok"),
        P("block", None, None, None, "tok"),
        P(None, None, None, "tok"),
        P(),
        P(),
    )
    step = jax.shard_map(
        on_device,
        mesh=mesh,
        in_specs=placed,
        out_specs=(
            P(None, ("block", "tok"), None),
            P("block", None, None, None, "tok"),
            P("block", None, None, None, "tok"),
        ),
        check_vma=False,
    )

    def run(*args):
        with jax.sharding.use_abstract_mesh(mesh.abstract_mesh):
            return step(*args)

    return run
```

```python
import functools

import jax
import jax.numpy as jnp
from jax import lax
from jax.experimental import pallas as pl
from jax.experimental.pallas import tpu as pltpu
from jax.sharding import PartitionSpec as P


F32 = jnp.float32
BF16 = jnp.bfloat16
VMEM = pl.BlockSpec(memory_space=pltpu.VMEM)
HBM = pl.BlockSpec(memory_space=pltpu.HBM)
DMA = pltpu.SemaphoreType.DMA


def mm(a, b, dims):
    return lax.dot_general(a, b, (dims, ((), ())), preferred_element_type=F32)


def call(kernel, out, in_specs, out_specs, scratch=(), aliases=None):
    return pl.pallas_call(
        kernel,
        out_shape=out,
        in_specs=in_specs,
        out_specs=out_specs,
        scratch_shapes=list(scratch),
        input_output_aliases=aliases or {},
        compiler_params=pltpu.CompilerParams(vmem_limit_bytes=12 << 20),
    )


def row_chunks(rows):
    for size in (256, 384, 128):
        if rows % size == 0:
            return [pl.ds(first, size) for first in range(0, rows, size)]
    return [pl.ds(0, rows)]


def assemble(me, shards, gu_ref, down_ref):
    n = len(shards)
    width = down_ref.shape[0]
    part = width // n
    for r, shard in enumerate(shards):
        at = pl.multiple_of(lax.rem(me - r + n, n) * part, part)
        gu_ref[pl.ds(at, part), :] = shard(0)
        gu_ref[pl.ds(width + at, part), :] = shard(1)
        down_ref[pl.ds(at, part), :] = shard(2)


def grads_core(divisor, k_ref, v_ref, gu_ref, down_ref, own_gu, own_down, hid_s, dout_s, dgu_s):
    rows, width = k_ref.shape
    for at in row_chunks(rows):
        both = mm(k_ref[at, :], gu_ref[...], ((1,), (1,)))
        gate, upper = both[:, :width], both[:, width:]
        dout = (-v_ref[at, :].astype(F32) / divisor).astype(BF16)
        dhid = mm(dout, down_ref[...], ((1,), (0,)))
        sigma = jax.nn.sigmoid(gate)
        silu = gate * sigma
        hid_s[at, :] = (silu * upper).astype(BF16)
        dout_s[at, :] = dout
        dgu_s[at, :width] = (dhid * upper * sigma * (1.0 + gate * (1.0 - sigma))).astype(BF16)
        dgu_s[at, width:] = (dhid * silu).astype(BF16)
    own_gu[...] = mm(dgu_s[...], k_ref[...], ((0,), (0,)))
    own_down[...] = mm(dout_s[...], hid_s[...], ((0,), (0,)))


def take_head(head, fast_ref, own_ref):
    pltpu.sync_copy(fast_ref.at[0, :, head], own_ref)


def take_piece(sources, begin_ref, piece_ref):
    block = lax.axis_index("block")
    piece = jnp.int32(0)
    for p, source in enumerate(sources):
        piece = jnp.where(block == source, jnp.int32(p), piece)
    pltpu.sync_copy(begin_ref.at[lax.rem(piece, 3), piece // 3], piece_ref)


def load_all(steps, heads, k_ref, v_ref, q_ref, m_ref, begin_ref, *refs):
    sems = refs[-1]
    copies = []

    def add(source, target):
        copies.append(pltpu.make_async_copy(source, target, sems.at[len(copies)]))
        copies[-1].start()

    targets = list(refs[:-1])
    for step in range(steps):
        for head in range(heads):
            for ref in (k_ref, v_ref, q_ref):
                target = targets.pop(0)
                width = target.shape[1]
                add(ref.at[step, :, pl.ds(head * width, width)], target)
    for head in range(heads):
        add(m_ref.at[0, :, head], targets.pop(0))
    for head in range(heads):
        add(begin_ref.at[:, head], targets.pop(0))
    for copy in copies:
        copy.wait()


def grads_one(n, head, divisor, decay_ref, k_ref, v_ref, m_ref, *refs):
    shards = refs[:n]
    gu_ref, down_ref, send_gu, send_down, own_gu, own_down, hid_s, dout_s, dgu_s = refs[n:]
    width = down_ref.shape[0]
    part = width // n
    me = lax.axis_index("tok")
    assemble(me, [lambda m, ref=ref: ref[m] for ref in shards], gu_ref, down_ref)
    grads_core(divisor, k_ref, v_ref, gu_ref, down_ref, own_gu, own_down, hid_s, dout_s, dgu_s)
    decay = decay_ref[:, head : head + 1]
    mine = pl.multiple_of(me * part, part)
    own_gu[pl.ds(mine, part), :] += decay * m_ref[0]
    own_gu[pl.ds(width + mine, part), :] += decay * m_ref[1]
    own_down[pl.ds(mine, part), :] += decay * m_ref[2]
    send_gu[...] = own_gu[...].astype(BF16)
    send_down[...] = own_down[...].astype(BF16)


def grads_two(n, divisor, k_ref, v_ref, begin_ref, *refs):
    (pgu_ref, pdown_ref), pieces = refs[:2], refs[2 : 2 + 3 * (n - 1)]
    gu_ref, down_ref, own_gu, own_down, send_gu, *sends = refs[2 + 3 * (n - 1) : -3]
    hid_s, dout_s, dgu_s = refs[-3:]
    leading = lax.axis_index("block") == 0

    @pl.when(leading)
    def _():
        shards = [lambda m: begin_ref[m]]
        for r in range(n - 1):
            shards.append(lambda m, r=r: pieces[3 * r + m][...])
        assemble(lax.axis_index("tok"), shards, gu_ref, down_ref)

    @pl.when(jnp.logical_not(leading))
    def _():
        gu_ref[...] = pgu_ref[...]
        down_ref[...] = pdown_ref[...]

    grads_core(divisor, k_ref, v_ref, gu_ref, down_ref, own_gu, own_down, hid_s, dout_s, dgu_s)
    send_gu[...] = own_gu[...].astype(BF16)
    first = 0
    for send in sends:
        send[...] = own_down[pl.ds(first, send.shape[0]), :].astype(BF16)
        first += send.shape[0]


def updated(rate, old_ref, at, moment):
    old = old_ref[at, :].astype(F32)
    moved = old - rate * moment
    old_norm = jnp.sqrt(jnp.mean(old * old, axis=1, keepdims=True) + 1e-06)
    new_norm = jnp.sqrt(jnp.mean(moved * moved, axis=1, keepdims=True) + 1e-06)
    return (moved * (old_norm / new_norm)).astype(BF16)


def summed(own_ref, recvs, first, size, sent_from=0):
    total = own_ref[pl.ds(first, size), :]
    for recv in recvs:
        total = total + recv[pl.ds(first - sent_from, size), :].astype(F32)
    return total


def update_one(n, head, mats, rate_ref, old_ref, own_ref, *refs):
    recvs = refs[: n - 1]
    new_ref, moment_ref = refs[-2:]
    width = own_ref.shape[1]
    for i, m in enumerate(mats):
        at = pl.ds(i * width, width)
        moment = summed(own_ref, recvs, i * width, width)
        new_ref[at, :] = updated(rate_ref[head : head + 1, m : m + 1], old_ref, at, moment)
        moment_ref[m * width : (m + 1) * width, :] = moment.astype(BF16)


def store_mine(n, m, head, me, new_s, moment_s, fast_s, mine_s, fast_ref, moment_ref, sems):
    width = moment_s.shape[1]
    part = width // n
    mine = pl.multiple_of(me * part, part)
    fast_s[...] = new_s[pl.ds(mine, part), :]
    mine_s[...] = moment_s[pl.ds(mine, part), :]
    stores = [
        pltpu.make_async_copy(fast_s, fast_ref.at[0, m, head], sems.at[0]),
        pltpu.make_async_copy(mine_s, moment_ref.at[0, m, head], sems.at[1]),
    ]
    for store in stores:
        store.start()
    return stores


def update_two_gu(n, head, rate_ref, decay_ref, old_ref, own_ref, earlier_ref, q_ref, *refs):
    recvs = refs[: n - 1]
    hq_ref, fast_ref, moment_ref, gu_s, moment_s, fast_s, mine_s, sems = refs[-8:]
    width = own_ref.shape[1]
    stores = []
    for m in range(2):
        at = pl.ds(m * width, width)
        moment = decay_ref[:, head : head + 1] * earlier_ref[at, :].astype(F32)
        moment = moment + summed(own_ref, recvs, m * width, width)
        new_s = gu_s.at[at, :]
        new_s[...] = updated(rate_ref[head : head + 1, m : m + 1], old_ref, at, moment)
        moment_s[...] = moment
        stores += store_mine(
            n,
            m,
            head,
            lax.axis_index("tok"),
            new_s,
            moment_s,
            fast_s.at[m],
            mine_s.at[m],
            fast_ref,
            moment_ref,
            sems.at[m],
        )
    for at in row_chunks(q_ref.shape[0]):
        both = mm(q_ref[at, :], gu_s[...], ((1,), (1,)))
        hq_ref[at, :] = (jax.nn.silu(both[:, :width]) * both[:, width:]).astype(BF16)
    for store in stores:
        store.wait()


def update_two_down(n, head, first, rate_ref, decay_ref, old_ref, own_ref, earlier_ref, hq_ref, *refs):
    recvs = refs[: n - 1]
    width = old_ref.shape[1]
    size = recvs[0].shape[0]
    last = first + size == width
    if last:
        out_ref, fast_ref, moment_ref, new_s, kept_s, out_s, fast_s, mine_s, out_sems, sems = refs[-10:]
    else:
        out_ref, new_s, kept_s, out_s, out_sems = refs[-5:]
    if first and last:
        before_new, before_kept = refs[n - 1 : n + 1]
        new_s[:first, :] = before_new[:first, :]
        kept_s[:first, :] = before_kept[:first, :]
    at = pl.ds(first, size)
    moment = decay_ref[:, head : head + 1] * earlier_ref[pl.ds(2 * width + first, size), :].astype(F32)
    moment = moment + summed(own_ref, recvs, first, size, first)
    new_s[at, :] = updated(rate_ref[head : head + 1, 2:], old_ref, at, moment)
    kept_s[at, :] = moment
    stores = []
    if last:
        me = lax.axis_index("tok")
        stores = store_mine(
            n, 2, head, me, new_s, kept_s, fast_s, mine_s, fast_ref, moment_ref, sems
        )
    cols = pl.ds(head * width + first, size)
    for i, rows in enumerate(row_chunks(hq_ref.shape[0])):
        out_s[rows, :] = mm(hq_ref[rows, :], new_s[at, :], ((1,), (1,))).astype(BF16)
        stores.append(
            pltpu.make_async_copy(out_s.at[rows, :], out_ref.at[1, rows, cols], out_sems.at[i])
        )
        stores[-1].start()
    for store in stores:
        store.wait()


def apply_one(head, q_ref, pgu_ref, pdown_ref, *refs):
    out_ref, out_s, sems = refs[-3:]
    rows, width = q_ref.shape
    stores = []
    for i, at in enumerate(row_chunks(rows)):
        both = mm(q_ref[at, :], pgu_ref[...], ((1,), (1,)))
        hq = (jax.nn.silu(both[:, :width]) * both[:, width:]).astype(BF16)
        out_s[at, :] = mm(hq, pdown_ref[...], ((1,), (1,))).astype(BF16)
        stores.append(
            pltpu.make_async_copy(
                out_s.at[at, :], out_ref.at[0, at, pl.ds(head * width, width)], sems.at[i]
            )
        )
        stores[-1].start()
    for store in stores:
        store.wait()


def on_device(keys, values, queries, fast_in, moment_in, initial_fast, rates, decays):
    n = lax.axis_size("tok")
    blocks = lax.axis_size("block")
    steps, rows, features = keys.shape
    heads = rates.shape[1]
    width = features // heads
    part = width // n
    chunks = len(row_chunks(rows))
    divisor = float(rows * n)
    fast_t = jnp.swapaxes(fast_in, 3, 4)
    moment_t = jnp.swapaxes(moment_in, 3, 4)
    begin_t = jnp.swapaxes(initial_fast, 2, 3)
    rates = rates.T
    decays = decays.reshape(1, heads)
    keys, values, queries, fast_t, moment_t, begin_t = (
        pltpu.with_memory_space_constraint(x, pltpu.HBM)
        for x in (keys, values, queries, fast_t, moment_t, begin_t)
    )

    def turned(x):
        return [lax.ppermute(x, "tok", [(i, (i + r) % n) for i in range(n)]) for r in range(1, n)]

    def forward(x):
        return lax.ppermute(x, "block", [(i, i + 1) for i in range(blocks - 1)])

    def shape(*dims, dtype=BF16):
        return jax.ShapeDtypeStruct(dims, dtype)

    row_scratch = pltpu.VMEM((rows, width), BF16)
    grad_scratch = (row_scratch, row_scratch, pltpu.VMEM((rows, 2 * width), BF16))
    grad_out = (
        shape(2 * width, width),
        shape(width, width),
        shape(2 * width, width),
        shape(width, width),
        shape(2 * width, width, dtype=F32),
        shape(width, width, dtype=F32),
    )

    recv_fast, owned = [], []
    for h in range(heads):
        owned.append(
            call(functools.partial(take_head, h), shape(3, part, width), [HBM], VMEM)(fast_t)
        )
        recv_fast.append(turned(owned[h]))

    sources = [(2 * (p + 1)) % blocks for p in range(3 * heads)]
    piece = call(functools.partial(take_piece, sources), shape(part, width), [HBM], VMEM)(begin_t)
    crossed = [
        lax.ppermute(
            piece,
            ("block", "tok"),
            [(s * n + i, s * n + (i + r) % n) for s in sorted(set(sources)) for i in range(n)],
        )
        for r in range(1, n)
    ]

    loaded = list(
        call(
            functools.partial(load_all, steps, heads),
            (shape(rows, width),) * (3 * steps * heads)
            + (shape(3, part, width, dtype=F32),) * heads
            + (shape(3, part, width),) * heads,
            [HBM] * 5,
            (VMEM,) * (3 * steps * heads + 2 * heads),
            (DMA((3 * steps * heads + 2 * heads,)),),
        )(keys, values, queries, moment_t, begin_t)
    )
    kvq = [[[loaded.pop(0) for _ in range(3)] for _ in range(heads)] for _ in range(steps)]
    m_own, begin_own = loaded[:heads], loaded[heads:]

    first = [
        call(
            functools.partial(grads_one, n, h, divisor),
            grad_out,
            [VMEM] * (4 + n),
            (VMEM,) * 6,
            grad_scratch,
        )(decays, *kvq[0][h][:2], m_own[h], owned[h], *recv_fast[h])
        for h in range(heads)
    ]

    packs, moments = [], []
    for h in range(heads):
        gu, down, send_gu, send_down, own_gu, own_down = first[h]
        recv_gu, recv_down = turned(send_gu), turned(send_down)
        pack, moment = [], []
        for mats, old, own, recvs in (
            ((0, 1), gu, own_gu, recv_gu), ((2,), down, own_down, recv_down)
        ):
            new, *moment = call(
                functools.partial(update_one, n, h, mats),
                (shape(len(mats) * width, width), shape(3 * width, width)),
                [VMEM] * (2 + n + len(moment)),
                (VMEM, VMEM),
                aliases={2 + n: 1} if moment else None,
            )(rates, old, own, *recvs, *moment)
            pack.append(new)
        packs.append(pack)
        moments.append(forward(moment[0]))

    begins = []
    for p in range(3 * heads):
        begins.append(
            [
                lax.ppermute(
                    x, ("block", "tok"), [(sources[p] * n + i, i) for i in range(n)]
                )
                for x in crossed
            ]
        )

    second = []
    for h in range(heads):
        arrived = [forward(packs[h][0]), forward(packs[h][1])]
        pieces = [begins[3 * h + m][r] for r in range(n - 1) for m in range(3)]
        cuts = [width - 128, 128] if h == heads - 1 and width % 128 == 0 else [width]
        second.append(
            call(
                functools.partial(grads_two, n, divisor),
                (
                    shape(2 * width, width),
                    shape(width, width),
                    shape(2 * width, width, dtype=F32),
                    shape(width, width, dtype=F32),
                    shape(2 * width, width),
                )
                + tuple(shape(size, width) for size in cuts),
                [VMEM] * (5 + 3 * (n - 1)),
                (VMEM,) * (5 + len(cuts)),
                grad_scratch,
            )(*kvq[1][h][:2], begin_own[h], *arrived, *pieces)
        )

    out_shape = jax.ShapeDtypeStruct(keys.shape, BF16)
    outputs = None
    for h in range(heads):
        prior = [] if outputs is None else [outputs]
        outputs = call(
            functools.partial(apply_one, h),
            out_shape,
            [VMEM] * 3 + [HBM] * len(prior),
            HBM,
            (row_scratch, DMA((chunks,))),
            aliases={3: 0} if prior else None,
        )(kvq[0][h][2], *packs[h], *prior)

    fast_shape = jax.ShapeDtypeStruct(fast_t.shape, BF16)
    moment_shape = jax.ShapeDtypeStruct(moment_t.shape, F32)
    ends = []
    for h in range(heads):
        gu, down, own_gu, own_down, send_gu, *sends = second[h]
        recv_gu = turned(send_gu)
        recv_down = [turned(x) for x in sends]
        at = 5 + n
        hq, *ends = call(
            functools.partial(update_two_gu, n, h),
            (shape(rows, width), fast_shape, moment_shape),
            [VMEM] * (5 + n) + [HBM] * len(ends),
            (VMEM, HBM, HBM),
            (
                pltpu.VMEM((2 * width, width), BF16),
                pltpu.VMEM((width, width), F32),
                pltpu.VMEM((2, part, width), BF16),
                pltpu.VMEM((2, part, width), F32),
                DMA((2, 2)),
            ),
            aliases={at: 1, at + 1: 2} if ends else None,
        )(rates, decays, gu, own_gu, moments[h], kvq[1][h][2], *recv_gu, *ends)
        kept, first_row = [], 0
        for recvs in recv_down:
            size = recvs[0].shape[0]
            last = first_row + size == width
            if last:
                outs = (out_shape, fast_shape, moment_shape)
                aliases = {at + len(kept) + j: j for j in range(3)}
                extra = [*kept, outputs, *ends]
            else:
                outs = (out_shape, shape(width, width), shape(width, width, dtype=F32))
                aliases = {at: 0}
                extra = [outputs]
            buffers = (pltpu.VMEM((width, width), BF16), pltpu.VMEM((width, width), F32))
            mine = (pltpu.VMEM((part, width), BF16), pltpu.VMEM((part, width), F32))
            outputs, *rest = call(
                functools.partial(update_two_down, n, h, first_row),
                outs,
                [VMEM] * (5 + n + len(kept)) + [HBM] * (len(extra) - len(kept)),
                (HBM,) * 3 if last else (HBM, VMEM, VMEM),
                (buffers if last else ())
                + (pltpu.VMEM((rows, size), BF16),)
                + (mine if last else ())
                + (DMA((chunks,)),)
                + ((DMA((2,)),) if last else ()),
                aliases=aliases,
            )(rates, decays, down, own_down, moments[h], hq, *recvs, *extra)
            if last:
                ends = rest
            else:
                kept = rest
            first_row += size
    return (outputs, jnp.swapaxes(ends[0], 3, 4), jnp.swapaxes(ends[1], 3, 4))


def solution(mesh):
    placed = (
        P(None, ("block", "tok"), None),
        P(None, ("block", "tok"), None),
        P(None, ("block", "tok"), None),
        P("block", None, None, None, "tok"),
        P("block", None, None, None, "tok"),
        P(None, None, None, "tok"),
        P(),
        P(),
    )
    step = jax.shard_map(
        on_device,
        mesh=mesh,
        in_specs=placed,
        out_specs=(
            P(None, ("block", "tok"), None),
            P("block", None, None, None, "tok"),
            P("block", None, None, None, "tok"),
        ),
        check_vma=False,
    )

    def run(*args):
        with jax.sharding.use_abstract_mesh(mesh.abstract_mesh):
            return step(*args)

    return run
```

```python
import functools

import jax
import jax.numpy as jnp
from jax import lax
from jax.experimental import pallas as pl
from jax.experimental.pallas import tpu as pltpu
from jax.sharding import PartitionSpec as P


F32 = jnp.float32
BF16 = jnp.bfloat16
VMEM = pl.BlockSpec(memory_space=pltpu.VMEM)
HBM = pl.BlockSpec(memory_space=pltpu.HBM)
DMA = pltpu.SemaphoreType.DMA


def mm(a, b, dims):
    return lax.dot_general(a, b, (dims, ((), ())), preferred_element_type=F32)


def call(kernel, out, in_specs, out_specs, scratch=(), aliases=None):
    return pl.pallas_call(
        kernel,
        out_shape=out,
        in_specs=in_specs,
        out_specs=out_specs,
        scratch_shapes=list(scratch),
        input_output_aliases=aliases or {},
        compiler_params=pltpu.CompilerParams(vmem_limit_bytes=12 << 20),
    )


def row_chunks(rows):
    for size in (256, 384, 128):
        if rows % size == 0:
            return [pl.ds(first, size) for first in range(0, rows, size)]
    return [pl.ds(0, rows)]


def assemble(me, shards, gu_ref, down_ref):
    n = len(shards)
    width = down_ref.shape[0]
    part = width // n
    for r, shard in enumerate(shards):
        at = pl.multiple_of(lax.rem(me - r + n, n) * part, part)
        gu_ref[pl.ds(at, part), :] = shard(0)
        gu_ref[pl.ds(width + at, part), :] = shard(1)
        down_ref[pl.ds(at, part), :] = shard(2)


def grads_core(divisor, k_ref, v_ref, gu_ref, down_ref, own_gu, own_down, hid_s, dout_s, dgu_s):
    rows, width = k_ref.shape
    for at in row_chunks(rows):
        both = mm(k_ref[at, :], gu_ref[...], ((1,), (1,)))
        gate, upper = both[:, :width], both[:, width:]
        dout = (-v_ref[at, :].astype(F32) / divisor).astype(BF16)
        dhid = mm(dout, down_ref[...], ((1,), (0,)))
        sigma = jax.nn.sigmoid(gate)
        silu = gate * sigma
        hid_s[at, :] = (silu * upper).astype(BF16)
        dout_s[at, :] = dout
        dgu_s[at, :width] = (dhid * upper * sigma * (1.0 + gate * (1.0 - sigma))).astype(BF16)
        dgu_s[at, width:] = (dhid * silu).astype(BF16)
    own_gu[...] = mm(dgu_s[...], k_ref[...], ((0,), (0,)))
    own_down[...] = mm(dout_s[...], hid_s[...], ((0,), (0,)))


def take_head(head, fast_ref, own_ref, sems):
    copies = [
        pltpu.make_async_copy(fast_ref.at[0, m, head], own_ref.at[m], sems.at[m])
        for m in range(own_ref.shape[0])
    ]
    for copy in copies:
        copy.start()
    for copy in copies:
        copy.wait()


def take_piece(sources, begin_ref, piece_ref):
    block = lax.axis_index("block")
    piece = jnp.int32(0)
    for p, source in enumerate(sources):
        piece = jnp.where(block == source, jnp.int32(p), piece)
    pltpu.sync_copy(begin_ref.at[lax.rem(piece, 3), piece // 3], piece_ref)


def load_all(steps, heads, k_ref, v_ref, q_ref, m_ref, begin_ref, *refs):
    sems = refs[-1]
    copies = []

    def add(source, target):
        copies.append(pltpu.make_async_copy(source, target, sems.at[len(copies)]))
        copies[-1].start()

    targets = list(refs[:-1])
    for step in range(steps):
        for head in range(heads):
            for ref in (k_ref, v_ref, q_ref):
                target = targets.pop(0)
                width = target.shape[1]
                add(ref.at[step, :, pl.ds(head * width, width)], target)
    for head in range(heads):
        add(m_ref.at[0, :, head], targets.pop(0))
    for head in range(heads):
        add(begin_ref.at[:, head], targets.pop(0))
    for copy in copies:
        copy.wait()


def grads_one(n, head, divisor, decay_ref, k_ref, v_ref, m_ref, *refs):
    shards = refs[:n]
    gu_ref, down_ref, send_gu, send_down, own_gu, own_down, hid_s, dout_s, dgu_s = refs[n:]
    width = down_ref.shape[0]
    part = width // n
    me = lax.axis_index("tok")
    assemble(me, [lambda m, ref=ref: ref[m] for ref in shards], gu_ref, down_ref)
    grads_core(divisor, k_ref, v_ref, gu_ref, down_ref, own_gu, own_down, hid_s, dout_s, dgu_s)
    decay = decay_ref[:, head : head + 1]
    mine = pl.multiple_of(me * part, part)
    own_gu[pl.ds(mine, part), :] += decay * m_ref[0]
    own_gu[pl.ds(width + mine, part), :] += decay * m_ref[1]
    own_down[pl.ds(mine, part), :] += decay * m_ref[2]
    send_gu[...] = own_gu[...].astype(BF16)
    send_down[...] = own_down[...].astype(BF16)


def grads_two(n, divisor, k_ref, v_ref, begin_ref, *refs):
    (pgu_ref, pdown_ref), pieces = refs[:2], refs[2 : 2 + 3 * (n - 1)]
    gu_ref, down_ref, own_gu, own_down, send_gu, *sends = refs[2 + 3 * (n - 1) : -3]
    hid_s, dout_s, dgu_s = refs[-3:]
    leading = lax.axis_index("block") == 0

    @pl.when(leading)
    def _():
        shards = [lambda m: begin_ref[m]]
        for r in range(n - 1):
            shards.append(lambda m, r=r: pieces[3 * r + m][...])
        assemble(lax.axis_index("tok"), shards, gu_ref, down_ref)

    @pl.when(jnp.logical_not(leading))
    def _():
        gu_ref[...] = pgu_ref[...]
        down_ref[...] = pdown_ref[...]

    grads_core(divisor, k_ref, v_ref, gu_ref, down_ref, own_gu, own_down, hid_s, dout_s, dgu_s)
    send_gu[...] = own_gu[...].astype(BF16)
    first = 0
    for send in sends:
        send[...] = own_down[pl.ds(first, send.shape[0]), :].astype(BF16)
        first += send.shape[0]


def updated(rate, old_ref, at, moment):
    old = old_ref[at, :].astype(F32)
    moved = old - rate * moment
    old_norm = jnp.sqrt(jnp.mean(old * old, axis=1, keepdims=True) + 1e-06)
    new_norm = jnp.sqrt(jnp.mean(moved * moved, axis=1, keepdims=True) + 1e-06)
    return (moved * (old_norm / new_norm)).astype(BF16)


def summed(own_ref, recvs, first, size, sent_from=0):
    total = own_ref[pl.ds(first, size), :]
    for recv in recvs:
        total = total + recv[pl.ds(first - sent_from, size), :].astype(F32)
    return total


def update_one(n, head, mats, rate_ref, old_ref, own_ref, *refs):
    recvs = refs[: n - 1]
    new_ref, moment_ref = refs[-2:]
    width = own_ref.shape[1]
    if mats[0]:
        before = refs[n - 1]
        moment_ref[: mats[0] * width, :] = before[...]
    for i, m in enumerate(mats):
        at = pl.ds(i * width, width)
        moment = summed(own_ref, recvs, i * width, width)
        new_ref[at, :] = updated(rate_ref[head : head + 1, m : m + 1], old_ref, at, moment)
        moment_ref[m * width : (m + 1) * width, :] = moment.astype(BF16)


def store_mine(n, m, head, me, new_s, moment_s, fast_s, mine_s, fast_ref, moment_ref, sems):
    width = moment_s.shape[1]
    part = width // n
    mine = pl.multiple_of(me * part, part)
    fast_s[...] = new_s[pl.ds(mine, part), :]
    mine_s[...] = moment_s[pl.ds(mine, part), :]
    stores = [
        pltpu.make_async_copy(fast_s, fast_ref.at[0, m, head], sems.at[0]),
        pltpu.make_async_copy(mine_s, moment_ref.at[0, m, head], sems.at[1]),
    ]
    for store in stores:
        store.start()
    return stores


def update_two_gu(n, head, rate_ref, decay_ref, old_ref, own_ref, earlier_ref, q_ref, *refs):
    recvs = refs[: n - 1]
    hq_ref, fast_ref, moment_ref, gu_s, moment_s, fast_s, mine_s, sems = refs[-8:]
    width = own_ref.shape[1]
    stores = []
    for m in range(2):
        at = pl.ds(m * width, width)
        moment = decay_ref[:, head : head + 1] * earlier_ref[at, :].astype(F32)
        moment = moment + summed(own_ref, recvs, m * width, width)
        new_s = gu_s.at[at, :]
        new_s[...] = updated(rate_ref[head : head + 1, m : m + 1], old_ref, at, moment)
        moment_s[...] = moment
        stores += store_mine(
            n,
            m,
            head,
            lax.axis_index("tok"),
            new_s,
            moment_s,
            fast_s.at[m],
            mine_s.at[m],
            fast_ref,
            moment_ref,
            sems.at[m],
        )
    for at in row_chunks(q_ref.shape[0]):
        both = mm(q_ref[at, :], gu_s[...], ((1,), (1,)))
        hq_ref[at, :] = (jax.nn.silu(both[:, :width]) * both[:, width:]).astype(BF16)
    for store in stores:
        store.wait()


def update_two_down(n, head, first, rate_ref, decay_ref, old_ref, own_ref, earlier_ref, hq_ref, *refs):
    recvs = refs[: n - 1]
    width = old_ref.shape[1]
    size = recvs[0].shape[0]
    last = first + size == width
    if last:
        out_ref, fast_ref, moment_ref, new_s, kept_s, out_s, fast_s, mine_s, out_sems, sems = refs[-10:]
    else:
        out_ref, new_s, kept_s, out_s, out_sems = refs[-5:]
    if first and last:
        before_new, before_kept = refs[n - 1 : n + 1]
        new_s[:first, :] = before_new[:first, :]
        kept_s[:first, :] = before_kept[:first, :]
    at = pl.ds(first, size)
    moment = decay_ref[:, head : head + 1] * earlier_ref[pl.ds(2 * width + first, size), :].astype(F32)
    moment = moment + summed(own_ref, recvs, first, size, first)
    new_s[at, :] = updated(rate_ref[head : head + 1, 2:], old_ref, at, moment)
    kept_s[at, :] = moment
    stores = []
    if last:
        me = lax.axis_index("tok")
        stores = store_mine(
            n, 2, head, me, new_s, kept_s, fast_s, mine_s, fast_ref, moment_ref, sems
        )
    cols = pl.ds(head * width + first, size)
    for i, rows in enumerate(row_chunks(hq_ref.shape[0])):
        out_s[rows, :] = mm(hq_ref[rows, :], new_s[at, :], ((1,), (1,))).astype(BF16)
        stores.append(
            pltpu.make_async_copy(out_s.at[rows, :], out_ref.at[1, rows, cols], out_sems.at[i])
        )
        stores[-1].start()
    for store in stores:
        store.wait()


def apply_one(head, q_ref, pgu_ref, pdown_ref, *refs):
    out_ref, out_s, sems = refs[-3:]
    rows, width = q_ref.shape
    stores = []
    for i, at in enumerate(row_chunks(rows)):
        both = mm(q_ref[at, :], pgu_ref[...], ((1,), (1,)))
        hq = (jax.nn.silu(both[:, :width]) * both[:, width:]).astype(BF16)
        out_s[at, :] = mm(hq, pdown_ref[...], ((1,), (1,))).astype(BF16)
        stores.append(
            pltpu.make_async_copy(
                out_s.at[at, :], out_ref.at[0, at, pl.ds(head * width, width)], sems.at[i]
            )
        )
        stores[-1].start()
    for store in stores:
        store.wait()


def on_device(keys, values, queries, fast_in, moment_in, initial_fast, rates, decays):
    n = lax.axis_size("tok")
    blocks = lax.axis_size("block")
    steps, rows, features = keys.shape
    heads = rates.shape[1]
    width = features // heads
    part = width // n
    chunks = len(row_chunks(rows))
    divisor = float(rows * n)
    fast_t = jnp.swapaxes(fast_in, 3, 4)
    moment_t = jnp.swapaxes(moment_in, 3, 4)
    begin_t = jnp.swapaxes(initial_fast, 2, 3)
    rates = rates.T
    decays = decays.reshape(1, heads)
    keys, values, queries, fast_t, moment_t, begin_t = (
        pltpu.with_memory_space_constraint(x, pltpu.HBM)
        for x in (keys, values, queries, fast_t, moment_t, begin_t)
    )

    def turned(x):
        return [lax.ppermute(x, "tok", [(i, (i + r) % n) for i in range(n)]) for r in range(1, n)]

    def forward(x):
        return lax.ppermute(x, "block", [(i, i + 1) for i in range(blocks - 1)])

    def shape(*dims, dtype=BF16):
        return jax.ShapeDtypeStruct(dims, dtype)

    row_scratch = pltpu.VMEM((rows, width), BF16)
    grad_scratch = (row_scratch, row_scratch, pltpu.VMEM((rows, 2 * width), BF16))
    grad_out = (
        shape(2 * width, width),
        shape(width, width),
        shape(2 * width, width),
        shape(width, width),
        shape(2 * width, width, dtype=F32),
        shape(width, width, dtype=F32),
    )

    recv_fast, owned = [], []
    for h in range(heads):
        owned.append(
            call(
                functools.partial(take_head, h), shape(3, part, width), [HBM], VMEM, (DMA((3,)),)
            )(fast_t)
        )
        recv_fast.append(turned(owned[h]))

    apart = max(blocks // (3 * heads + 2), 1)
    sources = [apart * (p + 1) % blocks for p in range(3 * heads)]
    piece = call(functools.partial(take_piece, sources), shape(part, width), [HBM], VMEM)(begin_t)
    crossed = [
        lax.ppermute(
            piece,
            ("block", "tok"),
            [(s * n + i, s * n + (i + r) % n) for s in sorted(set(sources)) for i in range(n)],
        )
        for r in range(1, n)
    ]

    loaded = list(
        call(
            functools.partial(load_all, steps, heads),
            (shape(rows, width),) * (3 * steps * heads)
            + (shape(3, part, width, dtype=F32),) * heads
            + (shape(3, part, width),) * heads,
            [HBM] * 5,
            (VMEM,) * (3 * steps * heads + 2 * heads),
            (DMA((3 * steps * heads + 2 * heads,)),),
        )(keys, values, queries, moment_t, begin_t)
    )
    kvq = [[[loaded.pop(0) for _ in range(3)] for _ in range(heads)] for _ in range(steps)]
    m_own, begin_own = loaded[:heads], loaded[heads:]

    first = [
        call(
            functools.partial(grads_one, n, h, divisor),
            grad_out,
            [VMEM] * (4 + n),
            (VMEM,) * 6,
            grad_scratch,
        )(decays, *kvq[0][h][:2], m_own[h], owned[h], *recv_fast[h])
        for h in range(heads)
    ]

    packs, moments = [], []
    for h in range(heads):
        gu, down, send_gu, send_down, own_gu, own_down = first[h]
        recv_gu, recv_down = turned(send_gu), turned(send_down)
        pack, moment = [], []
        for mats, old, own, recvs in (
            ((0, 1), gu, own_gu, recv_gu), ((2,), down, own_down, recv_down)
        ):
            new, *moment = call(
                functools.partial(update_one, n, h, mats),
                (shape(len(mats) * width, width), shape((mats[-1] + 1) * width, width)),
                [VMEM] * (2 + n + len(moment)),
                (VMEM, VMEM),
            )(rates, old, own, *recvs, *moment)
            pack.append(new)
        packs.append(pack)
        moments.append(forward(moment[0]))

    begins = []
    for p in range(3 * heads):
        begins.append(
            [
                lax.ppermute(
                    x, ("block", "tok"), [(sources[p] * n + i, i) for i in range(n)]
                )
                for x in crossed
            ]
        )

    second = []
    for h in range(heads):
        arrived = [forward(packs[h][0]), forward(packs[h][1])]
        pieces = [begins[3 * h + m][r] for r in range(n - 1) for m in range(3)]
        cuts = [128, width - 128] if h == heads - 1 and width % 128 == 0 else [width]
        second.append(
            call(
                functools.partial(grads_two, n, divisor),
                (
                    shape(2 * width, width),
                    shape(width, width),
                    shape(2 * width, width, dtype=F32),
                    shape(width, width, dtype=F32),
                    shape(2 * width, width),
                )
                + tuple(shape(size, width) for size in cuts),
                [VMEM] * (5 + 3 * (n - 1)),
                (VMEM,) * (5 + len(cuts)),
                grad_scratch,
            )(*kvq[1][h][:2], begin_own[h], *arrived, *pieces)
        )

    out_shape = jax.ShapeDtypeStruct(keys.shape, BF16)
    outputs = None
    for h in range(heads):
        prior = [] if outputs is None else [outputs]
        outputs = call(
            functools.partial(apply_one, h),
            out_shape,
            [VMEM] * 3 + [HBM] * len(prior),
            HBM,
            (row_scratch, DMA((chunks,))),
            aliases={3: 0} if prior else None,
        )(kvq[0][h][2], *packs[h], *prior)

    fast_shape = jax.ShapeDtypeStruct(fast_t.shape, BF16)
    moment_shape = jax.ShapeDtypeStruct(moment_t.shape, F32)
    ends = []
    for h in range(heads):
        gu, down, own_gu, own_down, send_gu, *sends = second[h]
        recv_gu = turned(send_gu)
        recv_down = [turned(x) for x in sends]
        at = 5 + n
        hq, *ends = call(
            functools.partial(update_two_gu, n, h),
            (shape(rows, width), fast_shape, moment_shape),
            [VMEM] * (5 + n) + [HBM] * len(ends),
            (VMEM, HBM, HBM),
            (
                pltpu.VMEM((2 * width, width), BF16),
                pltpu.VMEM((width, width), F32),
                pltpu.VMEM((2, part, width), BF16),
                pltpu.VMEM((2, part, width), F32),
                DMA((2, 2)),
            ),
            aliases={at: 1, at + 1: 2} if ends else None,
        )(rates, decays, gu, own_gu, moments[h], kvq[1][h][2], *recv_gu, *ends)
        kept, first_row = [], 0
        for recvs in recv_down:
            size = recvs[0].shape[0]
            last = first_row + size == width
            if last:
                outs = (out_shape, fast_shape, moment_shape)
                aliases = {at + len(kept) + j: j for j in range(3)}
                extra = [*kept, outputs, *ends]
            else:
                outs = (out_shape, shape(width, width), shape(width, width, dtype=F32))
                aliases = {at: 0}
                extra = [outputs]
            buffers = (pltpu.VMEM((width, width), BF16), pltpu.VMEM((width, width), F32))
            mine = (pltpu.VMEM((part, width), BF16), pltpu.VMEM((part, width), F32))
            outputs, *rest = call(
                functools.partial(update_two_down, n, h, first_row),
                outs,
                [VMEM] * (5 + n + len(kept)) + [HBM] * (len(extra) - len(kept)),
                (HBM,) * 3 if last else (HBM, VMEM, VMEM),
                (buffers if last else ())
                + (pltpu.VMEM((rows, size), BF16),)
                + (mine if last else ())
                + (DMA((chunks,)),)
                + ((DMA((2,)),) if last else ()),
                aliases=aliases,
            )(rates, decays, down, own_down, moments[h], hq, *recvs, *extra)
            if last:
                ends = rest
            else:
                kept = rest
            first_row += size
    return (outputs, jnp.swapaxes(ends[0], 3, 4), jnp.swapaxes(ends[1], 3, 4))


def solution(mesh):
    placed = (
        P(None, ("block", "tok"), None),
        P(None, ("block", "tok"), None),
        P(None, ("block", "tok"), None),
        P("block", None, None, None, "tok"),
        P("block", None, None, None, "tok"),
        P(None, None, None, "tok"),
        P(),
        P(),
    )
    step = jax.shard_map(
        on_device,
        mesh=mesh,
        in_specs=placed,
        out_specs=(
            P(None, ("block", "tok"), None),
            P("block", None, None, None, "tok"),
            P("block", None, None, None, "tok"),
        ),
        check_vma=False,
    )

    def run(*args):
        with jax.sharding.use_abstract_mesh(mesh.abstract_mesh):
            return step(*args)

    return run
```

```python
import functools
import math

import jax
import jax.numpy as jnp
from jax import lax
from jax.experimental import pallas as pl
from jax.experimental.pallas import tpu as pltpu
from jax.sharding import PartitionSpec as P


F32 = jnp.float32
BF16 = jnp.bfloat16
VMEM = pl.BlockSpec(memory_space=pltpu.VMEM)
HBM = pl.BlockSpec(memory_space=pltpu.HBM)
DMA = pltpu.SemaphoreType.DMA


def mm(a, b, dims):
    return lax.dot_general(a, b, (dims, ((), ())), preferred_element_type=F32)


def call(kernel, out, in_specs, out_specs, scratch=(), aliases=None):
    return pl.pallas_call(
        kernel,
        out_shape=out,
        in_specs=in_specs,
        out_specs=out_specs,
        scratch_shapes=list(scratch),
        input_output_aliases=aliases or {},
        compiler_params=pltpu.CompilerParams(vmem_limit_bytes=12 << 20),
    )


def row_chunks(rows):
    for size in (256, 384, 128):
        if rows % size == 0:
            return [pl.ds(first, size) for first in range(0, rows, size)]
    return [pl.ds(0, rows)]


def assemble(me, shards, gu_ref, down_ref):
    n = len(shards)
    width = down_ref.shape[0]
    part = width // n
    for r, shard in enumerate(shards):
        at = pl.multiple_of(lax.rem(me - r + n, n) * part, part)
        gu_ref[pl.ds(at, part), :] = shard(0)
        gu_ref[pl.ds(width + at, part), :] = shard(1)
        down_ref[pl.ds(at, part), :] = shard(2)


def grads_core(divisor, k_ref, v_ref, gu_ref, down_ref, own_gu, own_down, hid_s, dout_s, dgu_s):
    rows, width = k_ref.shape
    for at in row_chunks(rows):
        both = mm(k_ref[at, :], gu_ref[...], ((1,), (1,)))
        gate, upper = both[:, :width], both[:, width:]
        dout = (-v_ref[at, :].astype(F32) / divisor).astype(BF16)
        dhid = mm(dout, down_ref[...], ((1,), (0,)))
        sigma = jax.nn.sigmoid(gate)
        silu = gate * sigma
        hid_s[at, :] = (silu * upper).astype(BF16)
        dout_s[at, :] = dout
        dgu_s[at, :width] = (dhid * upper * sigma * (1.0 + gate * (1.0 - sigma))).astype(BF16)
        dgu_s[at, width:] = (dhid * silu).astype(BF16)
    own_gu[...] = mm(dgu_s[...], k_ref[...], ((0,), (0,)))
    own_down[...] = mm(dout_s[...], hid_s[...], ((0,), (0,)))


def take_head(head, fast_ref, own_ref):
    pltpu.sync_copy(fast_ref.at[0, :, head], own_ref)


def take_piece(sources, begin_ref, piece_ref):
    block = lax.axis_index("block")
    piece = jnp.int32(0)
    for p, source in enumerate(sources):
        piece = jnp.where(block == source, jnp.int32(p), piece)
    pltpu.sync_copy(begin_ref.at[lax.rem(piece, 3), piece // 3], piece_ref)


def load_all(steps, heads, k_ref, v_ref, q_ref, m_ref, begin_ref, *refs):
    sems = refs[-1]
    copies = []

    def add(source, target):
        copies.append(pltpu.make_async_copy(source, target, sems.at[len(copies)]))
        copies[-1].start()

    targets = list(refs[:-1])
    for step in range(steps):
        for head in range(heads):
            for ref in (k_ref, v_ref, q_ref):
                target = targets.pop(0)
                width = target.shape[1]
                add(ref.at[step, :, pl.ds(head * width, width)], target)
    for head in range(heads):
        add(m_ref.at[0, :, head], targets.pop(0))
    for head in range(heads):
        add(begin_ref.at[:, head], targets.pop(0))
    for copy in copies:
        copy.wait()


def grads_one(n, head, divisor, decay_ref, k_ref, v_ref, m_ref, *refs):
    shards = refs[:n]
    gu_ref, down_ref, send_gu, send_down, own_gu, own_down, hid_s, dout_s, dgu_s = refs[n:]
    width = down_ref.shape[0]
    part = width // n
    me = lax.axis_index("tok")
    assemble(me, [lambda m, ref=ref: ref[m] for ref in shards], gu_ref, down_ref)
    grads_core(divisor, k_ref, v_ref, gu_ref, down_ref, own_gu, own_down, hid_s, dout_s, dgu_s)
    decay = decay_ref[:, head : head + 1]
    mine = pl.multiple_of(me * part, part)
    own_gu[pl.ds(mine, part), :] += decay * m_ref[0]
    own_gu[pl.ds(width + mine, part), :] += decay * m_ref[1]
    own_down[pl.ds(mine, part), :] += decay * m_ref[2]
    send_gu[...] = own_gu[...].astype(BF16)
    send_down[...] = own_down[...].astype(BF16)


def grads_two(n, divisor, k_ref, v_ref, begin_ref, *refs):
    (pgu_ref, pdown_ref), pieces = refs[:2], refs[2 : 2 + 3 * (n - 1)]
    gu_ref, down_ref, own_gu, own_down, send_gu, *sends = refs[2 + 3 * (n - 1) : -3]
    hid_s, dout_s, dgu_s = refs[-3:]
    leading = lax.axis_index("block") == 0

    @pl.when(leading)
    def _():
        shards = [lambda m: begin_ref[m]]
        for r in range(n - 1):
            shards.append(lambda m, r=r: pieces[3 * r + m][...])
        assemble(lax.axis_index("tok"), shards, gu_ref, down_ref)

    @pl.when(jnp.logical_not(leading))
    def _():
        gu_ref[...] = pgu_ref[...]
        down_ref[...] = pdown_ref[...]

    grads_core(divisor, k_ref, v_ref, gu_ref, down_ref, own_gu, own_down, hid_s, dout_s, dgu_s)
    send_gu[...] = own_gu[...].astype(BF16)
    if len(sends) == 1:
        sends[0][...] = own_down[...].astype(BF16)
    else:
        partner = 1 - lax.axis_index("tok")
        for send, (first, size) in zip(sends, cut_rows(down_ref.shape[0], partner)):
            send[...] = own_down[pl.ds(first, size), :].astype(BF16)


def cut_rows(width, tok):
    return (
        (pl.multiple_of(tok * 128, 128), width - 128),
        (pl.multiple_of((1 - tok) * (width - 128), 128), 128),
    )


def updated(rate, old_ref, at, moment):
    old = old_ref[at, :].astype(F32)
    moved = old - rate * moment
    old_norm = jnp.sqrt(jnp.mean(old * old, axis=1, keepdims=True) + 1e-06)
    new_norm = jnp.sqrt(jnp.mean(moved * moved, axis=1, keepdims=True) + 1e-06)
    return (moved * (old_norm / new_norm)).astype(BF16)


def summed(own_ref, recvs, first, size, recv_first):
    total = own_ref[pl.ds(first, size), :]
    for recv in recvs:
        total = total + recv[pl.ds(recv_first, size), :].astype(F32)
    return total


def update_one(n, head, mats, rate_ref, old_ref, own_ref, *refs):
    recvs = refs[: n - 1]
    new_ref, moment_ref = refs[-2:]
    width = own_ref.shape[1]
    if mats[0]:
        before = refs[n - 1]
        moment_ref[: mats[0] * width, :] = before[...]
    for i, m in enumerate(mats):
        at = pl.ds(i * width, width)
        moment = summed(own_ref, recvs, i * width, width, i * width)
        new_ref[at, :] = updated(rate_ref[head : head + 1, m : m + 1], old_ref, at, moment)
        moment_ref[m * width : (m + 1) * width, :] = moment.astype(BF16)


def store_mine(m, head, mine, new_s, moment_s, fast_s, mine_s, fast_ref, moment_ref, sems):
    part = fast_s.shape[0]
    fast_s[...] = new_s[pl.ds(mine, part), :]
    mine_s[...] = moment_s[pl.ds(mine, part), :]
    stores = [
        pltpu.make_async_copy(fast_s, fast_ref.at[0, m, head], sems.at[0]),
        pltpu.make_async_copy(mine_s, moment_ref.at[0, m, head], sems.at[1]),
    ]
    for store in stores:
        store.start()
    return stores


def update_two_gu(n, head, rate_ref, decay_ref, old_ref, own_ref, earlier_ref, q_ref, *refs):
    recvs = refs[: n - 1]
    hq_ref, fast_ref, moment_ref, gu_s, moment_s, fast_s, mine_s, sems = refs[-8:]
    width = own_ref.shape[1]
    part = width // n
    mine = pl.multiple_of(lax.axis_index("tok") * part, part)
    stores = []
    for m in range(2):
        at = pl.ds(m * width, width)
        moment = decay_ref[:, head : head + 1] * earlier_ref[at, :].astype(F32)
        moment = moment + summed(own_ref, recvs, m * width, width, m * width)
        new_s = gu_s.at[at, :]
        new_s[...] = updated(rate_ref[head : head + 1, m : m + 1], old_ref, at, moment)
        moment_s[...] = moment
        stores += store_mine(
            m,
            head,
            mine,
            new_s,
            moment_s,
            fast_s.at[m],
            mine_s.at[m],
            fast_ref,
            moment_ref,
            sems.at[m],
        )
    for at in row_chunks(q_ref.shape[0]):
        both = mm(q_ref[at, :], gu_s[...], ((1,), (1,)))
        hq_ref[at, :] = (jax.nn.silu(both[:, :width]) * both[:, width:]).astype(BF16)
    for store in stores:
        store.wait()


def update_two_down(n, head, cut, rate_ref, decay_ref, old_ref, own_ref, earlier_ref, hq_ref, *refs):
    recvs = refs[: n - 1]
    width = old_ref.shape[1]
    part = width // n
    me = lax.axis_index("tok")
    if cut is None:
        first, size, mine = 0, width, me * part
    else:
        first, size = cut_rows(width, me)[cut]
        mine = me * part - first
    at = pl.ds(first, size)
    if cut == 1:
        out_ref, new_s, out_s, out_sems = refs[-4:]
    else:
        out_ref, fast_ref, moment_ref, new_s, out_s, out_sems, kept_s, fast_s, mine_s, sems = refs[-10:]
    moment = decay_ref[:, head : head + 1] * earlier_ref[pl.ds(2 * width + first, size), :].astype(F32)
    moment = moment + summed(own_ref, recvs, first, size, 0)
    new_s[...] = updated(rate_ref[head : head + 1, 2:], old_ref, at, moment)
    stores = []
    if cut != 1:
        kept_s[...] = moment
        mine = pl.multiple_of(mine, math.gcd(part, 128))
        stores = store_mine(
            2, head, mine, new_s, kept_s, fast_s, mine_s, fast_ref, moment_ref, sems
        )
    cols = pl.ds(pl.multiple_of(head * width + first, 128), size)
    for i, rows in enumerate(row_chunks(hq_ref.shape[0])):
        out_s[rows, :] = mm(hq_ref[rows, :], new_s[...], ((1,), (1,))).astype(BF16)
        stores.append(
            pltpu.make_async_copy(out_s.at[rows, :], out_ref.at[1, rows, cols], out_sems.at[i])
        )
        stores[-1].start()
    for store in stores:
        store.wait()


def apply_one(head, q_ref, pgu_ref, pdown_ref, *refs):
    out_ref, out_s, sems = refs[-3:]
    rows, width = q_ref.shape
    stores = []
    for i, at in enumerate(row_chunks(rows)):
        both = mm(q_ref[at, :], pgu_ref[...], ((1,), (1,)))
        hq = (jax.nn.silu(both[:, :width]) * both[:, width:]).astype(BF16)
        out_s[at, :] = mm(hq, pdown_ref[...], ((1,), (1,))).astype(BF16)
        stores.append(
            pltpu.make_async_copy(
                out_s.at[at, :], out_ref.at[0, at, pl.ds(head * width, width)], sems.at[i]
            )
        )
        stores[-1].start()
    for store in stores:
        store.wait()


def on_device(keys, values, queries, fast_in, moment_in, initial_fast, rates, decays):
    n = lax.axis_size("tok")
    blocks = lax.axis_size("block")
    steps, rows, features = keys.shape
    heads = rates.shape[1]
    width = features // heads
    part = width // n
    chunks = len(row_chunks(rows))
    divisor = float(rows * n)
    fast_t = jnp.swapaxes(fast_in, 3, 4)
    moment_t = jnp.swapaxes(moment_in, 3, 4)
    begin_t = jnp.swapaxes(initial_fast, 2, 3)
    rates = rates.T
    decays = decays.reshape(1, heads)
    keys, values, queries, fast_t, moment_t, begin_t = (
        pltpu.with_memory_space_constraint(x, pltpu.HBM)
        for x in (keys, values, queries, fast_t, moment_t, begin_t)
    )

    def turned(x):
        return [lax.ppermute(x, "tok", [(i, (i + r) % n) for i in range(n)]) for r in range(1, n)]

    def forward(x):
        return lax.ppermute(x, "block", [(i, i + 1) for i in range(blocks - 1)])

    def shape(*dims, dtype=BF16):
        return jax.ShapeDtypeStruct(dims, dtype)

    row_scratch = pltpu.VMEM((rows, width), BF16)
    grad_scratch = (row_scratch, row_scratch, pltpu.VMEM((rows, 2 * width), BF16))
    grad_out = (
        shape(2 * width, width),
        shape(width, width),
        shape(2 * width, width),
        shape(width, width),
        shape(2 * width, width, dtype=F32),
        shape(width, width, dtype=F32),
    )

    recv_fast, owned = [], []
    for h in range(heads):
        owned.append(
            call(functools.partial(take_head, h), shape(3, part, width), [HBM], VMEM)(fast_t)
        )
        recv_fast.append(turned(owned[h]))

    apart = max(blocks // (3 * heads + 2), 1)
    sources = [apart * (p + 1) % blocks for p in range(3 * heads)]
    piece = call(functools.partial(take_piece, sources), shape(part, width), [HBM], VMEM)(begin_t)
    crossed = [
        lax.ppermute(
            piece,
            ("block", "tok"),
            [(s * n + i, s * n + (i + r) % n) for s in sorted(set(sources)) for i in range(n)],
        )
        for r in range(1, n)
    ]

    loaded = list(
        call(
            functools.partial(load_all, steps, heads),
            (shape(rows, width),) * (3 * steps * heads)
            + (shape(3, part, width, dtype=F32),) * heads
            + (shape(3, part, width),) * heads,
            [HBM] * 5,
            (VMEM,) * (3 * steps * heads + 2 * heads),
            (DMA((3 * steps * heads + 2 * heads,)),),
        )(keys, values, queries, moment_t, begin_t)
    )
    kvq = [[[loaded.pop(0) for _ in range(3)] for _ in range(heads)] for _ in range(steps)]
    m_own, begin_own = loaded[:heads], loaded[heads:]

    first = [
        call(
            functools.partial(grads_one, n, h, divisor),
            grad_out,
            [VMEM] * (4 + n),
            (VMEM,) * 6,
            grad_scratch,
        )(decays, *kvq[0][h][:2], m_own[h], owned[h], *recv_fast[h])
        for h in range(heads)
    ]

    packs, moments = [], []
    for h in range(heads):
        gu, down, send_gu, send_down, own_gu, own_down = first[h]
        recv_gu, recv_down = turned(send_gu), turned(send_down)
        pack, moment = [], []
        for mats, old, own, recvs in (
            ((0, 1), gu, own_gu, recv_gu), ((2,), down, own_down, recv_down)
        ):
            new, *moment = call(
                functools.partial(update_one, n, h, mats),
                (shape(len(mats) * width, width), shape((mats[-1] + 1) * width, width)),
                [VMEM] * (2 + n + len(moment)),
                (VMEM, VMEM),
            )(rates, old, own, *recvs, *moment)
            pack.append(new)
        packs.append(pack)
        moments.append(forward(moment[0]))

    begins = []
    for p in range(3 * heads):
        begins.append(
            [
                lax.ppermute(
                    x, ("block", "tok"), [(sources[p] * n + i, i) for i in range(n)]
                )
                for x in crossed
            ]
        )

    second = []
    for h in range(heads):
        arrived = [forward(packs[h][0]), forward(packs[h][1])]
        pieces = [begins[3 * h + m][r] for r in range(n - 1) for m in range(3)]
        cuttable = n == 2 and width % 128 == 0 and part <= width - 128
        cuts = [width - 128, 128] if cuttable and h == heads - 1 else [width]
        second.append(
            call(
                functools.partial(grads_two, n, divisor),
                (
                    shape(2 * width, width),
                    shape(width, width),
                    shape(2 * width, width, dtype=F32),
                    shape(width, width, dtype=F32),
                    shape(2 * width, width),
                )
                + tuple(shape(size, width) for size in cuts),
                [VMEM] * (5 + 3 * (n - 1)),
                (VMEM,) * (5 + len(cuts)),
                grad_scratch,
            )(*kvq[1][h][:2], begin_own[h], *arrived, *pieces)
        )

    out_shape = jax.ShapeDtypeStruct(keys.shape, BF16)
    outputs = None
    for h in range(heads):
        prior = [] if outputs is None else [outputs]
        outputs = call(
            functools.partial(apply_one, h),
            out_shape,
            [VMEM] * 3 + [HBM] * len(prior),
            HBM,
            (row_scratch, DMA((chunks,))),
            aliases={3: 0} if prior else None,
        )(kvq[0][h][2], *packs[h], *prior)

    fast_shape = jax.ShapeDtypeStruct(fast_t.shape, BF16)
    moment_shape = jax.ShapeDtypeStruct(moment_t.shape, F32)
    ends = []
    for h in range(heads):
        gu, down, own_gu, own_down, send_gu, *sends = second[h]
        recv_gu = turned(send_gu)
        recv_down = [turned(x) for x in sends]
        at = 5 + n
        hq, *ends = call(
            functools.partial(update_two_gu, n, h),
            (shape(rows, width), fast_shape, moment_shape),
            [VMEM] * (5 + n) + [HBM] * len(ends),
            (VMEM, HBM, HBM),
            (
                pltpu.VMEM((2 * width, width), BF16),
                pltpu.VMEM((width, width), F32),
                pltpu.VMEM((2, part, width), BF16),
                pltpu.VMEM((2, part, width), F32),
                DMA((2, 2)),
            ),
            aliases={at: 1, at + 1: 2} if ends else None,
        )(rates, decays, gu, own_gu, moments[h], kvq[1][h][2], *recv_gu, *ends)
        for i, recvs in enumerate(recv_down):
            size = recvs[0].shape[0]
            outs = (out_shape, fast_shape, moment_shape)[: 1 if i else 3]
            extra = [outputs, *ends][: len(outs)]
            scratch = (
                pltpu.VMEM((size, width), BF16),
                pltpu.VMEM((rows, size), BF16),
                DMA((chunks,)),
            )
            if not i:
                scratch += (
                    pltpu.VMEM((size, width), F32),
                    pltpu.VMEM((part, width), BF16),
                    pltpu.VMEM((part, width), F32),
                    DMA((2,)),
                )
            outputs, *rest = call(
                functools.partial(update_two_down, n, h, i if len(recv_down) > 1 else None),
                outs,
                [VMEM] * (5 + n) + [HBM] * len(extra),
                (HBM,) * len(outs),
                scratch,
                aliases={at + j: j for j in range(len(outs))},
            )(rates, decays, down, own_down, moments[h], hq, *recvs, *extra)
            ends = rest or ends
    return (outputs, jnp.swapaxes(ends[0], 3, 4), jnp.swapaxes(ends[1], 3, 4))


def solution(mesh):
    placed = (
        P(None, ("block", "tok"), None),
        P(None, ("block", "tok"), None),
        P(None, ("block", "tok"), None),
        P("block", None, None, None, "tok"),
        P("block", None, None, None, "tok"),
        P(None, None, None, "tok"),
        P(),
        P(),
    )
    step = jax.shard_map(
        on_device,
        mesh=mesh,
        in_specs=placed,
        out_specs=(
            P(None, ("block", "tok"), None),
            P("block", None, None, None, "tok"),
            P("block", None, None, None, "tok"),
        ),
        check_vma=False,
    )

    def run(*args):
        with jax.sharding.use_abstract_mesh(mesh.abstract_mesh):
            return step(*args)

    return run
```

```python
import functools
import math

import jax
import jax.numpy as jnp
from jax import lax
from jax.experimental import pallas as pl
from jax.experimental.pallas import tpu as pltpu
from jax.sharding import PartitionSpec as P


F32 = jnp.float32
BF16 = jnp.bfloat16
VMEM = pl.BlockSpec(memory_space=pltpu.VMEM)
HBM = pl.BlockSpec(memory_space=pltpu.HBM)
DMA = pltpu.SemaphoreType.DMA


def mm(a, b, dims):
    return lax.dot_general(a, b, (dims, ((), ())), preferred_element_type=F32)


def call(kernel, out, in_specs, out_specs, scratch=(), aliases=None):
    return pl.pallas_call(
        kernel,
        out_shape=out,
        in_specs=in_specs,
        out_specs=out_specs,
        scratch_shapes=list(scratch),
        input_output_aliases=aliases or {},
        compiler_params=pltpu.CompilerParams(vmem_limit_bytes=12 << 20),
    )


def row_chunks(rows):
    for size in (256, 384, 128):
        if rows % size == 0:
            return [pl.ds(first, size) for first in range(0, rows, size)]
    return [pl.ds(0, rows)]


def assemble(me, shards, gu_ref, down_ref):
    n = len(shards)
    width = down_ref.shape[0]
    part = width // n
    for r, shard in enumerate(shards):
        at = pl.multiple_of(lax.rem(me - r + n, n) * part, part)
        gu_ref[pl.ds(at, part), :] = shard(0)
        gu_ref[pl.ds(width + at, part), :] = shard(1)
        down_ref[pl.ds(at, part), :] = shard(2)


def grads_core(divisor, k_ref, v_ref, gu_ref, down_ref, own_gu, own_down, hid_s, dout_s, dgu_s):
    rows, width = k_ref.shape
    for at in row_chunks(rows):
        both = mm(k_ref[at, :], gu_ref[...], ((1,), (1,)))
        gate, upper = both[:, :width], both[:, width:]
        dout = (-v_ref[at, :].astype(F32) / divisor).astype(BF16)
        dhid = mm(dout, down_ref[...], ((1,), (0,)))
        sigma = jax.nn.sigmoid(gate)
        silu = gate * sigma
        hid_s[at, :] = (silu * upper).astype(BF16)
        dout_s[at, :] = dout
        dgu_s[at, :width] = (dhid * upper * sigma * (1.0 + gate * (1.0 - sigma))).astype(BF16)
        dgu_s[at, width:] = (dhid * silu).astype(BF16)
    own_gu[...] = mm(dgu_s[...], k_ref[...], ((0,), (0,)))
    own_down[...] = mm(dout_s[...], hid_s[...], ((0,), (0,)))


def take_head(head, fast_ref, own_ref):
    pltpu.sync_copy(fast_ref.at[0, :, head], own_ref)


def take_piece(sources, begin_ref, piece_ref):
    block = lax.axis_index("block")
    piece = jnp.int32(0)
    for p, source in enumerate(sources):
        piece = jnp.where(block == source, jnp.int32(p), piece)
    pltpu.sync_copy(begin_ref.at[lax.rem(piece, 3), piece // 3], piece_ref)


def load_all(steps, heads, k_ref, v_ref, q_ref, m_ref, begin_ref, *refs):
    sems = refs[-1]
    copies = []

    def add(source, target):
        copies.append(pltpu.make_async_copy(source, target, sems.at[len(copies)]))
        copies[-1].start()

    targets = list(refs[:-1])
    for step in range(steps):
        for head in range(heads):
            for ref in (k_ref, v_ref, q_ref):
                target = targets.pop(0)
                width = target.shape[1]
                add(ref.at[step, :, pl.ds(head * width, width)], target)
    for head in range(heads):
        add(m_ref.at[0, :, head], targets.pop(0))
    for head in range(heads):
        add(begin_ref.at[:, head], targets.pop(0))
    for copy in copies:
        copy.wait()


def grads_one(n, head, divisor, decay_ref, k_ref, v_ref, m_ref, *refs):
    shards = refs[:n]
    gu_ref, down_ref, send_gu, send_down, own_gu, own_down, hid_s, dout_s, dgu_s = refs[n:]
    width = down_ref.shape[0]
    part = width // n
    me = lax.axis_index("tok")
    assemble(me, [lambda m, ref=ref: ref[m] for ref in shards], gu_ref, down_ref)
    grads_core(divisor, k_ref, v_ref, gu_ref, down_ref, own_gu, own_down, hid_s, dout_s, dgu_s)
    decay = decay_ref[:, head : head + 1]
    mine = pl.multiple_of(me * part, part)
    own_gu[pl.ds(mine, part), :] += decay * m_ref[0]
    own_gu[pl.ds(width + mine, part), :] += decay * m_ref[1]
    own_down[pl.ds(mine, part), :] += decay * m_ref[2]
    send_gu[...] = own_gu[...].astype(BF16)
    send_down[...] = own_down[...].astype(BF16)


def grads_two(n, divisor, k_ref, v_ref, begin_ref, *refs):
    (pgu_ref, pdown_ref), pieces = refs[:2], refs[2 : 2 + 3 * (n - 1)]
    gu_ref, down_ref, own_gu, own_down, send_gu, *sends = refs[2 + 3 * (n - 1) : -3]
    hid_s, dout_s, dgu_s = refs[-3:]
    leading = lax.axis_index("block") == 0

    @pl.when(leading)
    def _():
        shards = [lambda m: begin_ref[m]]
        for r in range(n - 1):
            shards.append(lambda m, r=r: pieces[3 * r + m][...])
        assemble(lax.axis_index("tok"), shards, gu_ref, down_ref)

    @pl.when(jnp.logical_not(leading))
    def _():
        gu_ref[...] = pgu_ref[...]
        down_ref[...] = pdown_ref[...]

    grads_core(divisor, k_ref, v_ref, gu_ref, down_ref, own_gu, own_down, hid_s, dout_s, dgu_s)
    send_gu[...] = own_gu[...].astype(BF16)
    if len(sends) == 1:
        sends[0][...] = own_down[...].astype(BF16)
    else:
        partner = 1 - lax.axis_index("tok")
        for send, (first, size) in zip(sends, cut_rows(down_ref.shape[0], partner)):
            send[...] = own_down[pl.ds(first, size), :].astype(BF16)


def cut_rows(width, tok):
    return (
        (pl.multiple_of(tok * 128, 128), width - 128),
        (pl.multiple_of((1 - tok) * (width - 128), 128), 128),
    )


def updated(rate, old_ref, at, moment):
    old = old_ref[at, :].astype(F32)
    moved = old - rate * moment
    old_norm = jnp.sqrt(jnp.mean(old * old, axis=1, keepdims=True) + 1e-06)
    new_norm = jnp.sqrt(jnp.mean(moved * moved, axis=1, keepdims=True) + 1e-06)
    return (moved * (old_norm / new_norm)).astype(BF16)


def summed(own_ref, recvs, first, size, recv_first):
    total = own_ref[pl.ds(first, size), :]
    for recv in recvs:
        total = total + recv[pl.ds(recv_first, size), :].astype(F32)
    return total


def update_one(n, head, mats, rate_ref, old_ref, own_ref, *refs):
    recvs = refs[: n - 1]
    new_ref, moment_ref = refs[-2:]
    width = own_ref.shape[1]
    if mats[0]:
        before = refs[n - 1]
        moment_ref[: mats[0] * width, :] = before[...]
    for i, m in enumerate(mats):
        at = pl.ds(i * width, width)
        moment = summed(own_ref, recvs, i * width, width, i * width)
        new_ref[at, :] = updated(rate_ref[head : head + 1, m : m + 1], old_ref, at, moment)
        moment_ref[m * width : (m + 1) * width, :] = moment.astype(BF16)


def store_mine(m, head, mine, new_s, moment_s, fast_s, mine_s, fast_ref, moment_ref, sems):
    part = fast_s.shape[0]
    fast_s[...] = new_s[pl.ds(mine, part), :]
    mine_s[...] = moment_s[pl.ds(mine, part), :]
    stores = [
        pltpu.make_async_copy(fast_s, fast_ref.at[0, m, head], sems.at[0]),
        pltpu.make_async_copy(mine_s, moment_ref.at[0, m, head], sems.at[1]),
    ]
    for store in stores:
        store.start()
    return stores


def update_two_gu(n, head, rate_ref, decay_ref, old_ref, own_ref, earlier_ref, q_ref, *refs):
    recvs = refs[: n - 1]
    hq_ref, fast_ref, moment_ref, gu_s, moment_s, fast_s, mine_s, sems = refs[-8:]
    width = own_ref.shape[1]
    part = width // n
    mine = pl.multiple_of(lax.axis_index("tok") * part, part)
    stores = []
    for m in range(2):
        at = pl.ds(m * width, width)
        moment = decay_ref[:, head : head + 1] * earlier_ref[at, :].astype(F32)
        moment = moment + summed(own_ref, recvs, m * width, width, m * width)
        new_s = gu_s.at[at, :]
        new_s[...] = updated(rate_ref[head : head + 1, m : m + 1], old_ref, at, moment)
        moment_s[...] = moment
        stores += store_mine(
            m,
            head,
            mine,
            new_s,
            moment_s,
            fast_s.at[m],
            mine_s.at[m],
            fast_ref,
            moment_ref,
            sems.at[m],
        )
    for at in row_chunks(q_ref.shape[0]):
        both = mm(q_ref[at, :], gu_s[...], ((1,), (1,)))
        hq_ref[at, :] = (jax.nn.silu(both[:, :width]) * both[:, width:]).astype(BF16)
    for store in stores:
        store.wait()


def update_two_down(n, head, cut, rate_ref, decay_ref, old_ref, own_ref, earlier_ref, hq_ref, *refs):
    recvs, refs = refs[: n - 1], refs[n - 1 :]
    width = old_ref.shape[1]
    part = width // n
    me = lax.axis_index("tok")
    parts = [(0, width)] if cut is None else cut_rows(width, me)
    first, size = parts[cut or 0]
    at = pl.ds(first, size)
    chunks = row_chunks(hq_ref.shape[0])

    def columns(which):
        first, size = parts[which]
        return pl.ds(pl.multiple_of(head * width + first, 128), size)

    if cut == 0:
        out_s, fast_s, mine_s, new_s, kept_s = refs
    elif cut == 1:
        before = refs[:3]
        out_ref, fast_ref, moment_ref, new_s, out_s, out_sems, sems = refs[-7:]
        stores = [
            pltpu.make_async_copy(before[0], out_ref.at[1, :, columns(0)], sems.at[0]),
            pltpu.make_async_copy(before[1], fast_ref.at[0, 2, head], sems.at[1]),
            pltpu.make_async_copy(before[2], moment_ref.at[0, 2, head], sems.at[2]),
        ]
        for store in stores:
            store.start()
    else:
        out_ref, fast_ref, moment_ref, new_s, out_s, out_sems, kept_s, fast_s, mine_s, sems = refs[-10:]
    moment = decay_ref[:, head : head + 1] * earlier_ref[pl.ds(2 * width + first, size), :].astype(F32)
    moment = moment + summed(own_ref, recvs, first, size, 0)
    new_s[...] = updated(rate_ref[head : head + 1, 2:], old_ref, at, moment)
    if cut != 1:
        kept_s[...] = moment
        mine = pl.ds(pl.multiple_of(me * part - first, math.gcd(part, 128)), part)
        fast_s[...] = new_s[mine, :]
        mine_s[...] = kept_s[mine, :]
    if cut is None:
        stores = [
            pltpu.make_async_copy(fast_s, fast_ref.at[0, 2, head], sems.at[0]),
            pltpu.make_async_copy(mine_s, moment_ref.at[0, 2, head], sems.at[1]),
        ]
        for store in stores:
            store.start()
    for i, rows in enumerate(chunks):
        out_s[rows, :] = mm(hq_ref[rows, :], new_s[...], ((1,), (1,))).astype(BF16)
        if cut != 0:
            stores.append(
                pltpu.make_async_copy(
                    out_s.at[rows, :], out_ref.at[1, rows, columns(cut or 0)], out_sems.at[i]
                )
            )
            stores[-1].start()
    if cut != 0:
        for store in stores:
            store.wait()


def apply_one(head, q_ref, pgu_ref, pdown_ref, *refs):
    out_ref, out_s, sems = refs[-3:]
    rows, width = q_ref.shape
    stores = []
    for i, at in enumerate(row_chunks(rows)):
        both = mm(q_ref[at, :], pgu_ref[...], ((1,), (1,)))
        hq = (jax.nn.silu(both[:, :width]) * both[:, width:]).astype(BF16)
        out_s[at, :] = mm(hq, pdown_ref[...], ((1,), (1,))).astype(BF16)
        stores.append(
            pltpu.make_async_copy(
                out_s.at[at, :], out_ref.at[0, at, pl.ds(head * width, width)], sems.at[i]
            )
        )
        stores[-1].start()
    for store in stores:
        store.wait()


def on_device(keys, values, queries, fast_in, moment_in, initial_fast, rates, decays):
    n = lax.axis_size("tok")
    blocks = lax.axis_size("block")
    steps, rows, features = keys.shape
    heads = rates.shape[1]
    width = features // heads
    part = width // n
    chunks = len(row_chunks(rows))
    divisor = float(rows * n)
    fast_t = jnp.swapaxes(fast_in, 3, 4)
    moment_t = jnp.swapaxes(moment_in, 3, 4)
    begin_t = jnp.swapaxes(initial_fast, 2, 3)
    rates = rates.T
    decays = decays.reshape(1, heads)
    keys, values, queries, fast_t, moment_t, begin_t = (
        pltpu.with_memory_space_constraint(x, pltpu.HBM)
        for x in (keys, values, queries, fast_t, moment_t, begin_t)
    )

    def turned(x):
        return [lax.ppermute(x, "tok", [(i, (i + r) % n) for i in range(n)]) for r in range(1, n)]

    def forward(x):
        return lax.ppermute(x, "block", [(i, i + 1) for i in range(blocks - 1)])

    def shape(*dims, dtype=BF16):
        return jax.ShapeDtypeStruct(dims, dtype)

    row_scratch = pltpu.VMEM((rows, width), BF16)
    grad_scratch = (row_scratch, row_scratch, pltpu.VMEM((rows, 2 * width), BF16))
    grad_out = (
        shape(2 * width, width),
        shape(width, width),
        shape(2 * width, width),
        shape(width, width),
        shape(2 * width, width, dtype=F32),
        shape(width, width, dtype=F32),
    )

    recv_fast, owned = [], []
    for h in range(heads):
        owned.append(
            call(functools.partial(take_head, h), shape(3, part, width), [HBM], VMEM)(fast_t)
        )
        recv_fast.append(turned(owned[h]))

    apart = max(blocks // (3 * heads + 2), 1)
    sources = [apart * (p + 1) % blocks for p in range(3 * heads)]
    piece = call(functools.partial(take_piece, sources), shape(part, width), [HBM], VMEM)(begin_t)
    crossed = [
        lax.ppermute(
            piece,
            ("block", "tok"),
            [(s * n + i, s * n + (i + r) % n) for s in sorted(set(sources)) for i in range(n)],
        )
        for r in range(1, n)
    ]

    loaded = list(
        call(
            functools.partial(load_all, steps, heads),
            (shape(rows, width),) * (3 * steps * heads)
            + (shape(3, part, width, dtype=F32),) * heads
            + (shape(3, part, width),) * heads,
            [HBM] * 5,
            (VMEM,) * (3 * steps * heads + 2 * heads),
            (DMA((3 * steps * heads + 2 * heads,)),),
        )(keys, values, queries, moment_t, begin_t)
    )
    kvq = [[[loaded.pop(0) for _ in range(3)] for _ in range(heads)] for _ in range(steps)]
    m_own, begin_own = loaded[:heads], loaded[heads:]

    first = [
        call(
            functools.partial(grads_one, n, h, divisor),
            grad_out,
            [VMEM] * (4 + n),
            (VMEM,) * 6,
            grad_scratch,
        )(decays, *kvq[0][h][:2], m_own[h], owned[h], *recv_fast[h])
        for h in range(heads)
    ]

    packs, moments = [], []
    for h in range(heads):
        gu, down, send_gu, send_down, own_gu, own_down = first[h]
        recv_gu, recv_down = turned(send_gu), turned(send_down)
        pack, moment = [], []
        for mats, old, own, recvs in (
            ((0, 1), gu, own_gu, recv_gu), ((2,), down, own_down, recv_down)
        ):
            new, *moment = call(
                functools.partial(update_one, n, h, mats),
                (shape(len(mats) * width, width), shape((mats[-1] + 1) * width, width)),
                [VMEM] * (2 + n + len(moment)),
                (VMEM, VMEM),
            )(rates, old, own, *recvs, *moment)
            pack.append(new)
        packs.append(pack)
        moments.append(forward(moment[0]))

    begins = []
    for p in range(3 * heads):
        begins.append(
            [
                lax.ppermute(
                    x, ("block", "tok"), [(sources[p] * n + i, i) for i in range(n)]
                )
                for x in crossed
            ]
        )

    second = []
    for h in range(heads):
        arrived = [forward(packs[h][0]), forward(packs[h][1])]
        pieces = [begins[3 * h + m][r] for r in range(n - 1) for m in range(3)]
        cuttable = n == 2 and width % 128 == 0 and part <= width - 128
        cuts = [width - 128, 128] if cuttable and h == heads - 1 else [width]
        second.append(
            call(
                functools.partial(grads_two, n, divisor),
                (
                    shape(2 * width, width),
                    shape(width, width),
                    shape(2 * width, width, dtype=F32),
                    shape(width, width, dtype=F32),
                    shape(2 * width, width),
                )
                + tuple(shape(size, width) for size in cuts),
                [VMEM] * (5 + 3 * (n - 1)),
                (VMEM,) * (5 + len(cuts)),
                grad_scratch,
            )(*kvq[1][h][:2], begin_own[h], *arrived, *pieces)
        )

    out_shape = jax.ShapeDtypeStruct(keys.shape, BF16)
    outputs = None
    for h in range(heads):
        prior = [] if outputs is None else [outputs]
        outputs = call(
            functools.partial(apply_one, h),
            out_shape,
            [VMEM] * 3 + [HBM] * len(prior),
            HBM,
            (row_scratch, DMA((chunks,))),
            aliases={3: 0} if prior else None,
        )(kvq[0][h][2], *packs[h], *prior)

    fast_shape = jax.ShapeDtypeStruct(fast_t.shape, BF16)
    moment_shape = jax.ShapeDtypeStruct(moment_t.shape, F32)
    ends = []
    for h in range(heads):
        gu, down, own_gu, own_down, send_gu, *sends = second[h]
        recv_gu = turned(send_gu)
        recv_down = [turned(x) for x in sends]
        at = 5 + n
        hq, *ends = call(
            functools.partial(update_two_gu, n, h),
            (shape(rows, width), fast_shape, moment_shape),
            [VMEM] * (5 + n) + [HBM] * len(ends),
            (VMEM, HBM, HBM),
            (
                pltpu.VMEM((2 * width, width), BF16),
                pltpu.VMEM((width, width), F32),
                pltpu.VMEM((2, part, width), BF16),
                pltpu.VMEM((2, part, width), F32),
                DMA((2, 2)),
            ),
            aliases={at: 1, at + 1: 2} if ends else None,
        )(rates, decays, gu, own_gu, moments[h], kvq[1][h][2], *recv_gu, *ends)
        before = []
        for i, recvs in enumerate(recv_down):
            cut = i if len(recv_down) > 1 else None
            size = recvs[0].shape[0]
            new = pltpu.VMEM((size, width), BF16)
            kept = pltpu.VMEM((size, width), F32)
            if cut == 0:
                outs = (shape(rows, size), shape(part, width), shape(part, width, dtype=F32))
                extra, scratch, space = [], (new, kept), VMEM
            else:
                outs = (out_shape, fast_shape, moment_shape)
                extra, space = [outputs, *ends], HBM
                scratch = (new, pltpu.VMEM((rows, size), BF16), DMA((chunks,)))
                if cut is None:
                    scratch += (kept, pltpu.VMEM((part, width), BF16))
                    scratch += (pltpu.VMEM((part, width), F32), DMA((2,)))
                else:
                    scratch += (DMA((3,)),)
            results = call(
                functools.partial(update_two_down, n, h, cut),
                outs,
                [VMEM] * (5 + n + len(before)) + [HBM] * len(extra),
                (space,) * 3,
                scratch,
                aliases={at + len(before) + j: j for j in range(len(extra))},
            )(rates, decays, down, own_down, moments[h], hq, *recvs, *before, *extra)
            if cut == 0:
                before = results
            else:
                outputs, *ends = results
    return (outputs, jnp.swapaxes(ends[0], 3, 4), jnp.swapaxes(ends[1], 3, 4))


def solution(mesh):
    placed = (
        P(None, ("block", "tok"), None),
        P(None, ("block", "tok"), None),
        P(None, ("block", "tok"), None),
        P("block", None, None, None, "tok"),
        P("block", None, None, None, "tok"),
        P(None, None, None, "tok"),
        P(),
        P(),
    )
    step = jax.shard_map(
        on_device,
        mesh=mesh,
        in_specs=placed,
        out_specs=(
            P(None, ("block", "tok"), None),
            P("block", None, None, None, "tok"),
            P("block", None, None, None, "tok"),
        ),
        check_vma=False,
    )

    def run(*args):
        with jax.sharding.use_abstract_mesh(mesh.abstract_mesh):
            return step(*args)

    return run
```

```python
import functools
import math

import jax
import jax.numpy as jnp
from jax import lax
from jax.experimental import pallas as pl
from jax.experimental.pallas import tpu as pltpu
from jax.sharding import PartitionSpec as P


F32 = jnp.float32
BF16 = jnp.bfloat16
VMEM = pl.BlockSpec(memory_space=pltpu.VMEM)
HBM = pl.BlockSpec(memory_space=pltpu.HBM)
DMA = pltpu.SemaphoreType.DMA


def mm(a, b, dims):
    return lax.dot_general(a, b, (dims, ((), ())), preferred_element_type=F32)


def call(kernel, out, in_specs, out_specs, scratch=(), aliases=None):
    return pl.pallas_call(
        kernel,
        out_shape=out,
        in_specs=in_specs,
        out_specs=out_specs,
        scratch_shapes=list(scratch),
        input_output_aliases=aliases or {},
        compiler_params=pltpu.CompilerParams(vmem_limit_bytes=12 << 20),
    )


def row_chunks(rows):
    for size in (256, 384, 128):
        if rows % size == 0:
            return [pl.ds(first, size) for first in range(0, rows, size)]
    return [pl.ds(0, rows)]


def assemble(me, shards, gu_ref, down_ref):
    n = len(shards)
    width = down_ref.shape[0]
    part = width // n
    for r, shard in enumerate(shards):
        at = pl.multiple_of(lax.rem(me - r + n, n) * part, part)
        gu_ref[pl.ds(at, part), :] = shard(0)
        gu_ref[pl.ds(width + at, part), :] = shard(1)
        down_ref[pl.ds(at, part), :] = shard(2)


def grads_core(divisor, k_ref, v_ref, gu_ref, down_ref, own_gu, own_down, hid_s, dout_s, dgu_s):
    rows, width = k_ref.shape
    for at in row_chunks(rows):
        both = mm(k_ref[at, :], gu_ref[...], ((1,), (1,)))
        gate, upper = both[:, :width], both[:, width:]
        dout = (-v_ref[at, :].astype(F32) / divisor).astype(BF16)
        dhid = mm(dout, down_ref[...], ((1,), (0,)))
        sigma = jax.nn.sigmoid(gate)
        silu = gate * sigma
        hid_s[at, :] = (silu * upper).astype(BF16)
        dout_s[at, :] = dout
        dgu_s[at, :width] = (dhid * upper * sigma * (1.0 + gate * (1.0 - sigma))).astype(BF16)
        dgu_s[at, width:] = (dhid * silu).astype(BF16)
    own_gu[...] = mm(dgu_s[...], k_ref[...], ((0,), (0,)))
    own_down[...] = mm(dout_s[...], hid_s[...], ((0,), (0,)))


def take_head(head, first, fast_ref, own_ref):
    pltpu.sync_copy(fast_ref.at[0, pl.ds(first, own_ref.shape[0]), head], own_ref)


def take_piece(sources, begin_ref, piece_ref):
    block = lax.axis_index("block")
    piece = jnp.int32(0)
    for p, source in enumerate(sources):
        piece = jnp.where(block == source, jnp.int32(p), piece)
    pltpu.sync_copy(begin_ref.at[lax.rem(piece, 3), piece // 3], piece_ref)


def load_all(steps, heads, k_ref, v_ref, q_ref, m_ref, begin_ref, *refs):
    sems = refs[-1]
    copies = []

    def add(source, target):
        copies.append(pltpu.make_async_copy(source, target, sems.at[len(copies)]))
        copies[-1].start()

    targets = list(refs[:-1])
    for step in range(steps):
        for head in range(heads):
            for ref in (k_ref, v_ref, q_ref):
                target = targets.pop(0)
                width = target.shape[1]
                add(ref.at[step, :, pl.ds(head * width, width)], target)
    for head in range(heads):
        add(m_ref.at[0, :, head], targets.pop(0))
    for head in range(heads):
        add(begin_ref.at[:, head], targets.pop(0))
    for copy in copies:
        copy.wait()


def grads_one(n, head, groups, divisor, decay_ref, k_ref, v_ref, m_ref, *refs):
    count = len(groups)
    shards, refs = refs[: n * count], refs[n * count :]

    def block(r, m):
        for ref, (first, end) in zip(shards[r * count :], groups):
            if first <= m < end:
                return ref[m - first]

    gu_ref, down_ref, send_gu, send_down, own_gu, own_down, hid_s, dout_s, dgu_s = refs
    width = down_ref.shape[0]
    part = width // n
    me = lax.axis_index("tok")
    assemble(me, [functools.partial(block, r) for r in range(n)], gu_ref, down_ref)
    grads_core(divisor, k_ref, v_ref, gu_ref, down_ref, own_gu, own_down, hid_s, dout_s, dgu_s)
    decay = decay_ref[:, head : head + 1]
    mine = pl.multiple_of(me * part, part)
    own_gu[pl.ds(mine, part), :] += decay * m_ref[0]
    own_gu[pl.ds(width + mine, part), :] += decay * m_ref[1]
    own_down[pl.ds(mine, part), :] += decay * m_ref[2]
    send_gu[...] = own_gu[...].astype(BF16)
    send_down[...] = own_down[...].astype(BF16)


def grads_two(n, divisor, k_ref, v_ref, begin_ref, *refs):
    (pgu_ref, pdown_ref), pieces = refs[:2], refs[2 : 2 + 3 * (n - 1)]
    gu_ref, down_ref, own_gu, own_down, send_gu, *sends = refs[2 + 3 * (n - 1) : -3]
    hid_s, dout_s, dgu_s = refs[-3:]
    leading = lax.axis_index("block") == 0

    @pl.when(leading)
    def _():
        shards = [lambda m: begin_ref[m]]
        for r in range(n - 1):
            shards.append(lambda m, r=r: pieces[3 * r + m][...])
        assemble(lax.axis_index("tok"), shards, gu_ref, down_ref)

    @pl.when(jnp.logical_not(leading))
    def _():
        gu_ref[...] = pgu_ref[...]
        down_ref[...] = pdown_ref[...]

    grads_core(divisor, k_ref, v_ref, gu_ref, down_ref, own_gu, own_down, hid_s, dout_s, dgu_s)
    send_gu[...] = own_gu[...].astype(BF16)
    if len(sends) == 1:
        sends[0][...] = own_down[...].astype(BF16)
    else:
        partner = 1 - lax.axis_index("tok")
        for send, (first, size) in zip(sends, cut_rows(down_ref.shape[0], partner)):
            send[...] = own_down[pl.ds(first, size), :].astype(BF16)


def cut_rows(width, tok):
    return (
        (pl.multiple_of(tok * 128, 128), width - 128),
        (pl.multiple_of((1 - tok) * (width - 128), 128), 128),
    )


def updated(rate, old_ref, at, moment):
    old = old_ref[at, :].astype(F32)
    moved = old - rate * moment
    old_norm = jnp.sqrt(jnp.mean(old * old, axis=1, keepdims=True) + 1e-06)
    new_norm = jnp.sqrt(jnp.mean(moved * moved, axis=1, keepdims=True) + 1e-06)
    return (moved * (old_norm / new_norm)).astype(BF16)


def summed(own_ref, recvs, first, size, recv_first):
    total = own_ref[pl.ds(first, size), :]
    for recv in recvs:
        total = total + recv[pl.ds(recv_first, size), :].astype(F32)
    return total


def update_one(n, head, mats, rate_ref, old_ref, own_ref, *refs):
    recvs = refs[: n - 1]
    new_ref, moment_ref = refs[-2:]
    width = own_ref.shape[1]
    if mats[0]:
        before = refs[n - 1]
        moment_ref[: mats[0] * width, :] = before[...]
    for i, m in enumerate(mats):
        at = pl.ds(i * width, width)
        moment = summed(own_ref, recvs, i * width, width, i * width)
        new_ref[at, :] = updated(rate_ref[head : head + 1, m : m + 1], old_ref, at, moment)
        moment_ref[m * width : (m + 1) * width, :] = moment.astype(BF16)


def store_mine(m, head, mine, new_s, moment_s, fast_s, mine_s, fast_ref, moment_ref, sems):
    part = fast_s.shape[0]
    fast_s[...] = new_s[pl.ds(mine, part), :]
    mine_s[...] = moment_s[pl.ds(mine, part), :]
    stores = [
        pltpu.make_async_copy(fast_s, fast_ref.at[0, m, head], sems.at[0]),
        pltpu.make_async_copy(mine_s, moment_ref.at[0, m, head], sems.at[1]),
    ]
    for store in stores:
        store.start()
    return stores


def update_two_gu(n, head, rate_ref, decay_ref, old_ref, own_ref, earlier_ref, q_ref, *refs):
    recvs = refs[: n - 1]
    hq_ref, fast_ref, moment_ref, gu_s, moment_s, fast_s, mine_s, sems = refs[-8:]
    width = own_ref.shape[1]
    part = width // n
    mine = pl.multiple_of(lax.axis_index("tok") * part, part)
    stores = []
    for m in range(2):
        at = pl.ds(m * width, width)
        moment = decay_ref[:, head : head + 1] * earlier_ref[at, :].astype(F32)
        moment = moment + summed(own_ref, recvs, m * width, width, m * width)
        new_s = gu_s.at[at, :]
        new_s[...] = updated(rate_ref[head : head + 1, m : m + 1], old_ref, at, moment)
        moment_s[...] = moment
        stores += store_mine(
            m,
            head,
            mine,
            new_s,
            moment_s,
            fast_s.at[m],
            mine_s.at[m],
            fast_ref,
            moment_ref,
            sems.at[m],
        )
    for at in row_chunks(q_ref.shape[0]):
        both = mm(q_ref[at, :], gu_s[...], ((1,), (1,)))
        hq_ref[at, :] = (jax.nn.silu(both[:, :width]) * both[:, width:]).astype(BF16)
    for store in stores:
        store.wait()


def update_two_down(n, head, cut, rate_ref, decay_ref, old_ref, own_ref, earlier_ref, hq_ref, *refs):
    recvs, refs = refs[: n - 1], refs[n - 1 :]
    width = old_ref.shape[1]
    part = width // n
    me = lax.axis_index("tok")
    parts = [(0, width)] if cut is None else cut_rows(width, me)
    first, size = parts[cut or 0]
    at = pl.ds(first, size)
    chunks = row_chunks(hq_ref.shape[0])

    def columns(which):
        first, size = parts[which]
        return pl.ds(pl.multiple_of(head * width + first, 128), size)

    if cut == 0:
        out_s, fast_s, mine_s, new_s, kept_s = refs
    elif cut == 1:
        before = refs[:3]
        out_ref, fast_ref, moment_ref, new_s, out_s, out_sems, sems = refs[-7:]
        stores = [
            pltpu.make_async_copy(before[0], out_ref.at[1, :, columns(0)], sems.at[0]),
            pltpu.make_async_copy(before[1], fast_ref.at[0, 2, head], sems.at[1]),
            pltpu.make_async_copy(before[2], moment_ref.at[0, 2, head], sems.at[2]),
        ]
        for store in stores:
            store.start()
    else:
        out_ref, fast_ref, moment_ref, new_s, out_s, out_sems, kept_s, fast_s, mine_s, sems = refs[-10:]
    moment = decay_ref[:, head : head + 1] * earlier_ref[pl.ds(2 * width + first, size), :].astype(F32)
    moment = moment + summed(own_ref, recvs, first, size, 0)
    new_s[...] = updated(rate_ref[head : head + 1, 2:], old_ref, at, moment)
    if cut != 1:
        kept_s[...] = moment
        mine = pl.ds(pl.multiple_of(me * part - first, math.gcd(part, 128)), part)
        fast_s[...] = new_s[mine, :]
        mine_s[...] = kept_s[mine, :]
    if cut is None:
        stores = [
            pltpu.make_async_copy(fast_s, fast_ref.at[0, 2, head], sems.at[0]),
            pltpu.make_async_copy(mine_s, moment_ref.at[0, 2, head], sems.at[1]),
        ]
        for store in stores:
            store.start()
    for i, rows in enumerate(chunks):
        out_s[rows, :] = mm(hq_ref[rows, :], new_s[...], ((1,), (1,))).astype(BF16)
        if cut != 0:
            stores.append(
                pltpu.make_async_copy(
                    out_s.at[rows, :], out_ref.at[1, rows, columns(cut or 0)], out_sems.at[i]
                )
            )
            stores[-1].start()
    if cut != 0:
        for store in stores:
            store.wait()


def apply_one(head, q_ref, pgu_ref, pdown_ref, *refs):
    out_ref, out_s, sems = refs[-3:]
    rows, width = q_ref.shape
    stores = []
    for i, at in enumerate(row_chunks(rows)):
        both = mm(q_ref[at, :], pgu_ref[...], ((1,), (1,)))
        hq = (jax.nn.silu(both[:, :width]) * both[:, width:]).astype(BF16)
        out_s[at, :] = mm(hq, pdown_ref[...], ((1,), (1,))).astype(BF16)
        stores.append(
            pltpu.make_async_copy(
                out_s.at[at, :], out_ref.at[0, at, pl.ds(head * width, width)], sems.at[i]
            )
        )
        stores[-1].start()
    for store in stores:
        store.wait()


def on_device(keys, values, queries, fast_in, moment_in, initial_fast, rates, decays):
    n = lax.axis_size("tok")
    blocks = lax.axis_size("block")
    steps, rows, features = keys.shape
    heads = rates.shape[1]
    width = features // heads
    part = width // n
    chunks = len(row_chunks(rows))
    divisor = float(rows * n)
    fast_t = jnp.swapaxes(fast_in, 3, 4)
    moment_t = jnp.swapaxes(moment_in, 3, 4)
    begin_t = jnp.swapaxes(initial_fast, 2, 3)
    rates = rates.T
    decays = decays.reshape(1, heads)
    keys, values, queries, fast_t, moment_t, begin_t = (
        pltpu.with_memory_space_constraint(x, pltpu.HBM)
        for x in (keys, values, queries, fast_t, moment_t, begin_t)
    )

    def turned(x):
        return [lax.ppermute(x, "tok", [(i, (i + r) % n) for i in range(n)]) for r in range(1, n)]

    def forward(x):
        return lax.ppermute(x, "block", [(i, i + 1) for i in range(blocks - 1)])

    def shape(*dims, dtype=BF16):
        return jax.ShapeDtypeStruct(dims, dtype)

    row_scratch = pltpu.VMEM((rows, width), BF16)
    grad_scratch = (row_scratch, row_scratch, pltpu.VMEM((rows, 2 * width), BF16))
    grad_out = (
        shape(2 * width, width),
        shape(width, width),
        shape(2 * width, width),
        shape(width, width),
        shape(2 * width, width, dtype=F32),
        shape(width, width, dtype=F32),
    )

    groups = [[(0, 1), (1, 3)] if h == 0 else [(0, 3)] for h in range(heads)]
    shards = []
    for h in range(heads):
        owned, received = [], []
        for begin, end in groups[h]:
            owned.append(
                call(
                    functools.partial(take_head, h, begin),
                    shape(end - begin, part, width),
                    [HBM],
                    VMEM,
                )(fast_t)
            )
            received.append(turned(owned[-1]))
        shards.append(owned + [group[r] for r in range(n - 1) for group in received])

    apart = max(blocks // (3 * heads + 2), 1)
    sources = [apart * (p + 1) % blocks for p in range(3 * heads)]
    piece = call(functools.partial(take_piece, sources), shape(part, width), [HBM], VMEM)(begin_t)
    crossed = [
        lax.ppermute(
            piece,
            ("block", "tok"),
            [(s * n + i, s * n + (i + r) % n) for s in sorted(set(sources)) for i in range(n)],
        )
        for r in range(1, n)
    ]

    loaded = list(
        call(
            functools.partial(load_all, steps, heads),
            (shape(rows, width),) * (3 * steps * heads)
            + (shape(3, part, width, dtype=F32),) * heads
            + (shape(3, part, width),) * heads,
            [HBM] * 5,
            (VMEM,) * (3 * steps * heads + 2 * heads),
            (DMA((3 * steps * heads + 2 * heads,)),),
        )(keys, values, queries, moment_t, begin_t)
    )
    kvq = [[[loaded.pop(0) for _ in range(3)] for _ in range(heads)] for _ in range(steps)]
    m_own, begin_own = loaded[:heads], loaded[heads:]

    first = [
        call(
            functools.partial(grads_one, n, h, groups[h], divisor),
            grad_out,
            [VMEM] * (4 + len(shards[h])),
            (VMEM,) * 6,
            grad_scratch,
        )(decays, *kvq[0][h][:2], m_own[h], *shards[h])
        for h in range(heads)
    ]

    packs, moments = [], []
    for h in range(heads):
        gu, down, send_gu, send_down, own_gu, own_down = first[h]
        recv_gu, recv_down = turned(send_gu), turned(send_down)
        pack, moment = [], []
        for mats, old, own, recvs in (
            ((0, 1), gu, own_gu, recv_gu), ((2,), down, own_down, recv_down)
        ):
            new, *moment = call(
                functools.partial(update_one, n, h, mats),
                (shape(len(mats) * width, width), shape((mats[-1] + 1) * width, width)),
                [VMEM] * (2 + n + len(moment)),
                (VMEM, VMEM),
            )(rates, old, own, *recvs, *moment)
            pack.append(new)
        packs.append(pack)
        moments.append(forward(moment[0]))

    begins = []
    for p in range(3 * heads):
        begins.append(
            [
                lax.ppermute(
                    x, ("block", "tok"), [(sources[p] * n + i, i) for i in range(n)]
                )
                for x in crossed
            ]
        )

    second = []
    for h in range(heads):
        arrived = [forward(packs[h][0]), forward(packs[h][1])]
        pieces = [begins[3 * h + m][r] for r in range(n - 1) for m in range(3)]
        cuttable = n == 2 and width % 128 == 0 and part <= width - 128
        cuts = [width - 128, 128] if cuttable and h == heads - 1 else [width]
        second.append(
            call(
                functools.partial(grads_two, n, divisor),
                (
                    shape(2 * width, width),
                    shape(width, width),
                    shape(2 * width, width, dtype=F32),
                    shape(width, width, dtype=F32),
                    shape(2 * width, width),
                )
                + tuple(shape(size, width) for size in cuts),
                [VMEM] * (5 + 3 * (n - 1)),
                (VMEM,) * (5 + len(cuts)),
                grad_scratch,
            )(*kvq[1][h][:2], begin_own[h], *arrived, *pieces)
        )

    out_shape = jax.ShapeDtypeStruct(keys.shape, BF16)
    outputs = None
    for h in range(heads):
        prior = [] if outputs is None else [outputs]
        outputs = call(
            functools.partial(apply_one, h),
            out_shape,
            [VMEM] * 3 + [HBM] * len(prior),
            HBM,
            (row_scratch, DMA((chunks,))),
            aliases={3: 0} if prior else None,
        )(kvq[0][h][2], *packs[h], *prior)

    fast_shape = jax.ShapeDtypeStruct(fast_t.shape, BF16)
    moment_shape = jax.ShapeDtypeStruct(moment_t.shape, F32)
    ends = []
    for h in range(heads):
        gu, down, own_gu, own_down, send_gu, *sends = second[h]
        recv_gu = turned(send_gu)
        recv_down = [turned(x) for x in sends]
        at = 5 + n
        hq, *ends = call(
            functools.partial(update_two_gu, n, h),
            (shape(rows, width), fast_shape, moment_shape),
            [VMEM] * (5 + n) + [HBM] * len(ends),
            (VMEM, HBM, HBM),
            (
                pltpu.VMEM((2 * width, width), BF16),
                pltpu.VMEM((width, width), F32),
                pltpu.VMEM((2, part, width), BF16),
                pltpu.VMEM((2, part, width), F32),
                DMA((2, 2)),
            ),
            aliases={at: 1, at + 1: 2} if ends else None,
        )(rates, decays, gu, own_gu, moments[h], kvq[1][h][2], *recv_gu, *ends)
        before = []
        for i, recvs in enumerate(recv_down):
            cut = i if len(recv_down) > 1 else None
            size = recvs[0].shape[0]
            new = pltpu.VMEM((size, width), BF16)
            kept = pltpu.VMEM((size, width), F32)
            if cut == 0:
                outs = (shape(rows, size), shape(part, width), shape(part, width, dtype=F32))
                extra, scratch, space = [], (new, kept), VMEM
            else:
                outs = (out_shape, fast_shape, moment_shape)
                extra, space = [outputs, *ends], HBM
                scratch = (new, pltpu.VMEM((rows, size), BF16), DMA((chunks,)))
                if cut is None:
                    scratch += (kept, pltpu.VMEM((part, width), BF16))
                    scratch += (pltpu.VMEM((part, width), F32), DMA((2,)))
                else:
                    scratch += (DMA((3,)),)
            results = call(
                functools.partial(update_two_down, n, h, cut),
                outs,
                [VMEM] * (5 + n + len(before)) + [HBM] * len(extra),
                (space,) * 3,
                scratch,
                aliases={at + len(before) + j: j for j in range(len(extra))},
            )(rates, decays, down, own_down, moments[h], hq, *recvs, *before, *extra)
            if cut == 0:
                before = results
            else:
                outputs, *ends = results
    return (outputs, jnp.swapaxes(ends[0], 3, 4), jnp.swapaxes(ends[1], 3, 4))


def solution(mesh):
    placed = (
        P(None, ("block", "tok"), None),
        P(None, ("block", "tok"), None),
        P(None, ("block", "tok"), None),
        P("block", None, None, None, "tok"),
        P("block", None, None, None, "tok"),
        P(None, None, None, "tok"),
        P(),
        P(),
    )
    step = jax.shard_map(
        on_device,
        mesh=mesh,
        in_specs=placed,
        out_specs=(
            P(None, ("block", "tok"), None),
            P("block", None, None, None, "tok"),
            P("block", None, None, None, "tok"),
        ),
        check_vma=False,
    )

    def run(*args):
        with jax.sharding.use_abstract_mesh(mesh.abstract_mesh):
            return step(*args)

    return run
```

```python
import functools
import math

import jax
import jax.numpy as jnp
from jax import lax
from jax.experimental import pallas as pl
from jax.experimental.pallas import tpu as pltpu
from jax.sharding import PartitionSpec as P


F32 = jnp.float32
BF16 = jnp.bfloat16
VMEM = pl.BlockSpec(memory_space=pltpu.VMEM)
HBM = pl.BlockSpec(memory_space=pltpu.HBM)
DMA = pltpu.SemaphoreType.DMA


def mm(a, b, dims):
    return lax.dot_general(a, b, (dims, ((), ())), preferred_element_type=F32)


def call(kernel, out, in_specs, out_specs, scratch=(), aliases=None):
    return pl.pallas_call(
        kernel,
        out_shape=out,
        in_specs=in_specs,
        out_specs=out_specs,
        scratch_shapes=list(scratch),
        input_output_aliases=aliases or {},
        compiler_params=pltpu.CompilerParams(vmem_limit_bytes=12 << 20),
    )


def row_chunks(rows):
    for size in (256, 384, 128):
        if rows % size == 0:
            return [pl.ds(first, size) for first in range(0, rows, size)]
    return [pl.ds(0, rows)]


def assemble(me, shards, gu_ref, down_ref):
    n = len(shards)
    width = down_ref.shape[0]
    part = width // n
    for r, shard in enumerate(shards):
        at = pl.multiple_of(lax.rem(me - r + n, n) * part, part)
        gu_ref[pl.ds(at, part), :] = shard(0)
        gu_ref[pl.ds(width + at, part), :] = shard(1)
        down_ref[pl.ds(at, part), :] = shard(2)


def grads_core(divisor, k_ref, v_ref, gu_ref, down_ref, own_gu, own_down, hid_s, dout_s, dgu_s):
    rows, width = k_ref.shape
    for at in row_chunks(rows):
        both = mm(k_ref[at, :], gu_ref[...], ((1,), (1,)))
        gate, upper = both[:, :width], both[:, width:]
        dout = (-v_ref[at, :].astype(F32) / divisor).astype(BF16)
        dhid = mm(dout, down_ref[...], ((1,), (0,)))
        sigma = jax.nn.sigmoid(gate)
        silu = gate * sigma
        hid_s[at, :] = (silu * upper).astype(BF16)
        dout_s[at, :] = dout
        dgu_s[at, :width] = (dhid * upper * sigma * (1.0 + gate * (1.0 - sigma))).astype(BF16)
        dgu_s[at, width:] = (dhid * silu).astype(BF16)
    own_gu[...] = mm(dgu_s[...], k_ref[...], ((0,), (0,)))
    own_down[...] = mm(dout_s[...], hid_s[...], ((0,), (0,)))


def take_head(head, first, fast_ref, own_ref):
    pltpu.sync_copy(fast_ref.at[0, pl.ds(first, own_ref.shape[0]), head], own_ref)


def take_piece(sources, begin_ref, piece_ref):
    block = lax.axis_index("block")
    piece = jnp.int32(0)
    for p, source in enumerate(sources):
        piece = jnp.where(block == source, jnp.int32(p), piece)
    pltpu.sync_copy(begin_ref.at[lax.rem(piece, 3), piece // 3], piece_ref)


def load_all(steps, heads, k_ref, v_ref, q_ref, m_ref, begin_ref, *refs):
    sems = refs[-1]
    copies = []

    def add(source, target):
        copies.append(pltpu.make_async_copy(source, target, sems.at[len(copies)]))
        copies[-1].start()

    targets = list(refs[:-1])
    for step in range(steps):
        for head in range(heads):
            for ref in (k_ref, v_ref, q_ref):
                target = targets.pop(0)
                width = target.shape[1]
                add(ref.at[step, :, pl.ds(head * width, width)], target)
    for head in range(heads):
        add(m_ref.at[0, :, head], targets.pop(0))
    for head in range(heads):
        add(begin_ref.at[:, head], targets.pop(0))
    for copy in copies:
        copy.wait()


def grads_one(n, head, groups, divisor, decay_ref, k_ref, v_ref, m_ref, *refs):
    count = len(groups)
    shards, refs = refs[: n * count], refs[n * count :]

    def block(r, m):
        for ref, (first, end) in zip(shards[r * count :], groups):
            if first <= m < end:
                return ref[m - first]

    gu_ref, down_ref, send_gu, send_down, own_gu, own_down, hid_s, dout_s, dgu_s = refs
    width = down_ref.shape[0]
    part = width // n
    me = lax.axis_index("tok")
    assemble(me, [functools.partial(block, r) for r in range(n)], gu_ref, down_ref)
    grads_core(divisor, k_ref, v_ref, gu_ref, down_ref, own_gu, own_down, hid_s, dout_s, dgu_s)
    decay = decay_ref[:, head : head + 1]
    mine = pl.multiple_of(me * part, part)
    own_gu[pl.ds(mine, part), :] += decay * m_ref[0]
    own_gu[pl.ds(width + mine, part), :] += decay * m_ref[1]
    own_down[pl.ds(mine, part), :] += decay * m_ref[2]
    send_gu[...] = own_gu[...].astype(BF16)
    send_down[...] = own_down[...].astype(BF16)


def grads_two(n, divisor, k_ref, v_ref, begin_ref, *refs):
    (pgu_ref, pdown_ref), pieces = refs[:2], refs[2 : 2 + 3 * (n - 1)]
    gu_ref, down_ref, own_gu, own_down, send_gu, *sends = refs[2 + 3 * (n - 1) : -3]
    hid_s, dout_s, dgu_s = refs[-3:]
    leading = lax.axis_index("block") == 0

    @pl.when(leading)
    def _():
        shards = [lambda m: begin_ref[m]]
        for r in range(n - 1):
            shards.append(lambda m, r=r: pieces[3 * r + m][...])
        assemble(lax.axis_index("tok"), shards, gu_ref, down_ref)

    @pl.when(jnp.logical_not(leading))
    def _():
        gu_ref[...] = pgu_ref[...]
        down_ref[...] = pdown_ref[...]

    grads_core(divisor, k_ref, v_ref, gu_ref, down_ref, own_gu, own_down, hid_s, dout_s, dgu_s)
    send_gu[...] = own_gu[...].astype(BF16)
    if len(sends) == 1:
        sends[0][...] = own_down[...].astype(BF16)
    else:
        partner = 1 - lax.axis_index("tok")
        for send, (first, size) in zip(sends, cut_rows(down_ref.shape[0], partner)):
            send[...] = own_down[pl.ds(first, size), :].astype(BF16)


def cut_rows(width, tok):
    return (
        (pl.multiple_of(tok * 128, 128), width - 128),
        (pl.multiple_of((1 - tok) * (width - 128), 128), 128),
    )


def updated(rate, old_ref, at, moment):
    old = old_ref[at, :].astype(F32)
    moved = old - rate * moment
    old_norm = jnp.sqrt(jnp.mean(old * old, axis=1, keepdims=True) + 1e-06)
    new_norm = jnp.sqrt(jnp.mean(moved * moved, axis=1, keepdims=True) + 1e-06)
    return (moved * (old_norm / new_norm)).astype(BF16)


def summed(own_ref, recvs, first, size, recv_first):
    total = own_ref[pl.ds(first, size), :]
    for recv in recvs:
        total = total + recv[pl.ds(recv_first, size), :].astype(F32)
    return total


def update_one(n, head, mats, rate_ref, old_ref, own_ref, *refs):
    recvs = refs[: n - 1]
    new_ref, moment_ref = refs[-2:]
    width = own_ref.shape[1]
    if mats[0]:
        before = refs[n - 1]
        moment_ref[: mats[0] * width, :] = before[...]
    for i, m in enumerate(mats):
        at = pl.ds(i * width, width)
        moment = summed(own_ref, recvs, i * width, width, i * width)
        new_ref[at, :] = updated(rate_ref[head : head + 1, m : m + 1], old_ref, at, moment)
        moment_ref[m * width : (m + 1) * width, :] = moment.astype(BF16)


def store_mine(m, head, mine, new_s, moment_s, fast_s, mine_s, fast_ref, moment_ref, sems):
    part = fast_s.shape[0]
    fast_s[...] = new_s[pl.ds(mine, part), :]
    mine_s[...] = moment_s[pl.ds(mine, part), :]
    stores = [
        pltpu.make_async_copy(fast_s, fast_ref.at[0, m, head], sems.at[0]),
        pltpu.make_async_copy(mine_s, moment_ref.at[0, m, head], sems.at[1]),
    ]
    for store in stores:
        store.start()
    return stores


def update_two_gu(n, head, rate_ref, decay_ref, old_ref, own_ref, earlier_ref, q_ref, *refs):
    recvs = refs[: n - 1]
    hq_ref, fast_ref, moment_ref, gu_s, moment_s, fast_s, mine_s, sems = refs[-8:]
    width = own_ref.shape[1]
    part = width // n
    mine = pl.multiple_of(lax.axis_index("tok") * part, part)
    stores = []
    for m in range(2):
        at = pl.ds(m * width, width)
        moment = decay_ref[:, head : head + 1] * earlier_ref[at, :].astype(F32)
        moment = moment + summed(own_ref, recvs, m * width, width, m * width)
        new_s = gu_s.at[at, :]
        new_s[...] = updated(rate_ref[head : head + 1, m : m + 1], old_ref, at, moment)
        moment_s[...] = moment
        stores += store_mine(
            m,
            head,
            mine,
            new_s,
            moment_s,
            fast_s.at[m],
            mine_s.at[m],
            fast_ref,
            moment_ref,
            sems.at[m],
        )
    for at in row_chunks(q_ref.shape[0]):
        both = mm(q_ref[at, :], gu_s[...], ((1,), (1,)))
        hq_ref[at, :] = (jax.nn.silu(both[:, :width]) * both[:, width:]).astype(BF16)
    for store in stores:
        store.wait()


def update_two_down(n, head, cut, rate_ref, decay_ref, old_ref, own_ref, earlier_ref, hq_ref, *refs):
    recvs, refs = refs[: n - 1], refs[n - 1 :]
    width = old_ref.shape[1]
    part = width // n
    me = lax.axis_index("tok")
    parts = [(0, width)] if cut is None else cut_rows(width, me)
    first, size = parts[cut or 0]
    at = pl.ds(first, size)
    chunks = row_chunks(hq_ref.shape[0])

    def columns(which):
        first, size = parts[which]
        return pl.ds(pl.multiple_of(head * width + first, 128), size)

    if cut == 0:
        out_s, fast_ref, moment_ref, new_s, kept_s, fast_s, mine_s, sems = refs[-8:]
    elif cut == 1:
        before = refs[0]
        out_ref, new_s, out_s, out_sems, sem = refs[-5:]
        stores = [pltpu.make_async_copy(before, out_ref.at[1, :, columns(0)], sem)]
        stores[0].start()
    else:
        out_ref, fast_ref, moment_ref, new_s, out_s, out_sems, kept_s, fast_s, mine_s, sems = refs[-10:]
    moment = decay_ref[:, head : head + 1] * earlier_ref[pl.ds(2 * width + first, size), :].astype(F32)
    moment = moment + summed(own_ref, recvs, first, size, 0)
    new_s[...] = updated(rate_ref[head : head + 1, 2:], old_ref, at, moment)
    if cut != 1:
        kept_s[...] = moment
        mine = pl.ds(pl.multiple_of(me * part - first, math.gcd(part, 128)), part)
        fast_s[...] = new_s[mine, :]
        mine_s[...] = kept_s[mine, :]
        stores = [
            pltpu.make_async_copy(fast_s, fast_ref.at[0, 2, head], sems.at[0]),
            pltpu.make_async_copy(mine_s, moment_ref.at[0, 2, head], sems.at[1]),
        ]
        for store in stores:
            store.start()
    for i, rows in enumerate(chunks):
        out_s[rows, :] = mm(hq_ref[rows, :], new_s[...], ((1,), (1,))).astype(BF16)
        if cut != 0:
            stores.append(
                pltpu.make_async_copy(
                    out_s.at[rows, :], out_ref.at[1, rows, columns(cut or 0)], out_sems.at[i]
                )
            )
            stores[-1].start()
    for store in stores:
        store.wait()


def apply_one(head, q_ref, pgu_ref, pdown_ref, *refs):
    out_ref, out_s, sems = refs[-3:]
    rows, width = q_ref.shape
    stores = []
    for i, at in enumerate(row_chunks(rows)):
        both = mm(q_ref[at, :], pgu_ref[...], ((1,), (1,)))
        hq = (jax.nn.silu(both[:, :width]) * both[:, width:]).astype(BF16)
        out_s[at, :] = mm(hq, pdown_ref[...], ((1,), (1,))).astype(BF16)
        stores.append(
            pltpu.make_async_copy(
                out_s.at[at, :], out_ref.at[0, at, pl.ds(head * width, width)], sems.at[i]
            )
        )
        stores[-1].start()
    for store in stores:
        store.wait()


def on_device(keys, values, queries, fast_in, moment_in, initial_fast, rates, decays):
    n = lax.axis_size("tok")
    blocks = lax.axis_size("block")
    steps, rows, features = keys.shape
    heads = rates.shape[1]
    width = features // heads
    part = width // n
    chunks = len(row_chunks(rows))
    divisor = float(rows * n)
    fast_t = jnp.swapaxes(fast_in, 3, 4)
    moment_t = jnp.swapaxes(moment_in, 3, 4)
    begin_t = jnp.swapaxes(initial_fast, 2, 3)
    rates = rates.T
    decays = decays.reshape(1, heads)
    keys, values, queries, fast_t, moment_t, begin_t = (
        pltpu.with_memory_space_constraint(x, pltpu.HBM)
        for x in (keys, values, queries, fast_t, moment_t, begin_t)
    )

    def turned(x):
        return [lax.ppermute(x, "tok", [(i, (i + r) % n) for i in range(n)]) for r in range(1, n)]

    def forward(x):
        return lax.ppermute(x, "block", [(i, i + 1) for i in range(blocks - 1)])

    def shape(*dims, dtype=BF16):
        return jax.ShapeDtypeStruct(dims, dtype)

    row_scratch = pltpu.VMEM((rows, width), BF16)
    grad_scratch = (row_scratch, row_scratch, pltpu.VMEM((rows, 2 * width), BF16))
    grad_out = (
        shape(2 * width, width),
        shape(width, width),
        shape(2 * width, width),
        shape(width, width),
        shape(2 * width, width, dtype=F32),
        shape(width, width, dtype=F32),
    )

    groups = [[(0, 1), (1, 3)] if h == 0 else [(0, 3)] for h in range(heads)]
    shards = []
    for h in range(heads):
        owned, received = [], []
        for begin, end in groups[h]:
            owned.append(
                call(
                    functools.partial(take_head, h, begin),
                    shape(end - begin, part, width),
                    [HBM],
                    VMEM,
                )(fast_t)
            )
            received.append(turned(owned[-1]))
        shards.append(owned + [group[r] for r in range(n - 1) for group in received])

    apart = max(blocks // (3 * heads + 2), 1)
    sources = [apart * (p + 1) % blocks for p in range(3 * heads)]
    piece = call(functools.partial(take_piece, sources), shape(part, width), [HBM], VMEM)(begin_t)
    crossed = [
        lax.ppermute(
            piece,
            ("block", "tok"),
            [(s * n + i, s * n + (i + r) % n) for s in sorted(set(sources)) for i in range(n)],
        )
        for r in range(1, n)
    ]

    loaded = list(
        call(
            functools.partial(load_all, steps, heads),
            (shape(rows, width),) * (3 * steps * heads)
            + (shape(3, part, width, dtype=F32),) * heads
            + (shape(3, part, width),) * heads,
            [HBM] * 5,
            (VMEM,) * (3 * steps * heads + 2 * heads),
            (DMA((3 * steps * heads + 2 * heads,)),),
        )(keys, values, queries, moment_t, begin_t)
    )
    kvq = [[[loaded.pop(0) for _ in range(3)] for _ in range(heads)] for _ in range(steps)]
    m_own, begin_own = loaded[:heads], loaded[heads:]

    first = [
        call(
            functools.partial(grads_one, n, h, groups[h], divisor),
            grad_out,
            [VMEM] * (4 + len(shards[h])),
            (VMEM,) * 6,
            grad_scratch,
        )(decays, *kvq[0][h][:2], m_own[h], *shards[h])
        for h in range(heads)
    ]

    packs, moments = [], []
    for h in range(heads):
        gu, down, send_gu, send_down, own_gu, own_down = first[h]
        recv_gu, recv_down = turned(send_gu), turned(send_down)
        pack, moment = [], []
        for mats, old, own, recvs in (
            ((0, 1), gu, own_gu, recv_gu), ((2,), down, own_down, recv_down)
        ):
            new, *moment = call(
                functools.partial(update_one, n, h, mats),
                (shape(len(mats) * width, width), shape((mats[-1] + 1) * width, width)),
                [VMEM] * (2 + n + len(moment)),
                (VMEM, VMEM),
            )(rates, old, own, *recvs, *moment)
            pack.append(new)
        packs.append(pack)
        moments.append(forward(moment[0]))

    begins = []
    for p in range(3 * heads):
        begins.append(
            [
                lax.ppermute(
                    x, ("block", "tok"), [(sources[p] * n + i, i) for i in range(n)]
                )
                for x in crossed
            ]
        )

    second = []
    for h in range(heads):
        arrived = [forward(packs[h][0]), forward(packs[h][1])]
        pieces = [begins[3 * h + m][r] for r in range(n - 1) for m in range(3)]
        cuttable = n == 2 and width % 128 == 0 and part <= width - 128
        cuts = [width - 128, 128] if cuttable and h == heads - 1 else [width]
        second.append(
            call(
                functools.partial(grads_two, n, divisor),
                (
                    shape(2 * width, width),
                    shape(width, width),
                    shape(2 * width, width, dtype=F32),
                    shape(width, width, dtype=F32),
                    shape(2 * width, width),
                )
                + tuple(shape(size, width) for size in cuts),
                [VMEM] * (5 + 3 * (n - 1)),
                (VMEM,) * (5 + len(cuts)),
                grad_scratch,
            )(*kvq[1][h][:2], begin_own[h], *arrived, *pieces)
        )

    out_shape = jax.ShapeDtypeStruct(keys.shape, BF16)
    outputs = None
    for h in range(heads):
        prior = [] if outputs is None else [outputs]
        outputs = call(
            functools.partial(apply_one, h),
            out_shape,
            [VMEM] * 3 + [HBM] * len(prior),
            HBM,
            (row_scratch, DMA((chunks,))),
            aliases={3: 0} if prior else None,
        )(kvq[0][h][2], *packs[h], *prior)

    fast_shape = jax.ShapeDtypeStruct(fast_t.shape, BF16)
    moment_shape = jax.ShapeDtypeStruct(moment_t.shape, F32)
    ends = []
    for h in range(heads):
        gu, down, own_gu, own_down, send_gu, *sends = second[h]
        recv_gu = turned(send_gu)
        recv_down = [turned(x) for x in sends]
        at = 5 + n
        hq, *ends = call(
            functools.partial(update_two_gu, n, h),
            (shape(rows, width), fast_shape, moment_shape),
            [VMEM] * (5 + n) + [HBM] * len(ends),
            (VMEM, HBM, HBM),
            (
                pltpu.VMEM((2 * width, width), BF16),
                pltpu.VMEM((width, width), F32),
                pltpu.VMEM((2, part, width), BF16),
                pltpu.VMEM((2, part, width), F32),
                DMA((2, 2)),
            ),
            aliases={at: 1, at + 1: 2} if ends else None,
        )(rates, decays, gu, own_gu, moments[h], kvq[1][h][2], *recv_gu, *ends)
        before = []
        for i, recvs in enumerate(recv_down):
            cut = i if len(recv_down) > 1 else None
            size = recvs[0].shape[0]
            new = pltpu.VMEM((size, width), BF16)
            kept = pltpu.VMEM((size, width), F32)
            mine = (pltpu.VMEM((part, width), BF16), pltpu.VMEM((part, width), F32), DMA((2,)))
            product = (pltpu.VMEM((rows, size), BF16), DMA((chunks,)))
            if cut == 0:
                outs = (shape(rows, size), fast_shape, moment_shape)
                extra, scratch, spaces = [*ends], (new, kept) + mine, (VMEM, HBM, HBM)
                aliases = {at: 1, at + 1: 2}
            elif cut == 1:
                outs, extra, spaces = (out_shape,), [outputs], (HBM,)
                scratch, aliases = (new, *product, DMA(())), {at + 1: 0}
            else:
                outs, extra, spaces = (out_shape, fast_shape, moment_shape), [outputs, *ends], (HBM,) * 3
                scratch, aliases = (new, *product, kept) + mine, {at + j: j for j in range(3)}
            results = call(
                functools.partial(update_two_down, n, h, cut),
                outs,
                [VMEM] * (5 + n + len(before)) + [HBM] * len(extra),
                spaces,
                scratch,
                aliases=aliases,
            )(rates, decays, down, own_down, moments[h], hq, *recvs, *before, *extra)
            if cut == 0:
                first_columns, *ends = results
                before = [first_columns]
            else:
                outputs, *rest = results
                ends = rest or ends
    return (outputs, jnp.swapaxes(ends[0], 3, 4), jnp.swapaxes(ends[1], 3, 4))


def solution(mesh):
    placed = (
        P(None, ("block", "tok"), None),
        P(None, ("block", "tok"), None),
        P(None, ("block", "tok"), None),
        P("block", None, None, None, "tok"),
        P("block", None, None, None, "tok"),
        P(None, None, None, "tok"),
        P(),
        P(),
    )
    step = jax.shard_map(
        on_device,
        mesh=mesh,
        in_specs=placed,
        out_specs=(
            P(None, ("block", "tok"), None),
            P("block", None, None, None, "tok"),
            P("block", None, None, None, "tok"),
        ),
        check_vma=False,
    )

    def run(*args):
        with jax.sharding.use_abstract_mesh(mesh.abstract_mesh):
            return step(*args)

    return run
```
